32 devices in a mesh: dp: 16 (over z, x, core), seq: 2 (over y).
Axes of the slice: x: 2, y: 2, z: 4, core: 2. Of those that a mesh axis runs over, the one named last changes fastest.
Arguments:
- src_embed: bfloat16 [16, 1024, 512], P('dp', 'seq'), may hold values from -6 to 6
- tgt_embed: bfloat16 [16, 1024, 512], P('dp'), may hold values from -6 to 6
- src_lengths: int32 [16, 32], P('dp'), may hold values from 1 to 128, 1024 in all within a row
- tgt_lengths: int32 [16, 32], P('dp'), may hold values from 1 to 128, 1024 in all within a row
- enc_cotangent: bfloat16 [16, 1024, 512], P('dp', 'seq'), may hold values from -8 to 8
- dec_cotangent: bfloat16 [16, 1024, 512], P('dp'), may hold values from -8 to 8
- enc_inproj: bfloat16 [512, 1536], replicated, may hold values from -0.25 to 0.25
- enc_outproj: bfloat16 [512, 512], replicated, may hold values from -0.75 to 0.75
- enc_upproj: bfloat16 [512, 2048], replicated, may hold values from -0.25 to 0.25
- enc_downproj: bfloat16 [2048, 512], replicated, may hold values from -0.125 to 0.125
- enc_gains: float32 [2, 512], replicated, may hold values from 0.25 to 1.75
- enc_biases: float32 [6, 512], replicated, may hold values from -1.75 to 1.75
- enc_upbias: float32 [2048], replicated, may hold values from -1.75 to 1.75
- dec_inproj: bfloat16 [512, 1536], replicated, may hold values from -0.25 to 0.25
- dec_outproj: bfloat16 [512, 512], replicated, may hold values from -0.75 to 0.75
- cross_query: bfloat16 [512, 512], replicated, may hold values from -0.25 to 0.25
- cross_keyval: bfloat16 [512, 1024], replicated, may hold values from -0.25 to 0.25
- cross_outproj: bfloat16 [512, 512], replicated, may hold values from -0.75 to 0.75
- dec_upproj: bfloat16 [512, 2048], replicated, may hold values from -0.25 to 0.25
- dec_downproj: bfloat16 [2048, 512], replicated, may hold values from -0.125 to 0.125
- dec_gains: float32 [3, 512], replicated, may hold values from 0.25 to 1.75
- dec_biases: float32 [10, 512], replicated, may hold values from -1.75 to 1.75
- dec_upbias: float32 [2048], replicated, may hold values from -1.75 to 1.75
Outputs:
- encoded: bfloat16 [16, 1024, 512], P('dp', 'seq')
- decoded: bfloat16 [16, 1024, 512], P('dp')
- src_grad: float32 [16, 1024, 512], P('dp', 'seq')
- tgt_grad: float32 [16, 1024, 512], P('dp')
- enc_inproj_grad: float32 [512, 1536], P('dp')
- enc_outproj_grad: float32 [512, 512], P('dp')
- enc_upproj_grad: float32 [512, 2048], P('dp')
- enc_downproj_grad: float32 [2048, 512], P('dp')
- enc_gains_grad: float32 [2, 512], P(None, 'dp')
- enc_biases_grad: float32 [6, 512], P(None, 'dp')
- enc_upbias_grad: float32 [2048], P('dp')
- dec_inproj_grad: float32 [512, 1536], P('dp')
- dec_outproj_grad: float32 [512, 512], P('dp')
- cross_query_grad: float32 [512, 512], P('dp')
- cross_keyval_grad: float32 [512, 1024], P('dp')
- cross_outproj_grad: float32 [512, 512], P('dp')
- dec_upproj_grad: float32 [512, 2048], P('dp')
- dec_downproj_grad: float32 [2048, 512], P('dp')
- dec_gains_grad: float32 [3, 512], P(None, 'dp')
- dec_biases_grad: float32 [10, 512], P(None, 'dp')
- dec_upbias_grad: float32 [2048], P('dp')
The draws below stay inside these ranges and needn't reach their ends.
Inputs may be any that keep to these rules, and one draw needn't show every extreme that they name: `src_lengths`: the 32 source sides of a row lie one after another and fill its 1024 positions; pair k of a source row and pair k of the same target row are one sentence pair. `tgt_lengths`: the 32 target sides of a row lie one after another and fill its 1024 positions.
All inputs are finite; a program needn't handle non-finite values.
Results may differ from the reference program's by a relative error of at most 0.04.
Values may be sent and summed in bfloat16 or wider, within the bound.
No kernel may reach another device: no remote copies, remote signals or barrier semaphores. Data moves between devices by JAX's collectives and lax.ppermute only.
A program may use at most 320 MiB of HBM per device.

```python
import math
from functools import partial
import jax
import jax.numpy as jnp
import numpy as np
from jax import lax

D = 512
HEADS = 8
HEAD_DIM = 64
FF = 2048
LEN = 1024
PAIRS = 32
MAXPAIR = 128
ROWS = 16


def strengthened(entries, rng, source, target, shards_of, factor):
    owner, partner = [(jnp.arange(entries.shape[dim]) // (entries.shape[dim] // shards_of)).reshape([-1 if axis == dim else 1 for axis in range(entries.ndim)]) for dim in (source, target)]
    chosen = jax.random.permutation(rng, shards_of)[partner]
    strong = (owner == chosen) | (owner == (partner + shards_of // 2) % shards_of)
    return jnp.where(strong, factor * entries, entries)


def block_scale(key, dims, shards, smallest, largest):
    level, own = 1.0, jax.random.fold_in(key, 6)
    for dim, shards_of in shards:
        draws = jnp.exp(jax.random.uniform(jax.random.fold_in(own, dim), (shards_of,), jnp.float32, smallest / len(shards), largest / len(shards)))
        level = level * jnp.repeat(draws, dims[dim] // shards_of).reshape([-1 if axis == dim else 1 for axis in range(len(dims))])
    return level


def length_profile(number_of, total, bound, slope):
    portions = [(1 << 20) // math.isqrt(grade ** slope) + 1 for grade in range(2, number_of + 1)]
    spare, given = total - bound - (number_of - 1), [1] * (number_of - 1)
    while spare > 0:
        movable = [i for i in range(number_of - 1) if given[i] < bound]
        whole, budget = sum([portions[i] for i in movable]), spare
        for i in movable:
            more = min(bound - given[i], max(1, budget * portions[i] // whole), spare)
            given[i] = given[i] + more
            spare = spare - more
    return np.array([bound] + given)


def uneven(own_key, count, total, most, lean):
    if count == 2:
        one = jax.random.randint(own_key, (), max(1, total - most), min(most, total - 1) + 1)
        return jnp.stack([one, total - one])
    tallies = jnp.asarray(length_profile(count, total, most, lean), jnp.int32)
    pairs = (count - 1) // 2
    donor, sink = tallies[1:1 + 2 * pairs:2], tallies[2:2 + 2 * pairs:2]
    slack = jnp.minimum(donor - 1, most - sink)
    passed = jax.random.randint(jax.random.fold_in(own_key, 1), (pairs,), 0, 1 << 20) % (slack + 1)
    tallies = tallies.at[1:1 + 2 * pairs:2].set(donor - passed).at[2:2 + 2 * pairs:2].set(sink + passed)
    return tallies[jax.random.permutation(jax.random.fold_in(own_key, 2), count)]


def noise(key, extent, width, bound, shards=(), kind=jnp.bfloat16):
    drawn = jax.random.normal(key, extent, jnp.float32) * width
    if len(shards) > 0:
        drawn = block_scale(key, extent, shards, -0.22, 0.18) * drawn
    return jnp.clip(drawn, min=-bound, max=bound).astype(kind)


def noise_with(key, shape, spread, reach, pieces, heavy, held_as=jnp.bfloat16):
    array = spread * jax.random.normal(key, shape, jnp.float32)
    if pieces:
        array = array * block_scale(key, shape, pieces, -0.22, 0.18)
    return jnp.clip(strengthened(array, jax.random.fold_in(key, 3), *heavy), -reach, reach).astype(held_as)


def setup_inputs(seed: int = 0) -> dict:
    keys = jax.random.split(jax.random.key(seed), 24)
    return {
        "src_embed": noise(keys[0], (ROWS, LEN, D), 1.0, 6.0, ((0, 16), (1, 2))),
        "tgt_embed": noise(keys[1], (ROWS, LEN, D), 1.0, 6.0, ((0, 16),)),
        "src_lengths": jax.vmap(lambda own: uneven(own, PAIRS, LEN, MAXPAIR, 2))(jax.random.split(keys[2], ROWS)).reshape((ROWS, PAIRS)).astype(jnp.int32),
        "tgt_lengths": jax.vmap(lambda own: uneven(own, PAIRS, LEN, MAXPAIR, 2))(jax.random.split(keys[3], ROWS)).reshape((ROWS, PAIRS)).astype(jnp.int32),
        "enc_cotangent": noise_with(keys[4], (ROWS, LEN, D), 1.0, 8.0, ((0, 16), (1, 2)), (0, 2, 16, 2.0)),
        "dec_cotangent": noise_with(keys[5], (ROWS, LEN, D), 1.0, 8.0, ((0, 16),), (0, 2, 16, 2.0)),
        "enc_inproj": noise(keys[6], (D, 3 * D), D ** -0.5, 0.25),
        "enc_outproj": noise(keys[7], (D, D), (D // 8) ** -0.5, 0.75),
        "enc_upproj": noise(keys[8], (D, FF), D ** -0.5, 0.25),
        "enc_downproj": noise(keys[9], (FF, D), FF ** -0.5, 0.125),
        "enc_gains": jnp.clip(1.0 + 0.15 * jax.random.normal(keys[10], (2, D), jnp.float32), 0.25, 1.75),
        "enc_biases": noise(keys[11], (6, D), 0.3, 1.75, (), jnp.float32),
        "enc_upbias": noise(keys[12], (FF,), 0.3, 1.75, (), jnp.float32),
        "dec_inproj": noise(keys[13], (D, 3 * D), D ** -0.5, 0.25),
        "dec_outproj": noise(keys[14], (D, D), (D // 8) ** -0.5, 0.75),
        "cross_query": noise(keys[15], (D, D), D ** -0.5, 0.25),
        "cross_keyval": noise(keys[16], (D, 2 * D), D ** -0.5, 0.25),
        "cross_outproj": noise(keys[17], (D, D), (D // 8) ** -0.5, 0.75),
        "dec_upproj": noise(keys[18], (D, FF), D ** -0.5, 0.25),
        "dec_downproj": noise(keys[19], (FF, D), FF ** -0.5, 0.125),
        "dec_gains": jnp.clip(1.0 + 0.15 * jax.random.normal(keys[20], (3, D), jnp.float32), 0.25, 1.75),
        "dec_biases": noise(keys[21], (10, D), 0.3, 1.75, (), jnp.float32),
        "dec_upbias": noise(keys[22], (FF,), 0.3, 1.75, (), jnp.float32),
    }


@jax.custom_vjp
def low(v):
    return lax.optimization_barrier(v.astype(jnp.bfloat16)).astype(jnp.float32)

@jax.custom_vjp
def low_back(v):
    return v

def low_keep(v):
    return (low(v), None)

def low_pass(kept, grad):
    return (grad,)

def back_keep(v):
    return (v, None)

def back_low(kept, grad):
    return (low(grad),)
low.defvjp(low_keep, low_pass)
low_back.defvjp(back_keep, back_low)

def matmul(left, right):
    return jnp.dot(left, right, precision=lax.Precision.HIGHEST, preferred_element_type=jnp.float32)

def sinusoid(places):
    half_width = D // 2
    frequency = jnp.exp(-math.log(10000.0) * jnp.arange(half_width, dtype=jnp.float32) / half_width)
    angles = places.astype(jnp.float32)[:, None] * frequency[None, :]
    return jnp.concatenate([jnp.sin(angles), jnp.cos(angles)], axis=-1)

def pairs_row(lengths):
    pair_ends = jnp.cumsum(lengths).astype(jnp.int32)
    places = jnp.arange(LEN, dtype=jnp.int32)
    finished = pair_ends[None, :] <= places[:, None]
    number = lax.optimization_barrier(jnp.sum(finished.astype(jnp.int32), axis=1)).astype(jnp.int32)
    pair_start = lax.optimization_barrier(jnp.sum(jnp.where(finished, lengths[None, :], 0), axis=1)).astype(jnp.int32)
    return (number, places - pair_start)

def layer_norm(values, gain_row, shift_row):
    centred = values - lax.optimization_barrier(jnp.mean(values, axis=-1, keepdims=True))
    inverse = lax.rsqrt(lax.optimization_barrier(jnp.mean(centred * centred, axis=-1, keepdims=True)) + 1e-05)
    return centred * inverse * gain_row + shift_row

def attend(query_rows, key_rows, value_rows, allowed):
    query_heads = query_rows.reshape(query_rows.shape[0], HEADS, HEAD_DIM)
    key_heads = key_rows.reshape(key_rows.shape[0], HEADS, HEAD_DIM)
    value_heads = value_rows.reshape(value_rows.shape[0], HEADS, HEAD_DIM)
    raw_scores = jnp.einsum('qhd,khd->hqk', query_heads, key_heads, precision=lax.Precision.HIGHEST)
    logits = jnp.where(allowed[None], low_back(raw_scores) * HEAD_DIM ** (-0.5), -1e+30)
    row_max = lax.optimization_barrier(jnp.max(logits, axis=-1, keepdims=True))
    exp_scores = jnp.exp(logits - row_max)
    attn_prob = exp_scores / lax.optimization_barrier(jnp.sum(exp_scores, axis=-1, keepdims=True))
    mixed = jnp.einsum('hqk,khd->qhd', low(attn_prob), value_heads, precision=lax.Precision.HIGHEST)
    return mixed.reshape(query_rows.shape[0], D)

def feed_forward(hidden, up_matrix, up_bias, down_matrix, down_bias):
    up_input = low_back(matmul(low(hidden), up_matrix)) + up_bias
    return low_back(matmul(low(jax.nn.silu(up_input)), down_matrix)) + down_bias

def row_pass(params, row_items):
    enc_in_w, enc_out_w, enc_up_w, enc_down_w, enc_gain_rows, enc_bias_rows, enc_up_bias, dec_in_w, dec_out_w, cross_q_w, cross_kv_w, cross_out_w, dec_up_w, dec_down_w, dec_gain_rows, dec_bias_rows, dec_up_bias = params
    src_row, tgt_row, src_pair, src_place, tgt_pair, tgt_place = row_items
    zero_row = jnp.zeros((D,), jnp.float32)
    src_in = src_row + sinusoid(src_place)
    enc_qkv = low(low_back(matmul(low(src_in), enc_in_w)) + jnp.concatenate([enc_bias_rows[0], zero_row, enc_bias_rows[1]]))
    enc_att = attend(enc_qkv[:, :D], enc_qkv[:, D:2 * D], enc_qkv[:, 2 * D:], src_pair[:, None] == src_pair[None, :])
    enc_first = src_in + low_back(matmul(low(low_back(enc_att)), enc_out_w)) + enc_bias_rows[2]
    enc_mid = layer_norm(enc_first, enc_gain_rows[0], enc_bias_rows[3])
    enc_second = enc_mid + feed_forward(enc_mid, enc_up_w, enc_up_bias, enc_down_w, enc_bias_rows[4])
    enc_final = layer_norm(enc_second, enc_gain_rows[1], enc_bias_rows[5])
    tgt_in = tgt_row + sinusoid(tgt_place)
    dec_qkv = low(low_back(matmul(low(tgt_in), dec_in_w)) + jnp.concatenate([dec_bias_rows[0], zero_row, dec_bias_rows[1]]))
    places = jnp.arange(LEN, dtype=jnp.int32)
    self_allowed = (tgt_pair[:, None] == tgt_pair[None, :]) & (places[None, :] <= places[:, None])
    dec_att = attend(dec_qkv[:, :D], dec_qkv[:, D:2 * D], dec_qkv[:, 2 * D:], self_allowed)
    dec_first = tgt_in + low_back(matmul(low(low_back(dec_att)), dec_out_w)) + dec_bias_rows[2]
    dec_mid = layer_norm(dec_first, dec_gain_rows[0], dec_bias_rows[3])
    cross_rows = low(low_back(matmul(low(dec_mid), cross_q_w)) + dec_bias_rows[4])
    memory = low(enc_final)
    cross_kv_rows = low(low_back(matmul(memory, cross_kv_w)) + jnp.concatenate([zero_row, dec_bias_rows[5]]))
    cross_att = attend(cross_rows, cross_kv_rows[:, :D], cross_kv_rows[:, D:], tgt_pair[:, None] == src_pair[None, :])
    dec_second = dec_mid + low_back(matmul(low(low_back(cross_att)), cross_out_w)) + dec_bias_rows[6]
    dec_mid_two = layer_norm(dec_second, dec_gain_rows[1], dec_bias_rows[7])
    dec_third = dec_mid_two + feed_forward(dec_mid_two, dec_up_w, dec_up_bias, dec_down_w, dec_bias_rows[8])
    dec_final = layer_norm(dec_third, dec_gain_rows[2], dec_bias_rows[9])
    return (enc_final, dec_final)

def reference(src_embed, tgt_embed, src_lengths, tgt_lengths, enc_cotangent, dec_cotangent, enc_inproj, enc_outproj, enc_upproj, enc_downproj, enc_gains, enc_biases, enc_upbias, dec_inproj, dec_outproj, cross_query, cross_keyval, cross_outproj, dec_upproj, dec_downproj, dec_gains, dec_biases, dec_upbias):
    params = tuple((weight.astype(jnp.float32) for weight in (enc_inproj, enc_outproj, enc_upproj, enc_downproj, enc_gains, enc_biases, enc_upbias, dec_inproj, dec_outproj, cross_query, cross_keyval, cross_outproj, dec_upproj, dec_downproj, dec_gains, dec_biases, dec_upbias)))
    src_pair, src_place = jax.vmap(pairs_row)(src_lengths)
    tgt_pair, tgt_place = jax.vmap(pairs_row)(tgt_lengths)

    def forward(src_rows, tgt_rows, weights):
        return lax.map(jax.checkpoint(partial(row_pass, weights)), (src_rows, tgt_rows, src_pair, src_place, tgt_pair, tgt_place))
    outputs, pullback = jax.vjp(forward, src_embed.astype(jnp.float32), tgt_embed.astype(jnp.float32), params)
    src_grad, tgt_grad, weight_grads = pullback((enc_cotangent.astype(jnp.float32), dec_cotangent.astype(jnp.float32)))
    return (outputs[0].astype(jnp.bfloat16), outputs[1].astype(jnp.bfloat16), src_grad, tgt_grad, weight_grads[0], weight_grads[1], weight_grads[2], weight_grads[3], weight_grads[4], weight_grads[5], weight_grads[6], weight_grads[7], weight_grads[8], weight_grads[9], weight_grads[10], weight_grads[11], weight_grads[12], weight_grads[13], weight_grads[14], weight_grads[15], weight_grads[16])
```

```python
import functools
import math

import jax
import jax.numpy as jnp
import numpy as np
from jax import lax
from jax.experimental import pallas as pl
from jax.experimental.pallas import tpu as pltpu
from jax.sharding import PartitionSpec as P

HEADS = 8
HEAD_DIM = 64
MAXPAIR = 128
BLOCK = 128
GROUP = 256
WINDOW = 256
LOW = jnp.bfloat16
F32 = jnp.float32
MASKED = -1e30


def place_table(features):
    half = features // 2
    frequency = np.exp(-math.log(10000.0) * np.arange(half, dtype=np.float32) / np.float32(half)).astype(np.float32)
    angles = (np.arange(MAXPAIR, dtype=np.float32)[:, None] * frequency[None, :]).astype(np.float32)
    table = np.concatenate([np.sin(angles), np.cos(angles)], axis=-1).astype(np.float32)
    pieces, rest = [], table
    for _ in range(3):
        piece = rest.astype(jnp.bfloat16)
        pieces.append(piece)
        rest = rest - piece.astype(np.float32)
    return np.stack(pieces)


def dot_nn(left, right):
    return lax.dot_general(left, right, (((1,), (0,)), ((), ())), preferred_element_type=F32)


def dot_nt(left, right):
    return lax.dot_general(left, right, (((1,), (1,)), ((), ())), preferred_element_type=F32)


def dot_tn(left, right):
    return lax.dot_general(left, right, (((0,), (0,)), ((), ())), preferred_element_type=F32)


def iota(shape, dim):
    return lax.broadcasted_iota(jnp.int32, shape, dim).astype(F32)


def pair_ends(len_row):
    count = len_row.shape[1]
    lengths = jnp.broadcast_to(len_row, (count, count))
    down, across = iota((count, count), 0), iota((count, count), 1)
    ends_col = jnp.sum(jnp.where(across <= down, lengths, 0.0), axis=1, keepdims=True)
    len_col = jnp.sum(jnp.where(across == down, lengths, 0.0), axis=1, keepdims=True)
    ends_row = jnp.sum(jnp.where(down <= across, len_col, 0.0), axis=0, keepdims=True)
    return (ends_row, ends_col)


def pair_col(ends_row, places, total):
    number = jnp.sum(jnp.where(ends_row <= places, 1.0, 0.0), axis=1, keepdims=True)
    return jnp.where((places >= 0.0) & (places < total), number, -1.0)


def pair_row(ends_col, places):
    return jnp.sum(jnp.where(ends_col <= places, 1.0, 0.0), axis=0, keepdims=True)


def with_places(embed, places, ends_row, len_row, table_ref):
    started = jnp.sum(jnp.where(ends_row <= places, len_row, 0.0), axis=1, keepdims=True)
    inside = places - started
    hot = jnp.where(iota((embed.shape[0], MAXPAIR), 1) == inside, 1.0, 0.0).astype(LOW)
    sines = dot_nn(hot, table_ref[0]) + dot_nn(hot, table_ref[1]) + dot_nn(hot, table_ref[2])
    return embed.astype(F32) + sines


def norm_forward(values, gain_row, shift_row):
    centred = values - jnp.mean(values, axis=-1, keepdims=True)
    inverse = lax.rsqrt(jnp.mean(centred * centred, axis=-1, keepdims=True) + 1e-05)
    normed = centred * inverse
    return (normed * gain_row + shift_row, normed, inverse)


def norm_backward(grad_rows, normed, inverse, gain_row):
    scaled = grad_rows * gain_row
    return inverse * (
        scaled
        - jnp.mean(scaled, axis=-1, keepdims=True)
        - normed * jnp.mean(scaled * normed, axis=-1, keepdims=True)
    )


def sigmoid(values):
    return 1.0 / (1.0 + jnp.exp(-values))


def col_sum(values):
    return jnp.sum(values, axis=0, keepdims=True)


def head_masks(scale):
    lane = lax.broadcasted_iota(jnp.int32, (1, GROUP), 1) // HEAD_DIM
    return [jnp.where(lane == h, scale, 0.0).astype(LOW) for h in range(GROUP // HEAD_DIM)]


def spread(rows, masks):
    return jnp.concatenate([rows * mask for mask in masks], axis=0)


def diagonal(wide):
    count = GROUP // HEAD_DIM
    return [
        wide[h * HEAD_DIM : (h + 1) * HEAD_DIM, h * BLOCK : (h + 1) * BLOCK] for h in range(count)
    ]


def attend_block(query, keys, values, bias, group):
    lanes = slice(group * GROUP, (group + 1) * GROUP)
    stacked = spread(query(lanes), head_masks(HEAD_DIM**-0.5))
    scores = dot_nt(keys(lanes), stacked)
    probs, maxima, sums = [], [], []
    for h in range(GROUP // HEAD_DIM):
        score = scores[:, h * BLOCK : (h + 1) * BLOCK] + bias
        row_max = jnp.max(score, axis=0, keepdims=True)
        exp_score = jnp.exp(score - row_max)
        maxima.append(row_max)
        sums.append(col_sum(exp_score))
        probs.append(exp_score.astype(LOW))
    wide = dot_tn(values(lanes), jnp.concatenate(probs, axis=1))
    return (diagonal(wide), maxima, sums)


def attend_local(rows_ref, count, width, att_ref, lse_ref, rule):
    def body(j, carry):
        first = pl.multiple_of(j * BLOCK, BLOCK)
        queries = pl.ds(pl.multiple_of(first + BLOCK, BLOCK), BLOCK)
        keys = pl.ds(first, width)
        bias = rule(first)
        for group in range(2):
            def part(rows, offset):
                return lambda lanes: rows_ref[rows, offset + lanes.start : offset + lanes.stop]

            outs, maxima, sums = attend_block(
                part(queries, 0), part(keys, 512), part(keys, 1024), bias, group
            )
            mixed = jnp.concatenate([o * (1.0 / s) for o, s in zip(outs, sums)], axis=0)
            att_ref[pl.ds(first, BLOCK), group * GROUP : (group + 1) * GROUP] = mixed.T.astype(
                att_ref.dtype
            )
            lse_ref[j, group : group + 1, :] = jnp.concatenate(
                [m + jnp.log(s) for m, s in zip(maxima, sums)], axis=1
            )
        return carry

    lax.fori_loop(0, count, body, 0)


def attend_back_block(query, grad, keys, values, bias, lse, deltas):
    stacked = spread(query, head_masks(HEAD_DIM**-0.5))
    grads = spread(grad, head_masks(1.0))
    scores = dot_nt(keys, stacked)
    prob_grads = dot_nt(values, grads)
    probs, score_grads = [], []
    for h in range(GROUP // HEAD_DIM):
        cols = slice(h * BLOCK, (h + 1) * BLOCK)
        prob = jnp.exp(scores[:, cols] + bias - lse[:, cols])
        prob_grad = prob_grads[:, cols]
        delta = col_sum(prob * prob_grad) if deltas is None else deltas[h]
        score_grads.append((prob * (prob_grad - delta)).astype(LOW))
        probs.append(prob.astype(LOW))
    prob_wide = jnp.concatenate(probs, axis=1)
    grad_wide = jnp.concatenate(score_grads, axis=1)
    value_grad = dot_nn(prob_wide, grads)
    key_grad = dot_nn(grad_wide, stacked)
    query_grad = jnp.concatenate(diagonal(dot_tn(keys, grad_wide)), axis=0) * HEAD_DIM**-0.5
    return (query_grad, key_grad, value_grad)


def attend_local_back(rows_ref, grad_ref, lse_ref, count, width, query_ref, keyval_ref, rule):
    keyval_ref[...] = jnp.zeros(keyval_ref.shape, F32)

    def body(j, carry):
        first = pl.multiple_of(j * BLOCK, BLOCK)
        queries = pl.ds(pl.multiple_of(first + BLOCK, BLOCK), BLOCK)
        own = pl.ds(first, BLOCK)
        keys = pl.ds(first, width)
        bias = rule(first)
        for group in range(2):
            low, high = group * GROUP, (group + 1) * GROUP
            query_grad, key_grad, value_grad = attend_back_block(
                rows_ref[queries, low:high],
                grad_ref[own, low:high],
                rows_ref[keys, 512 + low : 512 + high],
                rows_ref[keys, 1024 + low : 1024 + high],
                bias,
                lse_ref[j, group : group + 1, :],
                None,
            )
            query_ref[own, low:high] = query_grad.T
            keyval_ref[keys, low:high] += key_grad
            keyval_ref[keys, 512 + low : 512 + high] += value_grad
        return carry

    lax.fori_loop(0, count, body, 0)


def self_rule(ends, start, total, width, causal):
    ends_row, ends_col = ends

    def rule(first):
        shift = (start + first).astype(F32)
        key_places = iota((width, 1), 0) + (shift - BLOCK)
        query_places = iota((1, BLOCK), 1) + shift
        allowed = pair_col(ends_row, key_places, total) == pair_row(ends_col, query_places)
        if causal:
            allowed = allowed & (key_places <= query_places)
        return jnp.where(allowed, 0.0, MASKED)

    return rule


def put_blocks(result, block, held_ref, keep_ref, send_ref, mine, order, cols):
    devices = held_ref.shape[0]
    for i in range(devices):
        held_ref[i] = block(result, i)
    half = devices // 2
    bits = len(order)
    for place in range(devices):
        flips = sum(((place >> (bits - 1 - s)) & 1) << order[s] for s in range(bits))
        target = keep_ref if place < half else send_ref
        target[place % half, :, cols] = held_ref[mine ^ flips]


def put_rows(result, held_ref, keep_ref, send_ref, mine, order, col):
    width = result.shape[1]
    rows = keep_ref.shape[1]
    put_blocks(
        result.astype(LOW),
        lambda whole, i: whole[i * rows : (i + 1) * rows, :],
        held_ref,
        keep_ref,
        send_ref,
        mine,
        order,
        slice(col, col + width),
    )


def put_cols(whole_ref, held_ref, keep_ref, send_ref, mine, order):
    width = keep_ref.shape[2]
    put_blocks(
        whole_ref,
        lambda whole, i: whole[:, i * width : (i + 1) * width],
        held_ref,
        keep_ref,
        send_ref,
        mine,
        order,
        slice(0, width),
    )


def dec_pre_kernel(total, idx, embed, lens, table, w, biases, x_out, low_out, rows_out):
    count = x_out.shape[0]
    start = idx[0] * count
    len_row = lens[...].astype(F32)
    ends_row, _ = pair_ends(len_row)

    def chunk(source, rows, target, size):
        places = iota((size, 1), 0) + (start + target - BLOCK).astype(F32)
        x = with_places(embed[pl.ds(pl.multiple_of(source, BLOCK), size), :], places, ends_row, len_row, table)
        low = x.astype(LOW)
        if rows is not None:
            x_out[rows : rows + size, :] = x
            low_out[rows : rows + size, :] = low
        for c in range(3):
            part = dot_nn(low, w[:, c * 512 : (c + 1) * 512])
            if c != 1:
                part = part + biases[c // 2 : c // 2 + 1, :]
            rows_out[target : target + size, c * 512 : (c + 1) * 512] = part.astype(LOW)

    chunk(jnp.maximum(start - BLOCK, 0), None, 0, BLOCK)
    size = min(256, count)
    for at in range(0, count, size):
        chunk(start + at, at, BLOCK + at, size)


def enc_kernel(
    total, idx, left, own, right, lens, table, w_in, w_out, w_up, w_down, gains, biases, upbias,
    rows_out, low_out, lse_out, hid_out, mid_out, mid_inv_out, fin_out, fin_inv_out, encoded_out,
    x_ref,
):
    count = own.shape[0]
    start = idx[0] * count
    len_row = lens[...].astype(F32)
    ends = pair_ends(len_row)

    def chunk(embed, rows, target, size):
        places = iota((size, 1), 0) + (start + target - BLOCK).astype(F32)
        x = with_places(embed, places, ends[0], len_row, table)
        low = x.astype(LOW)
        if rows is not None:
            x_ref[rows : rows + size, :] = x
            low_out[rows : rows + size, :] = low
        for c in range(3):
            part = dot_nn(low, w_in[:, c * 512 : (c + 1) * 512])
            if c != 1:
                part = part + biases[c // 2 : c // 2 + 1, :]
            rows_out[target : target + size, c * 512 : (c + 1) * 512] = part.astype(LOW)

    size = min(256, count)
    chunk(left[...], None, 0, BLOCK)
    for at in range(0, count, size):
        chunk(own[at : at + size, :], at, BLOCK + at, size)
    chunk(right[...], None, BLOCK + count, BLOCK)
    width = 3 * BLOCK
    attend_local(
        rows_out, count // BLOCK, width, hid_out, lse_out, self_rule(ends, start, total, width, False)
    )

    def dense(step, carry):
        rows = pl.ds(pl.multiple_of(step * size, size), size)
        z = x_ref[rows, :] + dot_nn(hid_out[rows, :], w_out[...]) + biases[2:3, :]
        mid, normed, inverse = norm_forward(z, gains[0:1, :], biases[3:4, :])
        mid_out[rows, :] = normed
        mid_inv_out[rows, :] = inverse
        low = mid.astype(LOW)
        z = mid + biases[4:5, :]
        for c in range(0, w_up.shape[1], 512):
            up = dot_nn(low, w_up[:, c : c + 512]) + upbias[:, c : c + 512]
            active = (up * sigmoid(up)).astype(LOW)
            z = z + dot_nn(active, w_down[c : c + 512, :])
        final, normed, inverse = norm_forward(z, gains[1:2, :], biases[5:6, :])
        fin_out[rows, :] = normed
        fin_inv_out[rows, :] = inverse
        encoded_out[rows, :] = final.astype(LOW)
        return carry

    lax.fori_loop(0, count // size, dense, 0)


def dec_self_kernel(
    total, idx, x, rows_in, lens, w_out, w_query, gains, biases,
    lse_out, hid_out, normed_out, inv_out, query_out,
):
    count = x.shape[0]
    start = idx[0] * count
    ends = pair_ends(lens[...].astype(F32))
    width = 2 * BLOCK
    attend_local(
        rows_in, count // BLOCK, width, hid_out, lse_out, self_rule(ends, start, total, width, True)
    )
    size = min(256, count)

    def dense(step, carry):
        rows = pl.ds(pl.multiple_of(step * size, size), size)
        z = x[rows, :] + dot_nn(hid_out[rows, :], w_out[...]) + biases[2:3, :]
        mid, normed, inverse = norm_forward(z, gains[0:1, :], biases[3:4, :])
        normed_out[rows, :] = normed
        inv_out[rows, :] = inverse
        query = dot_nn(mid.astype(LOW), w_query[...]) + biases[4:5, :]
        query_out[rows, :] = query.astype(LOW)
        return carry

    lax.fori_loop(0, count // size, dense, 0)


def cross_span(src_lens, tgt_lens, first):
    def step(k, carry):
        begin, low, high = carry
        end = begin + tgt_lens[0, k]
        length = src_lens[0, k]
        low = low + jnp.where(end <= first, length, 0)
        high = high + jnp.where(begin <= first + (BLOCK - 1), length, 0)
        return (end, low, high)

    zero = jnp.int32(0)
    _, low, high = lax.fori_loop(0, src_lens.shape[1], step, (zero, zero, zero), unroll=True)
    low = (low // 16) * 16
    return (low, (high - low + (WINDOW - 1)) // WINDOW)


def cross_rule(src_ends_row, tgt_ends_col, first, begin, total):
    key_places = iota((WINDOW, 1), 0) + begin.astype(F32)
    query_places = iota((1, BLOCK), 1) + first.astype(F32)
    allowed = pair_col(src_ends_row, key_places, total) == pair_row(tgt_ends_col, query_places)
    return jnp.where(allowed, 0.0, MASKED)


def cross_kernel(
    total, idx, src_lens, tgt_lens, query, memory, others, src_vec, tgt_vec, w, biases,
    att_out, lse_out, keyval_out, memory_out,
    max_ref, sum_ref, acc_ref,
):
    count = query.shape[0]
    length = memory.shape[0]
    shards = others.shape[0] + 1
    start = idx[0] * count
    src_ends_row, _ = pair_ends(src_vec[...].astype(F32))
    _, tgt_ends_col = pair_ends(tgt_vec[...].astype(F32))
    size = min(256, length)
    for s in range(shards):
        base = lax.rem(idx[0] + s, shards) * length
        for at in range(0, length, size):
            rows = pl.ds(pl.multiple_of(base + at, BLOCK), size)
            source = memory[at : at + size, :] if s == 0 else others[s - 1, at : at + size, :]
            memory_out[rows, :] = source
            keyval_out[rows, :512] = dot_nn(source, w[:, :512]).astype(LOW)
            keyval_out[rows, 512:] = (dot_nn(source, w[:, 512:]) + biases[5:6, :]).astype(LOW)
    keyval_out[total:, :] = jnp.zeros((WINDOW, 1024), LOW)

    def body(j, carry):
        at = pl.multiple_of(j * BLOCK, BLOCK)
        rows = pl.ds(at, BLOCK)
        first = start + at
        low, windows = cross_span(src_lens, tgt_lens, first)
        max_ref[...] = jnp.full(max_ref.shape, MASKED, F32)
        sum_ref[...] = jnp.zeros(sum_ref.shape, F32)
        acc_ref[...] = jnp.zeros(acc_ref.shape, F32)

        def window(n, carry):
            begin = pl.multiple_of(low + n * WINDOW, 16)
            keys = pl.ds(begin, WINDOW)
            bias = cross_rule(src_ends_row, tgt_ends_col, first, begin, total)
            for group in range(2):
                def part(ref, rows, offset):
                    return lambda lanes: ref[rows, offset + lanes.start : offset + lanes.stop]

                outs, maxima, sums = attend_block(
                    part(query, rows, 0), part(keyval_out, keys, 0), part(keyval_out, keys, 512), bias, group
                )
                for h in range(4):
                    head = group * 4 + h
                    old = max_ref[head : head + 1, :]
                    new = jnp.maximum(old, maxima[h])
                    before, now = jnp.exp(old - new), jnp.exp(maxima[h] - new)
                    max_ref[head : head + 1, :] = new
                    sum_ref[head : head + 1, :] = sum_ref[head : head + 1, :] * before + sums[h] * now
                    part_rows = slice(head * HEAD_DIM, (head + 1) * HEAD_DIM)
                    acc_ref[part_rows, :] = acc_ref[part_rows, :] * before + outs[h] * now
            return carry

        lax.fori_loop(0, windows, window, 0)
        for group in range(2):
            heads = range(group * 4, group * 4 + 4)
            mixed = jnp.concatenate(
                [
                    acc_ref[h * HEAD_DIM : (h + 1) * HEAD_DIM, :] * (1.0 / sum_ref[h : h + 1, :])
                    for h in heads
                ],
                axis=0,
            )
            att_out[rows, group * GROUP : (group + 1) * GROUP] = mixed.T
            lse_out[j, group : group + 1, :] = jnp.concatenate(
                [max_ref[h : h + 1, :] + jnp.log(sum_ref[h : h + 1, :]) for h in heads], axis=1
            )
        return carry

    lax.fori_loop(0, count // BLOCK, body, 0)


def dec_tail_kernel(
    order, idx, att, normed_in, cot, w_out, w_up, w_down, gains, biases, upbias,
    decoded_out, att_grad_out, branch_out, sums_out, keep_rows, send_rows, keep_cols, send_cols,
    hid_ref, branch_ref, mid_ref, up_ref, active_ref, ffn_ref, up_low_ref, held_ref, held_cols, down_ref,
):
    count = att.shape[0]
    mine = idx[1]
    hidden = w_up.shape[1]
    sums_out[...] = jnp.zeros(sums_out.shape, F32)
    size = min(256, count)

    def dense(step, carry):
        rows = pl.ds(pl.multiple_of(step * size, size), size)
        hid = att[rows, :].astype(LOW)
        hid_ref[rows, :] = hid
        first = normed_in[rows, :] * gains[0:1, :] + biases[3:4, :]
        z = first + dot_nn(hid, w_out[...]) + biases[6:7, :]
        mid, normed, inverse = norm_forward(z, gains[1:2, :], biases[7:8, :])
        low = mid.astype(LOW)
        mid_ref[rows, :] = low
        z = mid + biases[8:9, :]
        for c in range(0, hidden, 512):
            up = dot_nn(low, w_up[:, c : c + 512]) + upbias[:, c : c + 512]
            up_ref[:, c : c + 512] = up
            active = (up * sigmoid(up)).astype(LOW)
            active_ref[rows, c : c + 512] = active
            z = z + dot_nn(active, w_down[c : c + 512, :])
        final, normed_final, inverse_final = norm_forward(z, gains[2:3, :], biases[9:10, :])
        decoded_out[rows, :] = final.astype(LOW)
        grad = cot[rows, :].astype(F32)
        ffn = norm_backward(grad, normed_final, inverse_final, gains[2:3, :])
        ffn_low = ffn.astype(LOW)
        ffn_ref[rows, :] = ffn_low
        mid_grad = ffn
        for c in range(0, hidden, 512):
            up = up_ref[:, c : c + 512]
            gate = sigmoid(up)
            up_grad = dot_nt(ffn_low, w_down[c : c + 512, :]) * (gate * (1.0 + up * (1.0 - gate)))
            sums_out[8 + c // 512 : 9 + c // 512, :] += col_sum(up_grad)
            up_low = up_grad.astype(LOW)
            up_low_ref[rows, c : c + 512] = up_low
            mid_grad = mid_grad + dot_nt(up_low, w_up[:, c : c + 512])
        branch = norm_backward(mid_grad, normed, inverse, gains[1:2, :])
        branch_low = branch.astype(LOW)
        branch_out[rows, :] = branch
        branch_ref[rows, :] = branch_low
        att_grad_out[rows, :] = dot_nt(branch_low, w_out[...]).astype(LOW)
        sums_out[0:1, :] += col_sum(mid_grad * normed)
        sums_out[1:2, :] += col_sum(grad * normed_final)
        sums_out[2:3, :] += col_sum(branch)
        sums_out[3:4, :] += col_sum(mid_grad)
        sums_out[4:5, :] += col_sum(ffn)
        sums_out[5:6, :] += col_sum(grad)
        return carry

    lax.fori_loop(0, count // size, dense, 0)
    feed_forward_grads(
        mid_ref, up_low_ref, ffn_ref, active_ref, hid_ref, branch_ref,
        keep_rows, send_rows, keep_cols, send_cols, held_ref, held_cols, down_ref, mine, order,
    )


def feed_forward_grads(
    mid_ref, up_low_ref, ffn_ref, active_ref, hid_ref, branch_ref,
    keep_rows, send_rows, keep_cols, send_cols, held_ref, held_cols, down_ref, mine, order,
):
    hidden = up_low_ref.shape[1]
    for c in range(0, hidden, 512):
        put_rows(
            dot_tn(mid_ref[...], up_low_ref[:, c : c + 512]), held_ref, keep_rows, send_rows, mine, order, c
        )
    put_rows(dot_tn(hid_ref[...], branch_ref[...]), held_ref, keep_rows, send_rows, mine, order, hidden)
    for c in range(0, hidden, 512):
        down_ref[:, c : c + 512] = dot_tn(ffn_ref[...], active_ref[:, c : c + 512]).astype(LOW)
    put_cols(down_ref, held_cols, keep_cols, send_cols, mine, order)


def cross_back_kernel(
    total, order, idx, src_lens, tgt_lens, query, keyval, memory, att, att_grad, lse, src_vec, tgt_vec,
    w_keyval, w_query, w_out, normed_in, inv_in, branch_in, hid_in, gains, biases,
    mem_own_out, mem_out, branch_out, att_grad_out, sums_out, keep_rows, send_rows,
    keyval_ref, query_ref, branch_ref, keyval_low, query_low, mid_ref, held_ref,
):
    count = query.shape[0]
    start = idx[0] * count
    mine = idx[1]
    src_ends_row, _ = pair_ends(src_vec[...].astype(F32))
    _, tgt_ends_col = pair_ends(tgt_vec[...].astype(F32))
    keyval_ref[...] = jnp.zeros(keyval_ref.shape, F32)
    query_ref[...] = jnp.zeros(query_ref.shape, F32)
    sums_out[...] = jnp.zeros(sums_out.shape, F32)
    select = jnp.where(
        lax.broadcasted_iota(jnp.int32, (HEADS, 512), 1) // HEAD_DIM
        == lax.broadcasted_iota(jnp.int32, (HEADS, 512), 0),
        1.0,
        0.0,
    )

    def body(j, carry):
        at = pl.multiple_of(j * BLOCK, BLOCK)
        rows = pl.ds(at, BLOCK)
        first = start + at
        low, windows = cross_span(src_lens, tgt_lens, first)
        weighed = att[rows, :] * att_grad[rows, :].astype(F32)
        deltas = lax.dot_general(
            select, weighed, (((1,), (1,)), ((), ())),
            precision=lax.Precision.HIGHEST, preferred_element_type=F32,
        )

        def window(n, carry):
            begin = pl.multiple_of(low + n * WINDOW, 16)
            keys = pl.ds(begin, WINDOW)
            bias = cross_rule(src_ends_row, tgt_ends_col, first, begin, total)
            for group in range(2):
                lo, hi = group * GROUP, (group + 1) * GROUP
                query_grad, key_grad, value_grad = attend_back_block(
                    query[rows, lo:hi],
                    att_grad[rows, lo:hi],
                    keyval[keys, lo:hi],
                    keyval[keys, 512 + lo : 512 + hi],
                    bias,
                    lse[j, group : group + 1, :],
                    [deltas[group * 4 + h : group * 4 + h + 1, :] for h in range(4)],
                )
                query_ref[rows, lo:hi] += query_grad.T
                keyval_ref[keys, lo:hi] += key_grad
                keyval_ref[keys, 512 + lo : 512 + hi] += value_grad
            return carry

        lax.fori_loop(0, windows, window, 0)
        return carry

    lax.fori_loop(0, count // BLOCK, body, 0)
    size = min(256, total)
    shards = mem_out.shape[0] + 1
    length = total // shards

    def to_memory(step, carry):
        rows = pl.ds(pl.multiple_of(step * size, size), size)
        grads = keyval_ref[rows, :]
        sums_out[4:5, :] += col_sum(grads[:, 512:])
        keyval_low[rows, :] = grads.astype(LOW)
        return carry

    lax.fori_loop(0, total // size, to_memory, 0)
    for s in range(shards):
        base = pl.multiple_of(lax.rem(idx[0] + s, shards) * length, BLOCK)
        grads = dot_nt(keyval_low[pl.ds(base, length), :], w_keyval[...])
        if s == 0:
            mem_own_out[...] = grads
        else:
            mem_out[s - 1] = grads.astype(LOW)
    size = min(256, count)

    def dense(step, carry):
        rows = pl.ds(pl.multiple_of(step * size, size), size)
        query_grad = query_ref[rows, :]
        low = query_grad.astype(LOW)
        query_low[rows, :] = low
        normed = normed_in[rows, :]
        mid_ref[rows, :] = (normed * gains[0:1, :] + biases[3:4, :]).astype(LOW)
        mid_grad = branch_in[rows, :] + dot_nt(low, w_query[...])
        branch = norm_backward(mid_grad, normed, inv_in[rows, :], gains[0:1, :])
        branch_low = branch.astype(LOW)
        branch_out[rows, :] = branch
        branch_ref[rows, :] = branch_low
        att_grad_out[rows, :] = dot_nt(branch_low, w_out[...]).astype(LOW)
        sums_out[0:1, :] += col_sum(mid_grad * normed)
        sums_out[1:2, :] += col_sum(branch)
        sums_out[2:3, :] += col_sum(mid_grad)
        sums_out[3:4, :] += col_sum(query_grad)
        return carry

    lax.fori_loop(0, count // size, dense, 0)
    for c in range(0, 1024, 512):
        put_rows(
            dot_tn(memory[...], keyval_low[:, c : c + 512]), held_ref, keep_rows, send_rows, mine, order, c
        )
    put_rows(dot_tn(mid_ref[...], query_low[...]), held_ref, keep_rows, send_rows, mine, order, 1024)
    put_rows(dot_tn(hid_in[...], branch_ref[...]), held_ref, keep_rows, send_rows, mine, order, 1536)


def dec_self_back_kernel(
    total, idx, rows_in, att_grad, lse, lens, own_out, halo_out, query_ref, keyval_ref
):
    count = att_grad.shape[0]
    ends = pair_ends(lens[...].astype(F32))
    width = 2 * BLOCK
    attend_local_back(
        rows_in, att_grad, lse, count // BLOCK, width, query_ref, keyval_ref,
        self_rule(ends, idx[0] * count, total, width, True),
    )
    halo_out[...] = keyval_ref[:BLOCK, :].astype(LOW)
    own_out[:, :512] = query_ref[...]
    own_out[:, 512:] = keyval_ref[BLOCK : BLOCK + count, :]


def enc_self_back_kernel(
    total, idx, rows_in, att_grad, lse, lens, own_out, left_out, right_out, query_ref, keyval_ref
):
    count = att_grad.shape[0]
    ends = pair_ends(lens[...].astype(F32))
    width = 3 * BLOCK
    attend_local_back(
        rows_in, att_grad, lse, count // BLOCK, width, query_ref, keyval_ref,
        self_rule(ends, idx[0] * count, total, width, False),
    )
    left_out[...] = keyval_ref[:BLOCK, :].astype(LOW)
    right_out[...] = keyval_ref[BLOCK + count :, :].astype(LOW)
    own_out[:, :512] = query_ref[...]
    own_out[:, 512:] = keyval_ref[BLOCK : BLOCK + count, :]


def input_grad_kernel(order, idx, own, halos, branch, low_in, w, grad_out, sums_out, keep_rows, send_rows, low_ref, own_ref, held_ref):
    count = own.shape[0]
    mine = idx[1]
    own_ref[...] = own[...]
    for first, halo in halos:
        at = 0 if first else count - BLOCK
        own_ref[at : at + BLOCK, 512:] += halo[...].astype(F32)
    sums_out[...] = jnp.zeros(sums_out.shape, F32)
    size = min(256, count)

    def dense(step, carry):
        rows = pl.ds(pl.multiple_of(step * size, size), size)
        grads = own_ref[rows, :]
        sums_out[0:1, :] += col_sum(grads[:, :512])
        sums_out[1:2, :] += col_sum(grads[:, 1024:])
        low = grads.astype(LOW)
        low_ref[rows, :] = low
        grad_out[rows, :] = (branch[rows, :] + dot_nt(low, w[...])).astype(grad_out.dtype)
        return carry

    lax.fori_loop(0, count // size, dense, 0)
    for c in range(0, 1536, 512):
        put_rows(
            dot_tn(low_in[...], low_ref[:, c : c + 512]), held_ref, keep_rows, send_rows, mine, order, c
        )


def dec_input_grad_kernel(order, idx, own, halo, *rest):
    input_grad_kernel(order, idx, own, ((False, halo),), *rest)


def enc_input_grad_kernel(order, idx, own, before, after, *rest):
    input_grad_kernel(order, idx, own, ((True, before), (False, after)), *rest)


def enc_tail_back_kernel(
    order, idx, cot, mem_own, mem_others, fin_in, fin_inv, mid_in, mid_inv, hid_in,
    w_out, w_up, w_down, gains, biases, upbias,
    branch_out, att_grad_out, sums_out, keep_rows, send_rows, keep_cols, send_cols,
    branch_ref, mid_ref, active_ref, ffn_ref, up_low_ref, held_ref, held_cols, down_ref,
):
    count = cot.shape[0]
    mine = idx[1]
    hidden = w_up.shape[1]
    sums_out[...] = jnp.zeros(sums_out.shape, F32)
    size = min(256, count)

    def dense(step, carry):
        rows = pl.ds(pl.multiple_of(step * size, size), size)
        grad = cot[rows, :].astype(F32) + mem_own[rows, :]
        for s in range(mem_others.shape[0]):
            grad = grad + mem_others[s, rows, :].astype(F32)
        normed_final = fin_in[rows, :]
        ffn = norm_backward(grad, normed_final, fin_inv[rows, :], gains[1:2, :])
        ffn_low = ffn.astype(LOW)
        ffn_ref[rows, :] = ffn_low
        normed = mid_in[rows, :]
        low = (normed * gains[0:1, :] + biases[3:4, :]).astype(LOW)
        mid_ref[rows, :] = low
        mid_grad = ffn
        for c in range(0, hidden, 512):
            up = dot_nn(low, w_up[:, c : c + 512]) + upbias[:, c : c + 512]
            gate = sigmoid(up)
            active_ref[rows, c : c + 512] = (up * gate).astype(LOW)
            up_grad = dot_nt(ffn_low, w_down[c : c + 512, :]) * (gate * (1.0 + up * (1.0 - gate)))
            sums_out[8 + c // 512 : 9 + c // 512, :] += col_sum(up_grad)
            up_low = up_grad.astype(LOW)
            up_low_ref[rows, c : c + 512] = up_low
            mid_grad = mid_grad + dot_nt(up_low, w_up[:, c : c + 512])
        branch = norm_backward(mid_grad, normed, mid_inv[rows, :], gains[0:1, :])
        branch_low = branch.astype(LOW)
        branch_out[rows, :] = branch
        branch_ref[rows, :] = branch_low
        att_grad_out[rows, :] = dot_nt(branch_low, w_out[...]).astype(LOW)
        sums_out[0:1, :] += col_sum(mid_grad * normed)
        sums_out[1:2, :] += col_sum(grad * normed_final)
        sums_out[2:3, :] += col_sum(branch)
        sums_out[3:4, :] += col_sum(mid_grad)
        sums_out[4:5, :] += col_sum(ffn)
        sums_out[5:6, :] += col_sum(grad)
        return carry

    lax.fori_loop(0, count // size, dense, 0)
    feed_forward_grads(
        mid_ref, up_low_ref, ffn_ref, active_ref, hid_in, branch_ref,
        keep_rows, send_rows, keep_cols, send_cols, held_ref, held_cols, down_ref, mine, order,
    )


VMEM = pl.BlockSpec(memory_space=pltpu.VMEM)
SMEM = pl.BlockSpec(memory_space=pltpu.SMEM)


def call(kernel, name, flops, scalars, operands, outs, scratch=()):
    shapes = [jax.ShapeDtypeStruct(shape, dtype) for shape, dtype in outs]
    moved = sum(math.prod(o.shape) * o.dtype.itemsize for o in (*operands, *shapes))
    return pl.pallas_call(
        kernel,
        name=name,
        out_shape=shapes,
        in_specs=[SMEM] * len(scalars) + [VMEM] * len(operands),
        out_specs=[VMEM] * len(shapes),
        scratch_shapes=[pltpu.VMEM(shape, dtype) for shape, dtype in scratch],
        cost_estimate=pl.CostEstimate(flops=int(flops), bytes_accessed=int(moved), transcendentals=0),
        compiler_params=pltpu.CompilerParams(vmem_limit_bytes=56 * 1024 * 1024),
    )(*scalars, *operands)


def log2(number):
    bits = number.bit_length() - 1
    assert number == 1 << bits
    return bits


def swapped(value, axis, bit, devices):
    return lax.ppermute(value, axis, [(i, i ^ (1 << bit)) for i in range(devices)])


def reduced(keep, send, order, devices, seq_count):
    received = []
    size = keep.shape[0]
    for stage, bit in enumerate(order):
        if stage:
            half = size // 2
            total = keep[half:size].astype(F32)
            for part in received:
                total = total + part[half:size].astype(F32)
            send = total.astype(LOW)
            size = half
        received.append(swapped(send, "dp", bit, devices))
    total = keep[:1].astype(F32)
    for part in received:
        total = total + part[:1].astype(F32)
    total = total[0]
    for bit in range(log2(seq_count)):
        low = lax.optimization_barrier(total.astype(LOW))
        total = low.astype(F32) + swapped(low, "seq", bit, seq_count).astype(F32)
    return total


def summed_small(value, devices, seq_count):
    for bit in range(log2(devices)):
        value = value + swapped(value, "dp", bit, devices)
    for bit in range(log2(seq_count)):
        value = value + swapped(value, "seq", bit, seq_count)
    return value


def from_shards(own, index, count):
    others = [
        lax.ppermute(own, "seq", [((i + s) % count, i) for i in range(count)]) for s in range(1, count)
    ]
    return jnp.stack(others)


def natural(own, others, index, count):
    if count == 2:
        first = index == 0
        return jnp.concatenate(
            [jnp.where(first, own, others[0]), jnp.where(first, others[0], own)], axis=0
        )
    turned = jnp.concatenate([own[None], others], axis=0)
    return jnp.concatenate(
        [
            lax.dynamic_index_in_dim(turned, lax.rem(b - index + count, count), 0, keepdims=False)
            for b in range(count)
        ],
        axis=0,
    )


def local(
    src_embed, tgt_embed, src_lengths, tgt_lengths, enc_cotangent, dec_cotangent,
    enc_inproj, enc_outproj, enc_upproj, enc_downproj, enc_gains, enc_biases, enc_upbias,
    dec_inproj, dec_outproj, cross_query, cross_keyval, cross_outproj, dec_upproj, dec_downproj,
    dec_gains, dec_biases, dec_upbias,
):
    _, count, features = src_embed.shape
    total = tgt_embed.shape[1]
    hidden = enc_upproj.shape[1]
    devices = lax.axis_size("dp")
    seq_count = lax.axis_size("seq")
    blocks = count // BLOCK
    share = features // devices
    order = tuple(range(log2(devices)))
    half = devices // 2
    seq_index = lax.axis_index("seq")
    dp_index = lax.axis_index("dp")
    idx = jnp.where(jnp.arange(2) == 0, seq_index, dp_index).astype(jnp.int32)
    table = jnp.asarray(place_table(features))
    src_own, tgt_all = src_embed[0], tgt_embed[0]
    enc_cot = enc_cotangent[0]
    dec_cot = lax.dynamic_slice_in_dim(dec_cotangent[0], seq_index * count, count, 0)
    enc_ub, dec_ub = enc_upbias[None], dec_upbias[None]
    up = [(i, i + 1) for i in range(seq_count - 1)]
    down = [(i + 1, i) for i in range(seq_count - 1)]

    left = lax.ppermute(src_own[count - BLOCK :], "seq", up)
    right = lax.ppermute(src_own[:BLOCK], "seq", down)

    def rows_pair(columns):
        shape = ((half, share, columns), LOW)
        return [shape, shape]

    def cols_pair():
        shape = ((half, features, hidden // devices), LOW)
        return [shape, shape]

    held_rows = ((devices, share, 512), LOW)
    held_cols = ((devices, features, hidden // devices), LOW)
    weight = 2 * count * features

    tgt_in, tgt_low, dec_rows = call(
        functools.partial(dec_pre_kernel, total), "dec_pre", weight * 1536, [idx],
        [tgt_all, tgt_lengths, table, dec_inproj, dec_biases],
        [((count, features), F32), ((count, features), LOW), ((count + BLOCK, 1536), LOW)],
    )
    (enc_rows, src_low, enc_lse, enc_hid, mid_normed, mid_inv, fin_normed, fin_inv, encoded) = call(
        functools.partial(enc_kernel, total), "enc_forward", weight * 8192, [idx],
        [left, src_own, right, src_lengths, table, enc_inproj, enc_outproj, enc_upproj, enc_downproj,
         enc_gains, enc_biases, enc_ub],
        [((count + 2 * BLOCK, 1536), LOW), ((count, features), LOW), ((blocks, 2, 512), F32),
         ((count, features), LOW), ((count, features), F32), ((count, 1), F32),
         ((count, features), F32), ((count, 1), F32), ((count, features), LOW)],
        [((count, features), F32)],
    )
    others = from_shards(encoded, seq_index, seq_count)
    dec_lse, dec_hid, self_normed, self_inv, cross_q = call(
        functools.partial(dec_self_kernel, total), "dec_self", weight * 4096, [idx],
        [tgt_in, dec_rows, tgt_lengths, dec_outproj, cross_query, dec_gains, dec_biases],
        [((blocks, 2, 512), F32), ((count, features), LOW), ((count, features), F32),
         ((count, 1), F32), ((count, features), LOW)],
    )
    cross_att, cross_lse, keyval, memory = call(
        functools.partial(cross_kernel, total), "cross", weight * 6144, [idx, src_lengths, tgt_lengths],
        [cross_q, encoded, others, src_lengths, tgt_lengths, cross_keyval, dec_biases],
        [((count, features), F32), ((blocks, 2, 512), F32), ((total + WINDOW, 1024), LOW),
         ((total, features), LOW)],
        [((HEADS, BLOCK), F32), ((HEADS, BLOCK), F32), ((features, BLOCK), F32)],
    )
    decoded, cross_att_grad, cross_branch, tail_sums, tail_keep, tail_send, down_keep, down_send = call(
        functools.partial(dec_tail_kernel, order), "dec_tail", weight * 16384, [idx],
        [cross_att, self_normed, dec_cot, cross_outproj, dec_upproj, dec_downproj, dec_gains,
         dec_biases, dec_ub],
        [((count, features), LOW), ((count, features), LOW), ((count, features), F32),
         ((16, features), F32), *rows_pair(hidden + 512), *cols_pair()],
        [((count, features), LOW), ((count, features), LOW), ((count, features), LOW),
         ((min(256, count), hidden), F32), ((count, hidden), LOW), ((count, features), LOW),
         ((count, hidden), LOW), held_rows, held_cols, ((features, hidden), LOW)],
    )
    mem_own, mem_send, self_branch, self_att_grad, cross_sums, cross_keep, cross_send = call(
        functools.partial(cross_back_kernel, total, order), "cross_back", weight * 10240,
        [idx, src_lengths, tgt_lengths],
        [cross_q, keyval, memory, cross_att, cross_att_grad, cross_lse, src_lengths, tgt_lengths,
         cross_keyval, cross_query, dec_outproj, self_normed, self_inv, cross_branch, dec_hid, dec_gains,
         dec_biases],
        [((count, features), F32), ((seq_count - 1, count, features), LOW), ((count, features), F32),
         ((count, features), LOW), ((8, features), F32), *rows_pair(2048)],
        [((total + WINDOW, 1024), F32), ((count, features), F32), ((count, features), LOW),
         ((total, 1024), LOW), ((count, features), LOW), ((count, features), LOW), held_rows],
    )
    mem_others = jnp.stack(
        [
            lax.ppermute(mem_send[s - 1], "seq", [(i, (i + s) % seq_count) for i in range(seq_count)])
            for s in range(1, seq_count)
        ]
    )
    self_own, self_halo = call(
        functools.partial(dec_self_back_kernel, total), "dec_self_back", weight * 4096, [idx],
        [dec_rows, self_att_grad, dec_lse, tgt_lengths],
        [((count, 1536), F32), ((BLOCK, 1024), LOW)],
        [((count, features), F32), ((count + BLOCK, 1024), F32)],
    )
    self_returned = lax.ppermute(self_halo, "seq", down)
    enc_branch, enc_att_grad, enc_sums, enc_keep, enc_send, enc_down_keep, enc_down_send = call(
        functools.partial(enc_tail_back_kernel, order), "enc_tail_back", weight * 12288, [idx],
        [enc_cot, mem_own, mem_others, fin_normed, fin_inv, mid_normed, mid_inv, enc_hid, enc_outproj,
         enc_upproj, enc_downproj, enc_gains, enc_biases, enc_ub],
        [((count, features), F32), ((count, features), LOW), ((16, features), F32),
         *rows_pair(hidden + 512), *cols_pair()],
        [((count, features), LOW), ((count, features), LOW), ((count, hidden), LOW),
         ((count, features), LOW), ((count, hidden), LOW), held_rows, held_cols, ((features, hidden), LOW)],
    )
    tgt_part, self_sums, self_keep, self_send = call(
        functools.partial(dec_input_grad_kernel, order), "dec_input_grad", weight * 3072, [idx],
        [self_own, self_returned, self_branch, tgt_low, dec_inproj],
        [((count, features), LOW), ((8, features), F32), *rows_pair(1536)],
        [((count, 1536), LOW), ((count, 1536), F32), held_rows],
    )
    enc_own, halo_left, halo_right = call(
        functools.partial(enc_self_back_kernel, total), "enc_self_back", weight * 4096, [idx],
        [enc_rows, enc_att_grad, enc_lse, src_lengths],
        [((count, 1536), F32), ((BLOCK, 1024), LOW), ((BLOCK, 1024), LOW)],
        [((count, features), F32), ((count + 2 * BLOCK, 1024), F32)],
    )
    after = lax.ppermute(halo_left, "seq", down)
    before = lax.ppermute(halo_right, "seq", up)
    src_grad, in_sums, in_keep, in_send = call(
        functools.partial(enc_input_grad_kernel, order), "enc_input_grad", weight * 3072, [idx],
        [enc_own, before, after, enc_branch, src_low, enc_inproj],
        [((count, features), F32), ((8, features), F32), *rows_pair(1536)],
        [((count, 1536), LOW), ((count, 1536), F32), held_rows],
    )

    finish = functools.partial(reduced, order=order, devices=devices, seq_count=seq_count)
    tail = finish(tail_keep, tail_send)
    dec_down = finish(down_keep, down_send)
    cross = finish(cross_keep, cross_send)
    selves = finish(self_keep, self_send)
    enc = finish(enc_keep, enc_send)
    enc_down = finish(enc_down_keep, enc_down_send)
    inputs = finish(in_keep, in_send)
    small = summed_small(
        jnp.concatenate([tail_sums, enc_sums, cross_sums, self_sums, in_sums], axis=0), devices, seq_count
    )
    tail_s, enc_s = small[:16], small[16:32]
    cross_s, self_s, in_s = small[32:40], small[40:48], small[48:56]

    def columns(rows):
        return lax.dynamic_slice_in_dim(jnp.concatenate(rows, axis=0), dp_index * share, share, 1)

    def hidden_part(rows):
        width = hidden // devices
        return lax.dynamic_slice_in_dim(rows.reshape(hidden), dp_index * width, width, 0)

    dec_gains_grad = columns([cross_s[0:1], tail_s[0:2]])
    dec_biases_grad = columns(
        [self_s[0:2], cross_s[1:4], cross_s[4:5], tail_s[2:6]]
    )
    enc_gains_grad = columns([enc_s[0:2]])
    enc_biases_grad = columns([in_s[0:2], enc_s[2:6]])
    decoded_all = natural(decoded, from_shards(decoded, seq_index, seq_count), seq_index, seq_count)
    tgt_all_grad = natural(
        tgt_part, from_shards(tgt_part, seq_index, seq_count), seq_index, seq_count
    ).astype(F32)
    return (
        encoded[None],
        decoded_all[None],
        src_grad[None],
        tgt_all_grad[None],
        inputs,
        enc[:, hidden:],
        enc[:, :hidden],
        enc_down.T,
        enc_gains_grad,
        enc_biases_grad,
        hidden_part(enc_s[8:12]),
        selves,
        cross[:, 1536:],
        cross[:, 1024:1536],
        cross[:, :1024],
        tail[:, hidden:],
        tail[:, :hidden],
        dec_down.T,
        dec_gains_grad,
        dec_biases_grad,
        hidden_part(tail_s[8:12]),
    )


def solution(mesh):
    rows, whole = P("dp", "seq", None), P("dp", None, None)
    return jax.shard_map(
        local,
        mesh=mesh,
        in_specs=(rows, whole, P("dp", None), P("dp", None), rows, whole, *([P()] * 17)),
        out_specs=(
            rows, whole, rows, whole,
            *([P("dp", None)] * 4), P(None, "dp"), P(None, "dp"), P("dp"),
            *([P("dp", None)] * 7), P(None, "dp"), P(None, "dp"), P("dp"),
        ),
        check_vma=False,
    )
```

```python
import functools
import math

import jax
import jax.numpy as jnp
import numpy as np
from jax import lax
from jax.experimental import pallas as pl
from jax.experimental.pallas import tpu as pltpu
from jax.sharding import PartitionSpec as P

HEADS = 8
HEAD_DIM = 64
MAXPAIR = 128
BLOCK = 128
GROUP = 256
WINDOW = 256
LOW = jnp.bfloat16
F32 = jnp.float32
MASKED = -1e30
FEATURES = 512
HIDDEN = 2048


def place_table(features):
    half = features // 2
    frequency = np.exp(-math.log(10000.0) * np.arange(half, dtype=np.float32) / np.float32(half)).astype(np.float32)
    angles = (np.arange(MAXPAIR, dtype=np.float32)[:, None] * frequency[None, :]).astype(np.float32)
    table = np.concatenate([np.sin(angles), np.cos(angles)], axis=-1).astype(np.float32)
    pieces, rest = [], table
    for _ in range(3):
        piece = rest.astype(jnp.bfloat16)
        pieces.append(piece)
        rest = rest - piece.astype(np.float32)
    return np.stack(pieces)


def dot_nn(left, right):
    return lax.dot_general(left, right, (((1,), (0,)), ((), ())), preferred_element_type=F32)


def dot_nt(left, right):
    return lax.dot_general(left, right, (((1,), (1,)), ((), ())), preferred_element_type=F32)


def dot_tn(left, right):
    return lax.dot_general(left, right, (((0,), (0,)), ((), ())), preferred_element_type=F32)


def iota(shape, dim):
    return lax.broadcasted_iota(jnp.int32, shape, dim).astype(F32)


def pair_ends(len_row):
    count = len_row.shape[1]
    lengths = jnp.broadcast_to(len_row, (count, count))
    down, across = iota((count, count), 0), iota((count, count), 1)
    ends_col = jnp.sum(jnp.where(across <= down, lengths, 0.0), axis=1, keepdims=True)
    len_col = jnp.sum(jnp.where(across == down, lengths, 0.0), axis=1, keepdims=True)
    ends_row = jnp.sum(jnp.where(down <= across, len_col, 0.0), axis=0, keepdims=True)
    return (ends_row, ends_col)


def pair_col(ends_row, places, total):
    number = jnp.sum(jnp.where(ends_row <= places, 1.0, 0.0), axis=1, keepdims=True)
    return jnp.where((places >= 0.0) & (places < total), number, -1.0)


def pair_row(ends_col, places):
    return jnp.sum(jnp.where(ends_col <= places, 1.0, 0.0), axis=0, keepdims=True)


def with_places(embed, places, ends_row, len_row, table_ref):
    started = jnp.sum(jnp.where(ends_row <= places, len_row, 0.0), axis=1, keepdims=True)
    inside = places - started
    hot = jnp.where(iota((embed.shape[0], MAXPAIR), 1) == inside, 1.0, 0.0).astype(LOW)
    sines = dot_nn(hot, table_ref[0]) + dot_nn(hot, table_ref[1]) + dot_nn(hot, table_ref[2])
    return embed.astype(F32) + sines


def norm_forward(values, gain_row, shift_row):
    centred = values - jnp.mean(values, axis=-1, keepdims=True)
    inverse = lax.rsqrt(jnp.mean(centred * centred, axis=-1, keepdims=True) + 1e-05)
    normed = centred * inverse
    return (normed * gain_row + shift_row, normed, inverse)


def norm_backward(grad_rows, normed, inverse, gain_row):
    scaled = grad_rows * gain_row
    return inverse * (
        scaled
        - jnp.mean(scaled, axis=-1, keepdims=True)
        - normed * jnp.mean(scaled * normed, axis=-1, keepdims=True)
    )


def sigmoid(values):
    return 0.5 * jnp.tanh(0.5 * values) + 0.5


def col_sum(values):
    return jnp.sum(values, axis=0, keepdims=True)


def head_masks(scale):
    lane = lax.broadcasted_iota(jnp.int32, (1, GROUP), 1) // HEAD_DIM
    return [jnp.where(lane == h, scale, 0.0).astype(LOW) for h in range(GROUP // HEAD_DIM)]


def spread(rows, masks):
    return jnp.concatenate([rows * mask for mask in masks], axis=0)


def diagonal(wide):
    count = GROUP // HEAD_DIM
    return [
        wide[h * HEAD_DIM : (h + 1) * HEAD_DIM, h * BLOCK : (h + 1) * BLOCK] for h in range(count)
    ]


def attend_block(query, keys, values, bias, group):
    lanes = slice(group * GROUP, (group + 1) * GROUP)
    stacked = spread(query(lanes), head_masks(HEAD_DIM**-0.5))
    scores = dot_nt(keys(lanes), stacked)
    probs, maxima, sums = [], [], []
    for h in range(GROUP // HEAD_DIM):
        score = scores[:, h * BLOCK : (h + 1) * BLOCK] + bias
        row_max = jnp.max(score, axis=0, keepdims=True)
        exp_score = jnp.exp(score - row_max)
        maxima.append(row_max)
        sums.append(col_sum(exp_score))
        probs.append(exp_score.astype(LOW))
    wide = dot_tn(values(lanes), jnp.concatenate(probs, axis=1))
    return (diagonal(wide), maxima, sums)


def attend_local(rows_ref, count, width, att_ref, lse_ref, rule):
    def body(j, carry):
        first = pl.multiple_of(j * BLOCK, BLOCK)
        queries = pl.ds(pl.multiple_of(first + BLOCK, BLOCK), BLOCK)
        keys = pl.ds(first, width)
        bias = rule(first)
        for group in range(2):
            def part(rows, offset):
                return lambda lanes: rows_ref[rows, offset + lanes.start : offset + lanes.stop]

            outs, maxima, sums = attend_block(
                part(queries, 0), part(keys, 512), part(keys, 1024), bias, group
            )
            mixed = jnp.concatenate([o * (1.0 / s) for o, s in zip(outs, sums)], axis=0)
            att_ref[pl.ds(first, BLOCK), group * GROUP : (group + 1) * GROUP] = mixed.T.astype(
                att_ref.dtype
            )
            lse_ref[j, group : group + 1, :] = jnp.concatenate(
                [m + jnp.log(s) for m, s in zip(maxima, sums)], axis=1
            )
        return carry

    lax.fori_loop(0, count, body, 0)


def attend_back_block(query, grad, keys, values, bias, lse, deltas):
    stacked = spread(query, head_masks(HEAD_DIM**-0.5))
    grads = spread(grad, head_masks(1.0))
    scores = dot_nt(keys, stacked)
    prob_grads = dot_nt(values, grads)
    probs, score_grads = [], []
    for h in range(GROUP // HEAD_DIM):
        cols = slice(h * BLOCK, (h + 1) * BLOCK)
        prob = jnp.exp(scores[:, cols] + bias - lse[:, cols])
        prob_grad = prob_grads[:, cols]
        delta = col_sum(prob * prob_grad) if deltas is None else deltas[h]
        score_grads.append((prob * (prob_grad - delta)).astype(LOW))
        probs.append(prob.astype(LOW))
    prob_wide = jnp.concatenate(probs, axis=1)
    grad_wide = jnp.concatenate(score_grads, axis=1)
    value_grad = dot_nn(prob_wide, grads)
    key_grad = dot_nn(grad_wide, stacked)
    query_grad = jnp.concatenate(diagonal(dot_tn(keys, grad_wide)), axis=0) * HEAD_DIM**-0.5
    return (query_grad, key_grad, value_grad)


def attend_local_back(rows_ref, grad_ref, lse_ref, count, width, query_ref, keyval_ref, rule):
    keyval_ref[...] = jnp.zeros(keyval_ref.shape, F32)

    def body(j, carry):
        first = pl.multiple_of(j * BLOCK, BLOCK)
        queries = pl.ds(pl.multiple_of(first + BLOCK, BLOCK), BLOCK)
        own = pl.ds(first, BLOCK)
        keys = pl.ds(first, width)
        bias = rule(first)
        for group in range(2):
            low, high = group * GROUP, (group + 1) * GROUP
            query_grad, key_grad, value_grad = attend_back_block(
                rows_ref[queries, low:high],
                grad_ref[own, low:high],
                rows_ref[keys, 512 + low : 512 + high],
                rows_ref[keys, 1024 + low : 1024 + high],
                bias,
                lse_ref[j, group : group + 1, :],
                None,
            )
            query_ref[own, low:high] = query_grad.T
            keyval_ref[keys, low:high] += key_grad
            keyval_ref[keys, 512 + low : 512 + high] += value_grad
        return carry

    lax.fori_loop(0, count, body, 0)


def self_rule(ends, start, total, width, causal):
    ends_row, ends_col = ends

    def rule(first):
        shift = (start + first).astype(F32)
        key_places = iota((width, 1), 0) + (shift - BLOCK)
        query_places = iota((1, BLOCK), 1) + shift
        allowed = pair_col(ends_row, key_places, total) == pair_row(ends_col, query_places)
        if causal:
            allowed = allowed & (key_places <= query_places)
        return jnp.where(allowed, 0.0, MASKED)

    return rule


class Loaded:
    def __init__(self, ref):
        self.ref = ref

    def get(self):
        return self.ref


class Coming:
    def __init__(self, far, near, sem):
        self.near = near
        self.copy = pltpu.make_async_copy(far, near, sem)
        self.copy.start()
        self.waiting = True

    def get(self):
        if self.waiting:
            self.copy.wait()
            self.waiting = False
        return self.near


class Leaving:
    def __init__(self, near, far, sem):
        self.ref = near
        self.copy = pltpu.make_async_copy(near, far, sem)
        self.started = False

    def flush(self):
        if not self.started:
            self.copy.start()
            self.started = True

    def finish(self):
        self.flush()
        self.copy.wait()


OVER_SEQ = "seq"


def put_rows(held, result, col):
    devices, rows, _ = held.shape
    width = result.shape[1]
    low = result.astype(LOW)
    for i in range(devices):
        held[i, :, col : col + width] = low[i * rows : (i + 1) * rows, :]


class Blocks:
    def __init__(self, keep, send, held, sems, numbers, order):
        self.keep, self.send, self.held, self.sems = (keep, send, held, sems)
        self.numbers, self.order = (numbers, order)
        self.used = []

    def spread(self, col, width):
        half, bits = (self.keep.shape[0], len(self.order))
        chunk = len(self.used)
        seq, mine = self.numbers[0], self.numbers[1]
        for place in range(2 * half):
            flips = {bit: (place >> (bits - 1 - s)) & 1 for s, bit in enumerate(self.order)}
            source = target = pl.ds(col, width)
            if OVER_SEQ in flips:
                source = pl.ds(pl.multiple_of((seq ^ flips.pop(OVER_SEQ)) * (width // 2), BLOCK), width // 2)
                target = pl.ds(0, width // 2)
            flip = sum(value << bit for bit, value in flips.items())
            refs = self.keep if place < half else self.send
            pltpu.make_async_copy(
                self.held.at[mine ^ flip, :, source],
                refs.at[place % half, :, target],
                self.sems.at[chunk],
            ).start()
        self.used.append(pl.ds(col, width))

    def fill(self, source, col):
        width = source.ref.shape[2]
        self.filling = pltpu.make_async_copy(
            source.ref, self.held.at[:, :, pl.ds(col, width)], self.sems.at[15]
        )
        self.filling.start()

    def filled(self):
        self.filling.wait()

    def put_rows(self, result, col):
        put_rows(self.held, result, col)

    def put_cols(self, result, sums, first, col):
        devices, rows, _ = self.held.shape
        width = result.shape[1] // (result.shape[1] * devices // HIDDEN)
        pieces = BLOCK // width
        low = result.astype(LOW)
        tall = low.shape[0] // pieces
        top = iota((rows, width), 0) == 0.0
        for n in range(result.shape[1] // width):
            at = slice(n * width, (n + 1) * width)
            piece = [low[p * tall : (p + 1) * tall, at] for p in range(pieces)]
            piece = piece[0] if pieces == 1 else jnp.concatenate(piece, axis=1)
            for g in range(tall // rows):
                self.held[first + n, :, col + g * BLOCK : col + (g + 1) * BLOCK] = piece[
                    g * rows : (g + 1) * rows, :
                ]
            row = jnp.where(top, sums[:, at], 0.0).astype(LOW)
            row = row if pieces == 1 else jnp.concatenate([row] * pieces, axis=1)
            end = col + (tall // rows) * BLOCK
            self.held[first + n, :, end : end + BLOCK] = row

    def finish(self):
        for chunk, cols in enumerate(self.used):
            whole = self.held.at[:, :, cols]
            pltpu.make_async_copy(whole, whole, self.sems.at[chunk]).wait()


NEAR, FAR, RAW = "near", "far", "raw"
IN_HBM = pl.BlockSpec(memory_space=pltpu.HBM)
IN_VMEM = pl.BlockSpec(memory_space=pltpu.VMEM)
IN_SMEM = pl.BlockSpec(memory_space=pltpu.SMEM)


LIMITS = {'rows_unpack': 14, 'tail_unpack': 6, 'last_unpack': 8, 'dec_pre': 8, 'enc_forward': 16, 'dec_self': 6, 'cross_tail': 27, 'cross_back': 13, 'dec_self_back': 18, 'enc_tail_back': 20, 'enc_self_back': 12, 'dec_input_grad': 10, 'enc_input_grad': 9}
MICROS = {'dec_pre': 30, 'enc_forward': 30, 'dec_self': 30, 'cross_tail': 30, 'cross_back': 30, 'dec_self_back': 30, 'enc_tail_back': 30, 'enc_self_back': 30, 'dec_input_grad': 30, 'enc_input_grad': 30}


def call(kernel, name, scalars, operands, outs, scratch=(), blocks=(), order=(), ahead=()):
    arrays, specs = [], []
    for array, mode, *_ in (*operands, *ahead):
        near = mode == NEAR
        arrays.append(pltpu.with_memory_space_constraint(array, pltpu.VMEM if near else pltpu.HBM))
        specs.append(IN_VMEM if near else IN_HBM)

    def taken(array, mode, start=None, size=None):
        return array.shape if size is None else (size, *array.shape[1:])

    shapes, out_specs = [], []
    for shape, dtype, mode in outs:
        shapes.append((pltpu.VMEM if mode == NEAR else pltpu.HBM)(shape, dtype))
        out_specs.append(IN_VMEM if mode == NEAR else IN_HBM)
    over_seq = OVER_SEQ in order
    devices = 1 << (len(order) - over_seq)
    share = FEATURES // devices
    for columns in blocks:
        shapes += [pltpu.HBM(((1 << len(order)) // 2, share, columns // (1 + over_seq)), LOW)] * 2
        out_specs += [IN_HBM] * 2
    for one in ahead:
        shapes.append(pltpu.VMEM(taken(*one), one[0].dtype))
        out_specs.append(IN_VMEM)
    far_in = [i for i, one in enumerate(operands) if one[1] == FAR]
    far_out = [i for i, one in enumerate(outs) if one[2] == FAR]
    extra = [pltpu.VMEM(shape, dtype) for shape, dtype in scratch]
    extra += [pltpu.VMEM(taken(*operands[i]), operands[i][0].dtype) for i in far_in]
    extra += [pltpu.VMEM(outs[i][0], outs[i][1]) for i in far_out]
    extra += [pltpu.VMEM((devices, share, columns), LOW) for columns in blocks]
    extra += [pltpu.SemaphoreType.DMA((len(far_in) + len(far_out) + len(ahead) + 1,))]
    extra += [pltpu.SemaphoreType.DMA((16,)) for _ in blocks]

    def body(*refs):
        refs = list(refs)
        take = lambda n: [refs.pop(0) for _ in range(n)]
        numbers = take(len(scalars))
        ins = take(len(operands))
        sources = take(len(ahead))
        results = take(len(outs))
        sends = [take(2) for _ in blocks]
        copies = take(len(ahead))
        temps = take(len(scratch))
        near_in = take(len(far_in))
        near_out = take(len(far_out))
        helds = take(len(blocks))
        sems = take(1)[0]
        block_sems = take(len(blocks))
        used = iter(range(len(far_in) + len(far_out) + len(ahead)))

        def coming(ref, near, array, mode, start=None, size=None):
            source = ref if size is None else ref.at[pl.ds(start(numbers[0]), size)]
            return Coming(source, near, sems.at[next(used)])

        given = [Loaded(ref) for ref in ins]
        for n, i in enumerate(far_in):
            given[i] = coming(ins[i], near_in[n], *operands[i])
        later = [coming(ref, near, *one) for ref, near, one in zip(sources, copies, ahead)]
        leaving = {}
        for n, i in enumerate(far_out):
            leaving[i] = Leaving(near_out[n], results[i], sems.at[next(used)])
        made = [leaving.get(i, Loaded(results[i])) for i in range(len(outs))]
        moved = [
            Blocks(keep, send, held, sem, numbers[0], order)
            for (keep, send), held, sem in zip(sends, helds, block_sems)
        ]
        kernel(numbers, given, made, temps, *moved)
        for one in leaving.values():
            one.flush()
        for one in (*given, *later):
            one.get()
        for one in leaving.values():
            one.finish()
        for one in moved:
            one.finish()

    results = pl.pallas_call(
        body,
        name=name,
        out_shape=shapes,
        in_specs=[IN_SMEM] * len(scalars) + specs,
        out_specs=out_specs,
        scratch_shapes=extra,
        cost_estimate=pl.CostEstimate(flops=int(MICROS.get(name, 1) * 1.0 * 1.15e9), bytes_accessed=1, transcendentals=0),
        compiler_params=pltpu.CompilerParams(vmem_limit_bytes=LIMITS[name] * 1024 * 1024),
    )(*scalars, *arrays)
    made = len(outs) + 2 * len(blocks)
    return (results[: len(outs)], results[len(outs) : made], results[made:])


def input_rows(numbers, embeds, lens, table, w_in, biases, x_ref, low_ref, rows_ref, start, count, ends, len_row):
    def chunk(embed, rows, target, size):
        places = iota((size, 1), 0) + (start + target - BLOCK).astype(F32)
        x = with_places(embed, places, ends[0], len_row, table)
        low = x.astype(LOW)
        if rows is not None:
            x_ref[rows : rows + size, :] = x
            low_ref[rows : rows + size, :] = low
        for c in range(3):
            part = dot_nn(low, w_in[:, c * 512 : (c + 1) * 512])
            if c != 1:
                part = part + biases[c // 2 : c // 2 + 1, :]
            rows_ref[target : target + size, c * 512 : (c + 1) * 512] = part.astype(LOW)

    for embed, rows, target, size in embeds:
        chunk(embed, rows, target, size)


def dec_pre_kernel(numbers, ins, outs, temps):
    halo, own, lens, table, w, biases = ins
    x_out, low_out, rows_out = [o.ref for o in outs]
    count = x_out.shape[0]
    start = numbers[0][0] * count
    len_row = lens.get()[...].astype(F32)
    ends = pair_ends(len_row)
    halo, own, table, w, biases = [i.get() for i in (halo, own, table, w, biases)]
    size = min(256, count)
    embeds = [(halo[...], None, 0, BLOCK)]
    embeds += [(own[at : at + size, :], at, BLOCK + at, size) for at in range(0, count, size)]
    input_rows(numbers, embeds, lens, table, w, biases, x_out, low_out, rows_out, start, count, ends, len_row)


def enc_kernel(numbers, ins, outs, temps, total):
    left, own, right, lens, table, w_in, gains, biases, upbias, w_out, w_up, w_down = ins
    rows_out, low_out, lse_out, hid_out, mid_out, mid_inv_out, fin_out, fin_inv_out, encoded_out = outs
    (x_ref,) = temps
    count = x_ref.shape[0]
    start = numbers[0][0] * count
    len_row = lens.get()[...].astype(F32)
    ends = pair_ends(len_row)
    size = min(256, count)
    left, own, right, table, w_in, gains, biases, upbias = [
        i.get() for i in (left, own, right, table, w_in, gains, biases, upbias)
    ]
    embeds = [(left[...], None, 0, BLOCK)]
    embeds += [(own[at : at + size, :], at, BLOCK + at, size) for at in range(0, count, size)]
    embeds += [(right[...], None, BLOCK + count, BLOCK)]
    input_rows(
        numbers, embeds, lens, table, w_in, biases, x_ref, low_out.ref, rows_out.ref, start, count, ends, len_row
    )
    low_out.flush()
    rows_out.flush()
    width = 3 * BLOCK
    attend_local(
        rows_out.ref, count // BLOCK, width, hid_out.ref, lse_out.ref,
        self_rule(ends, start, total, width, False),
    )
    lse_out.flush()
    hid_out.flush()
    w_out, w_up, w_down = w_out.get(), w_up.get(), w_down.get()
    hid, mid_ref, mid_inv, fin_ref, fin_inv, encoded = [
        o.ref for o in (hid_out, mid_out, mid_inv_out, fin_out, fin_inv_out, encoded_out)
    ]

    def dense(step, carry):
        rows = pl.ds(pl.multiple_of(step * size, size), size)
        z = x_ref[rows, :] + dot_nn(hid[rows, :], w_out[...]) + biases[2:3, :]
        mid, normed, inverse = norm_forward(z, gains[0:1, :], biases[3:4, :])
        mid_ref[rows, :] = normed
        mid_inv[rows, :] = inverse
        low = mid.astype(LOW)
        z = mid + biases[4:5, :]
        for c in range(0, w_up.shape[1], 512):
            up = dot_nn(low, w_up[:, c : c + 512]) + upbias[:, c : c + 512]
            active = (up * sigmoid(up)).astype(LOW)
            z = z + dot_nn(active, w_down[c : c + 512, :])
        final, normed, inverse = norm_forward(z, gains[1:2, :], biases[5:6, :])
        fin_ref[rows, :] = normed
        fin_inv[rows, :] = inverse
        encoded[rows, :] = final.astype(LOW)
        return carry

    lax.fori_loop(0, count // size, dense, 0)


def dec_self_kernel(numbers, ins, outs, temps, total):
    x, rows_in, lens, gains, biases, w_out, w_query = ins
    lse_out, hid_out, normed_out, inv_out, query_out = outs
    x, rows_in, gains, biases = [i.get() for i in (x, rows_in, gains, biases)]
    count = x.shape[0]
    start = numbers[0][0] * count
    ends = pair_ends(lens.get()[...].astype(F32))
    width = 2 * BLOCK
    attend_local(
        rows_in, count // BLOCK, width, hid_out.ref, lse_out.ref,
        self_rule(ends, start, total, width, True),
    )
    size = min(256, count)
    w_out, w_query = w_out.get(), w_query.get()
    hid, normed_ref, inv_ref, query_ref = [o.ref for o in (hid_out, normed_out, inv_out, query_out)]

    def dense(step, carry):
        rows = pl.ds(pl.multiple_of(step * size, size), size)
        z = x[rows, :] + dot_nn(hid[rows, :], w_out[...]) + biases[2:3, :]
        mid, normed, inverse = norm_forward(z, gains[0:1, :], biases[3:4, :])
        normed_ref[rows, :] = normed
        inv_ref[rows, :] = inverse
        query = dot_nn(mid.astype(LOW), w_query[...]) + biases[4:5, :]
        query_ref[rows, :] = query.astype(LOW)
        return carry

    lax.fori_loop(0, count // size, dense, 0)


def cross_span(src_lens, tgt_lens, first):
    def step(k, carry):
        begin, low, high = carry
        end = begin + tgt_lens[0, k]
        length = src_lens[0, k]
        low = low + jnp.where(end <= first, length, 0)
        high = high + jnp.where(begin <= first + (BLOCK - 1), length, 0)
        return (end, low, high)

    zero = jnp.int32(0)
    _, low, high = lax.fori_loop(0, src_lens.shape[1], step, (zero, zero, zero), unroll=True)
    low = (low // 16) * 16
    return (low, (high - low + (WINDOW - 1)) // WINDOW)


def cross_rule(src_ends_row, tgt_ends_col, first, begin, total):
    key_places = iota((WINDOW, 1), 0) + begin.astype(F32)
    query_places = iota((1, BLOCK), 1) + first.astype(F32)
    allowed = pair_col(src_ends_row, key_places, total) == pair_row(tgt_ends_col, query_places)
    return jnp.where(allowed, 0.0, MASKED)


def cross_forward(numbers, query, memory, others, src_vec, tgt_vec, biases, w, att_out, lse_out, keyval_out, memory_out, max_ref, sum_ref, acc_ref, total):
    idx, src_lens, tgt_lens = numbers
    count = query.shape[0]
    length = memory.shape[0]
    shards = others.shape[0] + 1
    start = idx[0] * count
    src_ends_row, _ = pair_ends(src_vec[...].astype(F32))
    _, tgt_ends_col = pair_ends(tgt_vec[...].astype(F32))
    size = min(256, length)
    for s in range(shards):
        base = lax.rem(idx[0] + s, shards) * length
        for at in range(0, length, size):
            rows = pl.ds(pl.multiple_of(base + at, BLOCK), size)
            source = memory[at : at + size, :] if s == 0 else others[s - 1, at : at + size, :]
            memory_out[rows, :] = source
            keyval_out[rows, :512] = dot_nn(source, w[:, :512]).astype(LOW)
            keyval_out[rows, 512:] = (dot_nn(source, w[:, 512:]) + biases[5:6, :]).astype(LOW)
    keyval_out[total:, :] = jnp.zeros((WINDOW, 1024), LOW)

    def body(j, carry):
        at = pl.multiple_of(j * BLOCK, BLOCK)
        rows = pl.ds(at, BLOCK)
        first = start + at
        low, windows = cross_span(src_lens, tgt_lens, first)
        max_ref[...] = jnp.full(max_ref.shape, MASKED, F32)
        sum_ref[...] = jnp.zeros(sum_ref.shape, F32)
        acc_ref[...] = jnp.zeros(acc_ref.shape, F32)

        def window(n, carry):
            begin = pl.multiple_of(low + n * WINDOW, 16)
            keys = pl.ds(begin, WINDOW)
            bias = cross_rule(src_ends_row, tgt_ends_col, first, begin, total)
            for group in range(2):
                def part(ref, rows, offset):
                    return lambda lanes: ref[rows, offset + lanes.start : offset + lanes.stop]

                outs, maxima, sums = attend_block(
                    part(query, rows, 0), part(keyval_out, keys, 0), part(keyval_out, keys, 512), bias, group
                )
                for h in range(4):
                    head = group * 4 + h
                    old = max_ref[head : head + 1, :]
                    new = jnp.maximum(old, maxima[h])
                    before, now = jnp.exp(old - new), jnp.exp(maxima[h] - new)
                    max_ref[head : head + 1, :] = new
                    sum_ref[head : head + 1, :] = sum_ref[head : head + 1, :] * before + sums[h] * now
                    part_rows = slice(head * HEAD_DIM, (head + 1) * HEAD_DIM)
                    acc_ref[part_rows, :] = acc_ref[part_rows, :] * before + outs[h] * now
            return carry

        lax.fori_loop(0, windows, window, 0)
        for group in range(2):
            heads = range(group * 4, group * 4 + 4)
            mixed = jnp.concatenate(
                [
                    acc_ref[h * HEAD_DIM : (h + 1) * HEAD_DIM, :] * (1.0 / sum_ref[h : h + 1, :])
                    for h in heads
                ],
                axis=0,
            )
            att_out[rows, group * GROUP : (group + 1) * GROUP] = mixed.T
            lse_out[j, group : group + 1, :] = jnp.concatenate(
                [max_ref[h : h + 1, :] + jnp.log(sum_ref[h : h + 1, :]) for h in heads], axis=1
            )
        return carry

    lax.fori_loop(0, count // BLOCK, body, 0)


def feed_forward_grads(mid, up_low, ffn, active, hid, branch, sums, blocks):
    hidden = up_low.shape[1]
    devices, rows, _ = blocks.held.shape
    width = hidden // devices
    for c in range(0, hidden, 512):
        blocks.put_cols(
            dot_tn(ffn[...], active[:, c : c + 512]), sums[8 + c // 512 : 9 + c // 512, :], c // width, 0
        )
    down = hidden + BLOCK
    blocks.spread(0, down)
    for c in range(0, hidden, 512):
        blocks.put_rows(dot_tn(mid[...], up_low[:, c : c + 512]), down + c)
    blocks.spread(down, hidden)
    blocks.put_rows(dot_tn(hid[...], branch[...]), down + hidden)
    blocks.spread(down + hidden, 512)


def cross_tail_kernel(numbers, ins, outs, temps, blocks, total):
    (query, memory, others, src_vec, tgt_vec, gains, biases, upbias, w_keyval, normed_in, cot, w_out, w_up, w_down) = [
        i.get() for i in ins
    ]
    att, lse_out, keyval_out, memory_out, decoded_out, att_grad_out, branch_out, sums_out = [o.ref for o in outs]
    hid_ref, branch_ref, mid_ref, up_ref, active_ref, ffn_ref, up_low_ref, *running = temps
    cross_forward(
        numbers, query, memory, others, src_vec, tgt_vec, biases, w_keyval, att, lse_out, keyval_out, memory_out,
        *running, total,
    )
    count = att.shape[0]
    hidden = w_up.shape[1]
    sums_out[...] = jnp.zeros(sums_out.shape, F32)
    size = min(256, count)

    def dense(step, carry):
        rows = pl.ds(pl.multiple_of(step * size, size), size)
        hid = att[rows, :].astype(LOW)
        hid_ref[rows, :] = hid
        first = normed_in[rows, :] * gains[0:1, :] + biases[3:4, :]
        z = first + dot_nn(hid, w_out[...]) + biases[6:7, :]
        mid, normed, inverse = norm_forward(z, gains[1:2, :], biases[7:8, :])
        low = mid.astype(LOW)
        mid_ref[rows, :] = low
        z = mid + biases[8:9, :]
        for c in range(0, hidden, 512):
            up = dot_nn(low, w_up[:, c : c + 512]) + upbias[:, c : c + 512]
            gate = sigmoid(up)
            active = up * gate
            up_ref[:, c : c + 512] = gate + active * (1.0 - gate)
            active = active.astype(LOW)
            active_ref[rows, c : c + 512] = active
            z = z + dot_nn(active, w_down[c : c + 512, :])
        final, normed_final, inverse_final = norm_forward(z, gains[2:3, :], biases[9:10, :])
        decoded_out[rows, :] = final.astype(LOW)
        grad = cot[rows, :].astype(F32)
        ffn = norm_backward(grad, normed_final, inverse_final, gains[2:3, :])
        ffn_low = ffn.astype(LOW)
        ffn_ref[rows, :] = ffn_low
        mid_grad = ffn
        for c in range(0, hidden, 512):
            up_grad = dot_nt(ffn_low, w_down[c : c + 512, :]) * up_ref[:, c : c + 512]
            sums_out[8 + c // 512 : 9 + c // 512, :] += col_sum(up_grad)
            up_low = up_grad.astype(LOW)
            up_low_ref[rows, c : c + 512] = up_low
            mid_grad = mid_grad + dot_nt(up_low, w_up[:, c : c + 512])
        branch = norm_backward(mid_grad, normed, inverse, gains[1:2, :])
        branch_low = branch.astype(LOW)
        branch_out[rows, :] = branch
        branch_ref[rows, :] = branch_low
        att_grad_out[rows, :] = dot_nt(branch_low, w_out[...]).astype(LOW)
        sums_out[0:1, :] += col_sum(mid_grad * normed)
        sums_out[1:2, :] += col_sum(grad * normed_final)
        sums_out[2:3, :] += col_sum(branch)
        sums_out[3:4, :] += col_sum(mid_grad)
        sums_out[4:5, :] += col_sum(ffn)
        sums_out[5:6, :] += col_sum(grad)
        return carry

    lax.fori_loop(0, count // size, dense, 0)
    for out in (outs[0], outs[3], outs[4], outs[6]):
        out.flush()
    feed_forward_grads(
        mid_ref, up_low_ref, ffn_ref, active_ref, hid_ref, branch_ref, sums_out, blocks
    )


def cross_back_kernel(numbers, ins, outs, temps, total):
    idx, src_lens, tgt_lens = numbers
    query, keyval, att, att_grad, lse, src_vec, tgt_vec = [i.get() for i in ins[:7]]
    mem_own_out, mem_out, query_out, keyval_low, sums_out = [o.ref for o in outs]
    (keyval_ref,) = temps
    count = query.shape[0]
    start = idx[0] * count
    src_ends_row, _ = pair_ends(src_vec[...].astype(F32))
    _, tgt_ends_col = pair_ends(tgt_vec[...].astype(F32))
    keyval_ref[...] = jnp.zeros(keyval_ref.shape, F32)
    query_out[...] = jnp.zeros(query_out.shape, F32)
    sums_out[...] = jnp.zeros(sums_out.shape, F32)
    select = jnp.where(
        lax.broadcasted_iota(jnp.int32, (HEADS, 512), 1) // HEAD_DIM
        == lax.broadcasted_iota(jnp.int32, (HEADS, 512), 0),
        1.0,
        0.0,
    )

    def body(j, carry):
        at = pl.multiple_of(j * BLOCK, BLOCK)
        rows = pl.ds(at, BLOCK)
        first = start + at
        low, windows = cross_span(src_lens, tgt_lens, first)
        weighed = att[rows, :] * att_grad[rows, :].astype(F32)
        deltas = lax.dot_general(
            select, weighed, (((1,), (1,)), ((), ())),
            precision=lax.Precision.HIGHEST, preferred_element_type=F32,
        )

        def window(n, carry):
            begin = pl.multiple_of(low + n * WINDOW, 16)
            keys = pl.ds(begin, WINDOW)
            bias = cross_rule(src_ends_row, tgt_ends_col, first, begin, total)
            for group in range(2):
                lo, hi = group * GROUP, (group + 1) * GROUP
                query_grad, key_grad, value_grad = attend_back_block(
                    query[rows, lo:hi],
                    att_grad[rows, lo:hi],
                    keyval[keys, lo:hi],
                    keyval[keys, 512 + lo : 512 + hi],
                    bias,
                    lse[j, group : group + 1, :],
                    [deltas[group * 4 + h : group * 4 + h + 1, :] for h in range(4)],
                )
                query_out[rows, lo:hi] += query_grad.T
                keyval_ref[keys, lo:hi] += key_grad
                keyval_ref[keys, 512 + lo : 512 + hi] += value_grad
            return carry

        lax.fori_loop(0, windows, window, 0)
        return carry

    lax.fori_loop(0, count // BLOCK, body, 0)
    size = min(256, total)
    shards = mem_out.shape[0] + 1
    length = total // shards

    def to_memory(step, carry):
        rows = pl.ds(pl.multiple_of(step * size, size), size)
        grads = keyval_ref[rows, :]
        sums_out[0:1, :] += col_sum(grads[:, 512:])
        keyval_low[rows, :] = grads.astype(LOW)
        return carry

    lax.fori_loop(0, total // size, to_memory, 0)
    w_keyval = ins[7].get()
    for s in reversed(range(shards)):
        base = pl.multiple_of(lax.rem(idx[0] + s, shards) * length, BLOCK)
        grads = dot_nt(keyval_low[pl.ds(base, length), :], w_keyval[...])
        if s == 0:
            mem_own_out[...] = grads
        else:
            mem_out[s - 1] = grads.astype(LOW)


def dec_self_back_kernel(numbers, ins, outs, temps, total):
    query_grads, keyval_low, memory, normed_in, inv_in, branch_in, hid_in, gains, biases, w_query, w_out = [
        i.get() for i in ins[:11]
    ]
    branch_out, sums_out = [o.ref for o in outs[:2]]
    branch_ref, query_low, mid_ref, att_grad_out = temps[:4]
    count = query_grads.shape[0]
    sums_out[...] = jnp.zeros(sums_out.shape, F32)
    size = min(256, count)

    def dense(step, carry):
        rows = pl.ds(pl.multiple_of(step * size, size), size)
        query_grad = query_grads[rows, :]
        low = query_grad.astype(LOW)
        query_low[rows, :] = low
        normed = normed_in[rows, :]
        mid_ref[rows, :] = (normed * gains[0:1, :] + biases[3:4, :]).astype(LOW)
        mid_grad = branch_in[rows, :] + dot_nt(low, w_query[...])
        branch = norm_backward(mid_grad, normed, inv_in[rows, :], gains[0:1, :])
        branch_low = branch.astype(LOW)
        branch_out[rows, :] = branch
        branch_ref[rows, :] = branch_low
        att_grad_out[rows, :] = dot_nt(branch_low, w_out[...]).astype(LOW)
        sums_out[0:1, :] += col_sum(mid_grad * normed)
        sums_out[1:2, :] += col_sum(branch)
        sums_out[2:3, :] += col_sum(mid_grad)
        sums_out[3:4, :] += col_sum(query_grad)
        return carry

    lax.fori_loop(0, count // size, dense, 0)
    outs[0].flush()
    held = outs[2].ref
    for c in range(0, 1024, 512):
        put_rows(held, dot_tn(memory[...], keyval_low[:, c : c + 512]), c)
    put_rows(held, dot_tn(mid_ref[...], query_low[...]), 1024)
    put_rows(held, dot_tn(hid_in[...], branch_ref[...]), 1536)
    outs[2].flush()
    self_back(numbers, Loaded(att_grad_out), *ins[11:], outs[3:], *temps[4:], total, True)


def enc_self_back_kernel(numbers, ins, outs, temps, total):
    self_back(numbers, *ins, outs, *temps, total, False)


def self_back(numbers, att_grad, lse, lens, rows_in, outs, query_ref, keyval_ref, total, causal):
    own_out, halos = outs[0].ref, [o.ref for o in outs[1:]]
    rows_in, att_grad, lse = rows_in.get(), att_grad.get(), lse.get()
    count = att_grad.shape[0]
    ends = pair_ends(lens.get()[...].astype(F32))
    width = (2 if causal else 3) * BLOCK
    attend_local_back(
        rows_in, att_grad, lse, count // BLOCK, width, query_ref, keyval_ref,
        self_rule(ends, numbers[0][0] * count, total, width, causal),
    )
    if causal:
        halos[0][...] = keyval_ref[:BLOCK, :].astype(LOW)
    elif len(halos) == 1:
        edge = pl.multiple_of((1 - numbers[0][0]) * (BLOCK + count), BLOCK)
        halos[0][...] = keyval_ref[pl.ds(edge, BLOCK), :].astype(LOW)
    else:
        halos[0][...] = keyval_ref[:BLOCK, :].astype(LOW)
        halos[1][...] = keyval_ref[BLOCK + count :, :].astype(LOW)
    for out in outs[1:]:
        out.flush()
    own_out[:, :512] = query_ref[...]
    own_out[:, 512:] = keyval_ref[BLOCK : BLOCK + count, :]


def input_grad(own, edges, low_in, branch, w, grad_out, sums_out, low_ref, put, count):
    sums_out[...] = jnp.zeros(sums_out.shape, F32)
    size = min(256, count)

    def dense(step, carry):
        rows = pl.ds(pl.multiple_of(step * size, size), size)
        grads = own[rows, :]
        sums_out[0:1, :] += col_sum(grads[:, :512])
        sums_out[1:2, :] += col_sum(grads[:, 1024:])
        low_ref[rows, :] = grads.astype(LOW)
        return carry

    lax.fori_loop(0, count // size, dense, 0)
    returned = jnp.zeros((count, 1024), F32) if len(edges) > 1 and count == BLOCK else None
    for at, halo in edges:
        edge = pl.ds(at, BLOCK)
        grads = halo[...].astype(F32)
        sums_out[1:2, :] += col_sum(grads[:, 512:])
        if returned is not None:
            returned = grads = returned + grads
        low_ref[edge, 512:] = (own[edge, 512:] + grads).astype(LOW)
    for c in range(0, 1536, 512):
        put(dot_tn(low_in[...], low_ref[:, c : c + 512]), c)

    def back():
        def dense_grad(step, carry):
            rows = pl.ds(pl.multiple_of(step * size, size), size)
            grad_out[rows, :] = (branch[rows, :] + dot_nt(low_ref[rows, :], w[...])).astype(grad_out.dtype)
            return carry

        lax.fori_loop(0, count // size, dense_grad, 0)

    return back


def dec_input_grad_kernel(numbers, ins, outs, temps, blocks):
    blocks.fill(ins[-1], 1536)
    halo, own, branch, low_in, w = [i.get() for i in ins[:-1]]
    grad_out, sums_out = [o.ref for o in outs]
    (low_ref,) = temps
    count = own.shape[0]
    back = input_grad(
        own, [(count - BLOCK, halo)], low_in, branch, w, grad_out, sums_out, low_ref, blocks.put_rows, count
    )
    blocks.filled()
    blocks.spread(0, blocks.held.shape[2])
    back()


def enc_input_grad_kernel(numbers, ins, outs, temps, blocks, halo_count):
    halos = [i.get() for i in ins[:halo_count]]
    own, branch, low_in, w, *sums = [i.get() for i in ins[halo_count:]]
    (grad_out,) = [o.ref for o in outs]
    low_ref, sums_ref, small_ref = temps
    count = own.shape[0]
    if halo_count == 1:
        edges = [(pl.multiple_of((1 - numbers[0][0]) * (count - BLOCK), BLOCK), halos[0])]
    else:
        edges = [(0, halos[0]), (count - BLOCK, halos[1])]
    back = input_grad(own, edges, low_in, branch, w, grad_out, sums_ref, low_ref, blocks.put_rows, count)
    small_ref[...] = jnp.zeros(small_ref.shape, F32)
    for n, part in enumerate((*sums, sums_ref)):
        small_ref[n * 8 : (n + 1) * 8, :] = part[:8, :]
    blocks.put_rows(small_ref[...].T, 1536)
    blocks.spread(0, 1536 + BLOCK)
    back()


def enc_tail_back_kernel(numbers, ins, outs, temps, blocks):
    (mem_own, mem_others, cot, fin_in, fin_inv, mid_in, mid_inv, hid_in, gains, biases, upbias, w_down, w_up,
     w_out) = [i.get() for i in ins]
    branch_out, att_grad_out, sums_out = [o.ref for o in outs]
    branch_ref, mid_ref, active_ref, ffn_ref, up_low_ref = temps
    count = cot.shape[0]
    hidden = w_up.shape[1]
    sums_out[...] = jnp.zeros(sums_out.shape, F32)
    size = min(256, count)

    def dense(step, carry):
        rows = pl.ds(pl.multiple_of(step * size, size), size)
        grad = cot[rows, :].astype(F32) + mem_own[rows, :]
        for s in range(mem_others.shape[0]):
            grad = grad + mem_others[s, rows, :].astype(F32)
        normed_final = fin_in[rows, :]
        ffn = norm_backward(grad, normed_final, fin_inv[rows, :], gains[1:2, :])
        ffn_low = ffn.astype(LOW)
        ffn_ref[rows, :] = ffn_low
        normed = mid_in[rows, :]
        low = (normed * gains[0:1, :] + biases[3:4, :]).astype(LOW)
        mid_ref[rows, :] = low
        mid_grad = ffn
        for c in range(0, hidden, 512):
            up = dot_nn(low, w_up[:, c : c + 512]) + upbias[:, c : c + 512]
            gate = sigmoid(up)
            active = up * gate
            active_ref[rows, c : c + 512] = active.astype(LOW)
            up_grad = dot_nt(ffn_low, w_down[c : c + 512, :]) * (gate + active * (1.0 - gate))
            sums_out[8 + c // 512 : 9 + c // 512, :] += col_sum(up_grad)
            up_low = up_grad.astype(LOW)
            up_low_ref[rows, c : c + 512] = up_low
            mid_grad = mid_grad + dot_nt(up_low, w_up[:, c : c + 512])
        branch = norm_backward(mid_grad, normed, mid_inv[rows, :], gains[0:1, :])
        branch_low = branch.astype(LOW)
        branch_out[rows, :] = branch
        branch_ref[rows, :] = branch_low
        att_grad_out[rows, :] = dot_nt(branch_low, w_out[...]).astype(LOW)
        sums_out[0:1, :] += col_sum(mid_grad * normed)
        sums_out[1:2, :] += col_sum(grad * normed_final)
        sums_out[2:3, :] += col_sum(branch)
        sums_out[3:4, :] += col_sum(mid_grad)
        sums_out[4:5, :] += col_sum(ffn)
        sums_out[5:6, :] += col_sum(grad)
        return carry

    lax.fori_loop(0, count // size, dense, 0)
    outs[0].flush()
    feed_forward_grads(
        mid_ref, up_low_ref, ffn_ref, active_ref, hid_in, branch_ref, sums_out, blocks
    )


def log2(number):
    bits = number.bit_length() - 1
    assert number == 1 << bits
    return bits


def swapped(value, axis, bit, devices):
    return lax.ppermute(value, axis, [(i, i ^ (1 << bit)) for i in range(devices)])


class Chain:
    def __init__(self, token):
        self.token = token

    def tie(self, *values):
        self.token, *values = lax.optimization_barrier((self.token, *values))
        return values[0] if len(values) == 1 else values


class Reduction:
    def __init__(self, chain, arrays, order, devices, seq_count):
        self.chain, self.order, self.devices, self.seq_count = (chain, order, devices, seq_count)
        self.keep, send = arrays
        self.size = self.keep.shape[0]
        self.received, self.low, self.others = [], None, []
        self.push(send)

    def push(self, send):
        bit = self.order[len(self.received)]
        if bit == OVER_SEQ:
            self.received.append(swapped(send, "seq", 0, self.seq_count))
        else:
            self.received.append(swapped(send, "dp", bit, self.devices))

    def part(self, first, last):
        total = self.keep[first:last].astype(F32)
        for piece in self.received:
            total = total + piece[first:last].astype(F32)
        return total

    def next(self):
        self.received[-1] = self.chain.tie(self.received[-1])
        if len(self.received) < len(self.order):
            half = self.size // 2
            self.push(self.chain.tie(self.part(half, self.size).astype(LOW)))
            self.size = half
            return
        self.low = self.chain.tie(self.part(0, 1)[0].astype(LOW))
        if log2(self.seq_count):
            self.others.append(swapped(self.low, "seq", 0, self.seq_count))

    def pair(self):
        while self.low is None:
            self.next()
        low, other = self.low, self.others[0]
        if OVER_SEQ not in self.order:
            for bit in range(1, log2(self.seq_count)):
                low = lax.optimization_barrier((low.astype(F32) + other.astype(F32)).astype(LOW))
                other = swapped(low, "seq", bit, self.seq_count)
        return (low, other)


def from_shards(own, count):
    return jnp.stack(
        [lax.ppermute(own, "seq", [((i + s) % count, i) for i in range(count)]) for s in range(1, count)]
    )


def feed_forward_unpack(numbers, ins, outs, temps):
    low, other = [i.get() for i in ins]
    up_out, matrix_out, down_out, bias_out = [o.ref for o in outs]
    (total,) = temps
    total[...] = low[...].astype(F32) + other[...].astype(F32)
    share = up_out.shape[0]
    width = down_out.shape[0]
    pieces = BLOCK // width
    groups = FEATURES // pieces // share
    tall = jnp.concatenate([total[:, g * BLOCK : (g + 1) * BLOCK] for g in range(groups)], axis=0).T
    for p in range(pieces):
        rows = FEATURES // pieces
        down_out[:, p * rows : (p + 1) * rows] = tall[p * width : (p + 1) * width, :]
    end = groups * BLOCK
    bias_out[...] = total[0:1, end : end + width]
    up_out[...] = total[:, HIDDEN + BLOCK : 2 * HIDDEN + BLOCK]
    matrix_out[...] = total[:, 2 * HIDDEN + BLOCK :]


def decoder_unpack(numbers, ins, outs, temps, halved):
    low, other = [i.get() for i in ins]
    (total,) = temps
    if halved:
        width = low.shape[1]
        seq = numbers[0][0]
        total[:, pl.ds(pl.multiple_of(seq * width, BLOCK), width)] = low[...].astype(F32)
        total[:, pl.ds(pl.multiple_of((1 - seq) * width, BLOCK), width)] = other[...].astype(F32)
    else:
        total[...] = low[...].astype(F32) + other[...].astype(F32)
    at = 0
    for out in outs:
        width = out.ref.shape[1]
        out.ref[...] = total[:, at : at + width]
        at += width


def encoder_unpack(numbers, ins, outs, temps, picks):
    low, other = [i.get() for i in ins]
    total = low[...].astype(F32) + other[...].astype(F32)
    outs[0].ref[...] = total[:, :1536]
    small = total[:, 1536:].T
    for out, rows in zip(outs[1:], picks):
        for n, row in enumerate(rows):
            out.ref[n : n + 1, :] = small[row : row + 1, :]


def last_unpack(numbers, ins, outs, temps, picks, halved):
    feed_forward_unpack(numbers, ins[:2], outs[:4], temps[:1])
    for out in outs[:4]:
        out.flush()
    encoder_unpack(numbers, ins[2:4], outs[4:9], (), picks)
    for out in outs[4:9]:
        out.flush()
    decoder_unpack(numbers, ins[4:], outs[9:], temps[1:], halved)


def rows_unpack(numbers, ins, outs, temps):
    shards = numbers[0]
    for n, out in enumerate(outs):
        own, others = ins[2 * n].get(), ins[2 * n + 1].get()
        count = own.shape[0]
        parts = others.shape[0] + 1
        for s in range(parts):
            at = pl.ds(pl.multiple_of(lax.rem(shards[0] + s, parts) * count, BLOCK), count)
            out.ref[at, :] = (own[...] if s == 0 else others[s - 1]).astype(out.ref.dtype)
        out.flush()


def local(
    src_embed, tgt_embed, src_lengths, tgt_lengths, enc_cotangent, dec_cotangent,
    enc_inproj, enc_outproj, enc_upproj, enc_downproj, enc_gains, enc_biases, enc_upbias,
    dec_inproj, dec_outproj, cross_query, cross_keyval, cross_outproj, dec_upproj, dec_downproj,
    dec_gains, dec_biases, dec_upbias,
):
    _, count, features = src_embed.shape
    total = tgt_embed.shape[1]
    hidden = enc_upproj.shape[1]
    devices = lax.axis_size("dp")
    seq_count = lax.axis_size("seq")
    pair = seq_count == 2
    blocks = count // BLOCK
    bits = log2(devices)
    x_first = tuple(range(bits))
    y_first = (0, OVER_SEQ, *range(1, bits)) if seq_count == 2 else x_first
    seq_index = lax.axis_index("seq")
    dp_index = lax.axis_index("dp")
    idx = jnp.where(jnp.arange(2) == 0, seq_index, dp_index).astype(jnp.int32)
    chain = Chain(idx)
    table = jnp.asarray(place_table(features))
    src_own, tgt_all = src_embed[0], tgt_embed[0]
    enc_ub, dec_ub = enc_upbias[None], dec_upbias[None]
    up = [(i, i + 1) for i in range(seq_count - 1)]
    down = [(i + 1, i) for i in range(seq_count - 1)]
    swap = [(0, 1), (1, 0)]
    wide = (count, features)
    near = lambda *arrays: [(a, NEAR) for a in arrays]
    far = lambda *arrays: [(a, FAR) for a in arrays]
    part = functools.partial
    lse = ((blocks, 2, 512), F32)
    inv = ((count, 1), F32)
    begin = lambda numbers: pl.multiple_of(numbers[0] * count, BLOCK)
    before = lambda numbers: pl.multiple_of(jnp.maximum(numbers[0] * count - BLOCK, 0), BLOCK)

    if pair:
        edge = lax.dynamic_slice_in_dim(src_own, (1 - seq_index) * (count - BLOCK), BLOCK, 0)
        left = right = lax.ppermute(chain.tie(edge), "seq", swap)
    else:
        left = lax.ppermute(src_own[count - BLOCK :], "seq", up)
        right = lax.ppermute(src_own[:BLOCK], "seq", down)
    (tgt_in, tgt_low, dec_rows), _, enc_near = call(
        dec_pre_kernel, "dec_pre", [chain.token],
        [(tgt_all, FAR, before, BLOCK), (tgt_all, FAR, begin, count), *far(tgt_lengths, table, dec_inproj, dec_biases)],
        [(wide, F32, FAR), (wide, LOW, FAR), ((count + BLOCK, 1536), LOW, FAR)],
        ahead=far(src_own, src_lengths, table, enc_inproj, enc_gains, enc_biases, enc_ub),
    )
    tgt_low = chain.tie(tgt_low)
    (enc_rows, src_low, enc_lse, enc_hid, mid_normed, mid_inv, fin_normed, fin_inv, encoded), _, self_near = call(
        part(enc_kernel, total=total), "enc_forward", [chain.token],
        [*far(left), *near(enc_near[0]), *far(right), *near(*enc_near[1:]),
         *far(enc_outproj, enc_upproj, enc_downproj)],
        [((count + 2 * BLOCK, 1536), LOW, FAR), (wide, LOW, FAR), (*lse, FAR),
         (wide, LOW, FAR), (wide, F32, FAR), (*inv, FAR),
         (wide, F32, FAR), (*inv, FAR), (wide, LOW, FAR)],
        [(wide, F32)],
        ahead=far(tgt_in, dec_rows, tgt_lengths, dec_gains, dec_biases, dec_outproj, cross_query),
    )
    encoded = chain.tie(encoded)
    others = from_shards(encoded, seq_count)
    (dec_lse, dec_hid, self_normed, self_inv, cross_q), _, tail_near = call(
        part(dec_self_kernel, total=total), "dec_self", [chain.token], near(*self_near),
        [(*lse, FAR), (wide, LOW, FAR), (wide, F32, FAR), (*inv, FAR), (wide, LOW, FAR)],
        ahead=[*far(encoded, src_lengths, tgt_lengths, dec_gains, dec_biases, dec_ub, cross_keyval),
               (dec_cotangent[0], FAR, begin, count), *far(cross_outproj, dec_upproj, dec_downproj)],
    )
    (cross_att, cross_lse, keyval, memory, decoded, cross_att_grad, cross_branch, tail_sums), tail, back_near = call(
        part(cross_tail_kernel, total=total), "cross_tail", [chain.token, src_lengths, tgt_lengths],
        [*far(cross_q), *near(tail_near[0]), *far(others), *near(*tail_near[1:7]), *far(self_normed), *near(*tail_near[7:])],
        [(wide, F32, FAR), (*lse, NEAR), ((total + WINDOW, 1024), LOW, NEAR), ((total, features), LOW, FAR),
         (wide, LOW, FAR), (wide, LOW, NEAR), (wide, F32, FAR), ((16, features), F32, FAR)],
        [(wide, LOW), (wide, LOW), (wide, LOW), ((min(256, count), hidden), F32), ((count, hidden), LOW),
         (wide, LOW), ((count, hidden), LOW),
         ((HEADS, BLOCK), F32), ((HEADS, BLOCK), F32), ((features, BLOCK), F32)],
        [2 * hidden + BLOCK + 512], x_first,
        ahead=far(src_lengths, tgt_lengths),
    )
    decoded = chain.tie(decoded)
    decoded_others = from_shards(decoded, seq_count)
    make = part(Reduction, devices=devices, seq_count=seq_count)
    tail = make(chain, tail, x_first)
    (mem_own, mem_send, query_grads, keyval_grads, mem_sums), _, dense_near = call(
        part(cross_back_kernel, total=total), "cross_back", [chain.token, src_lengths, tgt_lengths],
        [*far(cross_q), *near(keyval), *far(cross_att), *near(cross_att_grad, cross_lse, *back_near), *far(cross_keyval)],
        [(wide, F32, FAR), ((seq_count - 1, *wide), LOW, FAR), (wide, F32, NEAR),
         ((total, 1024), LOW, NEAR), ((8, features), F32, FAR)],
        [((total + WINDOW, 1024), F32)],
        ahead=[*far(memory, self_normed, self_inv, cross_branch),
               *far(dec_hid, dec_gains, dec_biases, cross_query, dec_outproj, dec_lse, tgt_lengths, dec_rows)],
    )
    mem_send = chain.tie(mem_send)
    mem_others = jnp.stack(
        [
            lax.ppermute(mem_send[s - 1], "seq", [(i, (i + s) % seq_count) for i in range(seq_count)])
            for s in range(1, seq_count)
        ]
    )
    decoded_others = chain.tie(decoded_others)
    tail.next()
    (self_branch, cross_sums, cross_held, self_own, self_halo), _, enc_near = call(
        part(dec_self_back_kernel, total=total), "dec_self_back", [chain.token],
        near(query_grads, keyval_grads, *dense_near),
        [(wide, F32, FAR), ((8, features), F32, FAR), ((devices, features // devices, 2048), LOW, FAR),
         ((count, 1536), F32, FAR), ((BLOCK, 1024), LOW, FAR)],
        [(wide, LOW), (wide, LOW), (wide, LOW), (wide, LOW), (wide, F32), ((count + BLOCK, 1024), F32)],
        ahead=far(enc_cotangent[0], fin_normed, fin_inv, mid_normed, mid_inv, enc_hid, enc_gains, enc_biases,
                  enc_ub, enc_downproj, enc_upproj, enc_outproj),
    )
    self_halo = chain.tie(self_halo)
    self_returned = lax.ppermute(self_halo, "seq", down)
    mem_others = chain.tie(mem_others)
    (enc_branch, enc_att_grad, enc_sums), enc, self_near = call(
        enc_tail_back_kernel, "enc_tail_back", [chain.token],
        [*far(mem_own, mem_others), *near(*enc_near)],
        [(wide, F32, FAR), (wide, LOW, FAR), ((16, features), F32, FAR)],
        [(wide, LOW), (wide, LOW), ((count, hidden), LOW), (wide, LOW), ((count, hidden), LOW)],
        [2 * hidden + BLOCK + 512], x_first,
        ahead=far(self_own, self_branch, tgt_low, dec_inproj),
    )
    enc_sums = chain.tie(enc_sums)
    enc = make(chain, enc, x_first)
    self_returned = chain.tie(self_returned)
    (tgt_part, self_sums), cross, back_near = call(
        dec_input_grad_kernel, "dec_input_grad", [chain.token],
        [*far(self_returned), *near(*self_near), (cross_held, RAW)],
        [(wide, LOW, FAR), ((8, features), F32, FAR)],
        [((count, 1536), LOW)],
        [1536 + 2048], y_first,
        ahead=far(enc_att_grad, enc_lse, src_lengths, enc_rows),
    )
    tgt_part = chain.tie(tgt_part)
    cross = make(chain, cross, y_first)
    tgt_others = from_shards(tgt_part, seq_count)
    tail.next()
    enc.next()
    (enc_own, *halos), _, in_near = call(
        part(enc_self_back_kernel, total=total), "enc_self_back", [chain.token], near(*back_near),
        [((count, 1536), F32, NEAR)] + [((BLOCK, 1024), LOW, FAR)] * (1 if pair else 2),
        [(wide, F32), ((count + 2 * BLOCK, 1024), F32)],
        ahead=far(enc_branch, src_low, enc_inproj),
    )
    halos = [chain.tie(h) for h in halos]
    if pair:
        halos = [lax.ppermute(halos[0], "seq", swap)]
    else:
        halos = [lax.ppermute(halos[1], "seq", up), lax.ppermute(halos[0], "seq", down)]
    cross.next()
    tail.next()
    tgt_others = chain.tie(tgt_others)
    halos = [chain.tie(h) for h in halos]
    (src_grad,), ins, _ = call(
        part(enc_input_grad_kernel, halo_count=len(halos)), "enc_input_grad", [chain.token],
        [*far(*halos), *near(enc_own, *in_near), *far(tail_sums, mem_sums, cross_sums, self_sums, enc_sums)],
        [(wide, F32, FAR)],
        [((count, 1536), LOW), ((8, features), F32), ((BLOCK, features), F32)],
        [1536 + BLOCK], x_first,
    )
    src_grad = chain.tie(src_grad)
    ins = make(chain, ins, x_first)
    share = features // devices
    slim = lambda *widths: [((share, w), F32, FAR) for w in widths]
    matrices = [*slim(hidden, 512), ((hidden // devices, 512), F32, FAR), ((1, hidden // devices), F32, FAR)]
    all_rows = (total, features)
    packed = ((share, 2 * hidden + BLOCK + 512), F32)
    enc.next()
    ins.next()
    tail.next()
    cross.next()
    (decoded_all, tgt_all_grad), _, _ = call(
        rows_unpack, "rows_unpack", [chain.token], [*far(decoded), *near(decoded_others), *far(tgt_part), *near(tgt_others)],
        [(all_rows, LOW, FAR), (all_rows, F32, FAR)],
    )
    tgt_all_grad = chain.tie(tgt_all_grad)
    ins.next()
    (dec_up, cross_out, dec_down, dec_ub_grad), _, _ = call(
        feed_forward_unpack, "tail_unpack", [chain.token], near(*tail.pair()), matrices, [packed]
    )
    dec_up = chain.tie(dec_up)
    enc.next()
    cross.next()
    ins.next()
    enc.next()
    cross.next()
    ins.next()
    cross.next()
    t, m, c, d, e, i = range(0, 48, 8)
    picks = [
        (e, e + 1),
        (i, i + 1, e + 2, e + 3, e + 4, e + 5),
        (c, t, t + 1),
        (d, d + 1, c + 1, c + 2, c + 3, m, t + 2, t + 3, t + 4, t + 5),
    ]
    (enc_up, enc_out, enc_down, enc_ub_grad, enc_in, enc_gains_grad, enc_biases_grad, dec_gains_grad, dec_biases_grad,
     dec_in, keyval_grad, query_grad, dec_out), _, _ = call(
        part(last_unpack, picks=picks, halved=OVER_SEQ in y_first), "last_unpack", [chain.token],
        near(*enc.pair(), *ins.pair(), *cross.pair()),
        [*matrices, *slim(1536), *[((len(p), share), F32, FAR) for p in picks], *slim(1536, 1024, 512, 512)],
        [packed, ((share, 3584), F32)],
    )
    return (
        encoded[None],
        decoded_all[None],
        src_grad[None],
        tgt_all_grad[None],
        enc_in,
        enc_out,
        enc_up,
        enc_down,
        enc_gains_grad,
        enc_biases_grad,
        enc_ub_grad[0],
        dec_in,
        dec_out,
        query_grad,
        keyval_grad,
        cross_out,
        dec_up,
        dec_down,
        dec_gains_grad,
        dec_biases_grad,
        dec_ub_grad[0],
    )


def solution(mesh):
    rows, whole = P("dp", "seq", None), P("dp", None, None)
    return jax.shard_map(
        local,
        mesh=mesh,
        in_specs=(rows, whole, P("dp", None), P("dp", None), rows, whole, *([P()] * 17)),
        out_specs=(
            rows, whole, rows, whole,
            *([P("dp", None)] * 4), P(None, "dp"), P(None, "dp"), P("dp"),
            *([P("dp", None)] * 7), P(None, "dp"), P(None, "dp"), P("dp"),
        ),
        check_vma=False,
    )
```

```python
import functools
import math

import jax
import jax.numpy as jnp
import numpy as np
from jax import lax
from jax.experimental import pallas as pl
from jax.experimental.pallas import tpu as pltpu
from jax.sharding import PartitionSpec as P

HEADS = 8
HEAD_DIM = 64
MAXPAIR = 128
BLOCK = 128
GROUP = 256
WINDOW = 256
LOW = jnp.bfloat16
F32 = jnp.float32
MASKED = -1e30
FEATURES = 512
HIDDEN = 2048


def place_table(features):
    half = features // 2
    frequency = np.exp(-math.log(10000.0) * np.arange(half, dtype=np.float32) / np.float32(half)).astype(np.float32)
    angles = (np.arange(MAXPAIR, dtype=np.float32)[:, None] * frequency[None, :]).astype(np.float32)
    table = np.concatenate([np.sin(angles), np.cos(angles)], axis=-1).astype(np.float32)
    pieces, rest = [], table
    for _ in range(3):
        piece = rest.astype(jnp.bfloat16)
        pieces.append(piece)
        rest = rest - piece.astype(np.float32)
    return np.stack(pieces)


def dot_nn(left, right):
    return lax.dot_general(left, right, (((1,), (0,)), ((), ())), preferred_element_type=F32)


def dot_nt(left, right):
    return lax.dot_general(left, right, (((1,), (1,)), ((), ())), preferred_element_type=F32)


def dot_tn(left, right):
    return lax.dot_general(left, right, (((0,), (0,)), ((), ())), preferred_element_type=F32)


def iota(shape, dim):
    return lax.broadcasted_iota(jnp.int32, shape, dim).astype(F32)


def pair_ends(len_row):
    count = len_row.shape[1]
    lengths = jnp.broadcast_to(len_row, (count, count))
    down, across = iota((count, count), 0), iota((count, count), 1)
    ends_col = jnp.sum(jnp.where(across <= down, lengths, 0.0), axis=1, keepdims=True)
    len_col = jnp.sum(jnp.where(across == down, lengths, 0.0), axis=1, keepdims=True)
    ends_row = jnp.sum(jnp.where(down <= across, len_col, 0.0), axis=0, keepdims=True)
    return (ends_row, ends_col)


def pair_col(ends_row, places, total):
    number = jnp.sum(jnp.where(ends_row <= places, 1.0, 0.0), axis=1, keepdims=True)
    return jnp.where((places >= 0.0) & (places < total), number, -1.0)


def pair_row(ends_col, places):
    return jnp.sum(jnp.where(ends_col <= places, 1.0, 0.0), axis=0, keepdims=True)


def with_places(embed, places, ends_row, len_row, table_ref):
    started = jnp.sum(jnp.where(ends_row <= places, len_row, 0.0), axis=1, keepdims=True)
    inside = places - started
    hot = jnp.where(iota((embed.shape[0], MAXPAIR), 1) == inside, 1.0, 0.0).astype(LOW)
    sines = dot_nn(hot, table_ref[0]) + dot_nn(hot, table_ref[1]) + dot_nn(hot, table_ref[2])
    return embed.astype(F32) + sines


def norm_forward(values, gain_row, shift_row):
    centred = values - jnp.mean(values, axis=-1, keepdims=True)
    inverse = lax.rsqrt(jnp.mean(centred * centred, axis=-1, keepdims=True) + 1e-05)
    normed = centred * inverse
    return (normed * gain_row + shift_row, normed, inverse)


def norm_backward(grad_rows, normed, inverse, gain_row):
    scaled = grad_rows * gain_row
    return inverse * (
        scaled
        - jnp.mean(scaled, axis=-1, keepdims=True)
        - normed * jnp.mean(scaled * normed, axis=-1, keepdims=True)
    )


def sigmoid(values):
    return 0.5 * jnp.tanh(0.5 * values) + 0.5


def col_sum(values):
    return jnp.sum(values, axis=0, keepdims=True)


def head_masks(scale):
    lane = lax.broadcasted_iota(jnp.int32, (1, GROUP), 1) // HEAD_DIM
    return [jnp.where(lane == h, scale, 0.0).astype(LOW) for h in range(GROUP // HEAD_DIM)]


def spread(rows, masks):
    return jnp.concatenate([rows * mask for mask in masks], axis=0)


def diagonal(wide):
    count = GROUP // HEAD_DIM
    return [
        wide[h * HEAD_DIM : (h + 1) * HEAD_DIM, h * BLOCK : (h + 1) * BLOCK] for h in range(count)
    ]


def attend_block(query, keys, values, bias, group):
    lanes = slice(group * GROUP, (group + 1) * GROUP)
    stacked = spread(query(lanes), head_masks(HEAD_DIM**-0.5))
    scores = dot_nt(keys(lanes), stacked)
    probs, maxima, sums = [], [], []
    for h in range(GROUP // HEAD_DIM):
        score = scores[:, h * BLOCK : (h + 1) * BLOCK] + bias
        row_max = jnp.max(score, axis=0, keepdims=True)
        exp_score = jnp.exp(score - row_max)
        maxima.append(row_max)
        sums.append(col_sum(exp_score))
        probs.append(exp_score.astype(LOW))
    wide = dot_tn(values(lanes), jnp.concatenate(probs, axis=1))
    return (diagonal(wide), maxima, sums)


def attend_local(rows_ref, count, width, att_ref, lse_ref, rule):
    def body(j, carry):
        first = pl.multiple_of(j * BLOCK, BLOCK)
        queries = pl.ds(pl.multiple_of(first + BLOCK, BLOCK), BLOCK)
        keys = pl.ds(first, width)
        bias = rule(first)
        for group in range(2):
            def part(rows, offset):
                return lambda lanes: rows_ref[rows, offset + lanes.start : offset + lanes.stop]

            outs, maxima, sums = attend_block(
                part(queries, 0), part(keys, 512), part(keys, 1024), bias, group
            )
            mixed = jnp.concatenate([o * (1.0 / s) for o, s in zip(outs, sums)], axis=0)
            att_ref[pl.ds(first, BLOCK), group * GROUP : (group + 1) * GROUP] = mixed.T.astype(
                att_ref.dtype
            )
            lse_ref[j, group : group + 1, :] = jnp.concatenate(
                [m + jnp.log(s) for m, s in zip(maxima, sums)], axis=1
            )
        return carry

    lax.fori_loop(0, count, body, 0)


def attend_back_block(query, grad, keys, values, bias, lse, deltas):
    stacked = spread(query, head_masks(HEAD_DIM**-0.5))
    grads = spread(grad, head_masks(1.0))
    scores = dot_nt(keys, stacked)
    prob_grads = dot_nt(values, grads)
    probs, score_grads = [], []
    for h in range(GROUP // HEAD_DIM):
        cols = slice(h * BLOCK, (h + 1) * BLOCK)
        prob = jnp.exp(scores[:, cols] + bias - lse[:, cols])
        prob_grad = prob_grads[:, cols]
        delta = col_sum(prob * prob_grad) if deltas is None else deltas[h]
        score_grads.append((prob * (prob_grad - delta)).astype(LOW))
        probs.append(prob.astype(LOW))
    prob_wide = jnp.concatenate(probs, axis=1)
    grad_wide = jnp.concatenate(score_grads, axis=1)
    value_grad = dot_nn(prob_wide, grads)
    key_grad = dot_nn(grad_wide, stacked)
    query_grad = jnp.concatenate(diagonal(dot_tn(keys, grad_wide)), axis=0) * HEAD_DIM**-0.5
    return (query_grad, key_grad, value_grad)


def attend_local_back(rows_ref, grad_ref, lse_ref, count, width, query_ref, keyval_ref, rule):
    keyval_ref[...] = jnp.zeros(keyval_ref.shape, F32)

    def body(j, carry):
        first = pl.multiple_of(j * BLOCK, BLOCK)
        queries = pl.ds(pl.multiple_of(first + BLOCK, BLOCK), BLOCK)
        own = pl.ds(first, BLOCK)
        keys = pl.ds(first, width)
        bias = rule(first)
        for group in range(2):
            low, high = group * GROUP, (group + 1) * GROUP
            query_grad, key_grad, value_grad = attend_back_block(
                rows_ref[queries, low:high],
                grad_ref[own, low:high],
                rows_ref[keys, 512 + low : 512 + high],
                rows_ref[keys, 1024 + low : 1024 + high],
                bias,
                lse_ref[j, group : group + 1, :],
                None,
            )
            query_ref[own, low:high] = query_grad.T
            keyval_ref[keys, low:high] += key_grad
            keyval_ref[keys, 512 + low : 512 + high] += value_grad
        return carry

    lax.fori_loop(0, count, body, 0)


def self_rule(ends, start, total, width, causal):
    ends_row, ends_col = ends

    def rule(first):
        shift = (start + first).astype(F32)
        key_places = iota((width, 1), 0) + (shift - BLOCK)
        query_places = iota((1, BLOCK), 1) + shift
        allowed = pair_col(ends_row, key_places, total) == pair_row(ends_col, query_places)
        if causal:
            allowed = allowed & (key_places <= query_places)
        return jnp.where(allowed, 0.0, MASKED)

    return rule


class Loaded:
    def __init__(self, ref):
        self.ref = ref

    def get(self):
        return self.ref


class Coming:
    def __init__(self, far, near, sem):
        self.near = near
        self.copy = pltpu.make_async_copy(far, near, sem)
        self.copy.start()
        self.waiting = True

    def get(self):
        if self.waiting:
            self.copy.wait()
            self.waiting = False
        return self.near


class Leaving:
    def __init__(self, near, far, sem):
        self.ref = near
        self.copy = pltpu.make_async_copy(near, far, sem)
        self.started = False

    def flush(self):
        if not self.started:
            self.copy.start()
            self.started = True

    def finish(self):
        self.flush()
        self.copy.wait()


OVER_SEQ = "seq"


def put_rows(held, result, col):
    devices, rows, _ = held.shape
    cols = pl.ds(col if isinstance(col, int) else pl.multiple_of(col, BLOCK), result.shape[1])
    low = result.astype(LOW)
    for i in range(devices):
        held[i, :, cols] = low[i * rows : (i + 1) * rows, :]


class Blocks:
    def __init__(self, keep, send, held, sems, numbers, order):
        self.keep, self.send, self.held, self.sems = (keep, send, held, sems)
        self.numbers, self.order = (numbers, order)
        self.used = []

    def spread(self, col, width):
        half, bits = (self.keep.shape[0], len(self.order))
        chunk = len(self.used)
        seq, mine = self.numbers[0], self.numbers[1]
        for place in range(2 * half):
            flips = {bit: (place >> (bits - 1 - s)) & 1 for s, bit in enumerate(self.order)}
            source = target = pl.ds(col, width)
            if OVER_SEQ in flips:
                source = pl.ds(pl.multiple_of((seq ^ flips.pop(OVER_SEQ)) * (width // 2), BLOCK), width // 2)
                target = pl.ds(0, width // 2)
            flip = sum(value << bit for bit, value in flips.items())
            refs = self.keep if place < half else self.send
            pltpu.make_async_copy(
                self.held.at[mine ^ flip, :, source],
                refs.at[place % half, :, target],
                self.sems.at[chunk],
            ).start()
        self.used.append(pl.ds(col, width))

    def fill(self, source, col):
        width = source.ref.shape[2]
        self.filling = pltpu.make_async_copy(
            source.ref, self.held.at[:, :, pl.ds(col, width)], self.sems.at[15]
        )
        self.filling.start()

    def filled(self):
        self.filling.wait()

    def put_rows(self, result, col):
        put_rows(self.held, result, col)

    def put_cols(self, result, sums, first, col):
        devices, rows, _ = self.held.shape
        width = result.shape[1] // (result.shape[1] * devices // HIDDEN)
        pieces = BLOCK // width
        low = result.astype(LOW)
        tall = low.shape[0] // pieces
        top = iota((rows, width), 0) == 0.0
        for n in range(result.shape[1] // width):
            at = slice(n * width, (n + 1) * width)
            piece = [low[p * tall : (p + 1) * tall, at] for p in range(pieces)]
            piece = piece[0] if pieces == 1 else jnp.concatenate(piece, axis=1)
            for g in range(tall // rows):
                self.held[first + n, :, col + g * BLOCK : col + (g + 1) * BLOCK] = piece[
                    g * rows : (g + 1) * rows, :
                ]
            row = jnp.where(top, sums[:, at], 0.0).astype(LOW)
            row = row if pieces == 1 else jnp.concatenate([row] * pieces, axis=1)
            end = col + (tall // rows) * BLOCK
            self.held[first + n, :, end : end + BLOCK] = row

    def finish(self):
        for chunk, cols in enumerate(self.used):
            whole = self.held.at[:, :, cols]
            pltpu.make_async_copy(whole, whole, self.sems.at[chunk]).wait()


NEAR, FAR, RAW = "near", "far", "raw"
IN_HBM = pl.BlockSpec(memory_space=pltpu.HBM)
IN_VMEM = pl.BlockSpec(memory_space=pltpu.VMEM)
IN_SMEM = pl.BlockSpec(memory_space=pltpu.SMEM)


LIMITS = {'rows_unpack': 14, 'tail_unpack': 6, 'last_unpack': 8, 'dec_pre': 8, 'enc_forward': 19, 'dec_self': 10, 'cross_tail': 27, 'cross_back': 13, 'dec_self_back': 18, 'enc_tail_back': 20, 'enc_self_back': 12, 'dec_input_grad': 10, 'enc_input_grad': 9}
MICROS = {'dec_pre': 30, 'enc_forward': 30, 'dec_self': 30, 'cross_tail': 30, 'cross_back': 30, 'dec_self_back': 30, 'enc_tail_back': 30, 'enc_self_back': 30, 'dec_input_grad': 30, 'enc_input_grad': 30}


def call(kernel, name, scalars, operands, outs, scratch=(), blocks=(), order=(), ahead=()):
    arrays, specs = [], []
    for array, mode, *_ in (*operands, *ahead):
        near = mode == NEAR
        arrays.append(pltpu.with_memory_space_constraint(array, pltpu.VMEM if near else pltpu.HBM))
        specs.append(IN_VMEM if near else IN_HBM)

    def taken(array, mode, start=None, size=None):
        return array.shape if size is None else (size, *array.shape[1:])

    shapes, out_specs = [], []
    for shape, dtype, mode in outs:
        shapes.append((pltpu.VMEM if mode == NEAR else pltpu.HBM)(shape, dtype))
        out_specs.append(IN_VMEM if mode == NEAR else IN_HBM)
    over_seq = OVER_SEQ in order
    devices = 1 << (len(order) - over_seq)
    share = FEATURES // devices
    for columns in blocks:
        shapes += [pltpu.HBM(((1 << len(order)) // 2, share, columns // (1 + over_seq)), LOW)] * 2
        out_specs += [IN_HBM] * 2
    for one in ahead:
        shapes.append(pltpu.VMEM(taken(*one), one[0].dtype))
        out_specs.append(IN_VMEM)
    far_in = [i for i, one in enumerate(operands) if one[1] == FAR]
    far_out = [i for i, one in enumerate(outs) if one[2] == FAR]
    extra = [pltpu.VMEM(shape, dtype) for shape, dtype in scratch]
    extra += [pltpu.VMEM(taken(*operands[i]), operands[i][0].dtype) for i in far_in]
    extra += [pltpu.VMEM(outs[i][0], outs[i][1]) for i in far_out]
    extra += [pltpu.VMEM((devices, share, columns), LOW) for columns in blocks]
    extra += [pltpu.SemaphoreType.DMA((len(far_in) + len(far_out) + len(ahead) + 1,))]
    extra += [pltpu.SemaphoreType.DMA((16,)) for _ in blocks]

    def body(*refs):
        refs = list(refs)
        take = lambda n: [refs.pop(0) for _ in range(n)]
        numbers = take(len(scalars))
        ins = take(len(operands))
        sources = take(len(ahead))
        results = take(len(outs))
        sends = [take(2) for _ in blocks]
        copies = take(len(ahead))
        temps = take(len(scratch))
        near_in = take(len(far_in))
        near_out = take(len(far_out))
        helds = take(len(blocks))
        sems = take(1)[0]
        block_sems = take(len(blocks))
        used = iter(range(len(far_in) + len(far_out) + len(ahead)))

        def coming(ref, near, array, mode, start=None, size=None):
            source = ref if size is None else ref.at[pl.ds(start(numbers[0]), size)]
            return Coming(source, near, sems.at[next(used)])

        given = [Loaded(ref) for ref in ins]
        for n, i in enumerate(far_in):
            given[i] = coming(ins[i], near_in[n], *operands[i])
        later = [coming(ref, near, *one) for ref, near, one in zip(sources, copies, ahead)]
        leaving = {}
        for n, i in enumerate(far_out):
            leaving[i] = Leaving(near_out[n], results[i], sems.at[next(used)])
        made = [leaving.get(i, Loaded(results[i])) for i in range(len(outs))]
        moved = [
            Blocks(keep, send, held, sem, numbers[0], order)
            for (keep, send), held, sem in zip(sends, helds, block_sems)
        ]
        kernel(numbers, given, made, temps, *moved)
        for one in leaving.values():
            one.flush()
        for one in (*given, *later):
            one.get()
        for one in leaving.values():
            one.finish()
        for one in moved:
            one.finish()

    results = pl.pallas_call(
        body,
        name=name,
        out_shape=shapes,
        in_specs=[IN_SMEM] * len(scalars) + specs,
        out_specs=out_specs,
        scratch_shapes=extra,
        cost_estimate=pl.CostEstimate(flops=int(MICROS.get(name, 1.0) * 1.0 * 1.15e9), bytes_accessed=1, transcendentals=0),
        compiler_params=pltpu.CompilerParams(vmem_limit_bytes=LIMITS[name] * 1024 * 1024),
    )(*scalars, *arrays)
    made = len(outs) + 2 * len(blocks)
    return (results[: len(outs)], results[len(outs) : made], results[made:])


def input_rows(halos, own, table, w_in, biases, x_ref, low_ref, rows_ref, start, count, ends, len_row):
    def chunk(embed, target, size):
        places = iota((size, 1), 0) + (start + target - BLOCK).astype(F32)
        x = with_places(embed, places, ends[0], len_row, table)
        low = x.astype(LOW)
        for c in range(3):
            part = dot_nn(low, w_in[:, c * 512 : (c + 1) * 512])
            if c != 1:
                part = part + biases[c // 2 : c // 2 + 1, :]
            rows_ref[pl.ds(target, size), c * 512 : (c + 1) * 512] = part.astype(LOW)
        return (x, low)

    size = min(256, count)

    def body(step, carry):
        at = pl.multiple_of(step * size, size)
        rows = pl.ds(at, size)
        x_ref[rows, :], low_ref[rows, :] = chunk(own[rows, :], pl.multiple_of(at + BLOCK, BLOCK), size)
        return carry

    lax.fori_loop(0, count // size, body, 0)
    for embed, target in halos:
        chunk(embed[...], target, BLOCK)


def enc_kernel(numbers, ins, outs, temps, total):
    left, own, right, lens, table, w_in, gains, biases, upbias, w_out, w_up, w_down = ins
    rows_out, low_out, lse_out, hid_out, mid_out, mid_inv_out, fin_out, fin_inv_out, encoded_out = outs
    (x_ref,) = temps
    count = x_ref.shape[0]
    start = numbers[0][0] * count
    len_row = lens.get()[...].astype(F32)
    ends = pair_ends(len_row)
    size = min(256, count)
    left, own, right, table, w_in, gains, biases, upbias = [
        i.get() for i in (left, own, right, table, w_in, gains, biases, upbias)
    ]
    input_rows(
        [(left, 0), (right, BLOCK + count)], own, table, w_in, biases, x_ref, low_out.ref, rows_out.ref, start, count,
        ends, len_row,
    )
    low_out.flush()
    rows_out.flush()
    width = 3 * BLOCK
    attend_local(
        rows_out.ref, count // BLOCK, width, hid_out.ref, lse_out.ref,
        self_rule(ends, start, total, width, False),
    )
    lse_out.flush()
    hid_out.flush()
    w_out, w_up, w_down = w_out.get(), w_up.get(), w_down.get()
    hid, mid_ref, mid_inv, fin_ref, fin_inv, encoded = [
        o.ref for o in (hid_out, mid_out, mid_inv_out, fin_out, fin_inv_out, encoded_out)
    ]

    def dense(step, carry):
        rows = pl.ds(pl.multiple_of(step * size, size), size)
        z = x_ref[rows, :] + dot_nn(hid[rows, :], w_out[...]) + biases[2:3, :]
        mid, normed, inverse = norm_forward(z, gains[0:1, :], biases[3:4, :])
        mid_ref[rows, :] = normed
        mid_inv[rows, :] = inverse
        low = mid.astype(LOW)
        z = mid + biases[4:5, :]
        for c in range(0, w_up.shape[1], 512):
            up = dot_nn(low, w_up[:, c : c + 512]) + upbias[:, c : c + 512]
            active = (up * sigmoid(up)).astype(LOW)
            z = z + dot_nn(active, w_down[c : c + 512, :])
        final, normed, inverse = norm_forward(z, gains[1:2, :], biases[5:6, :])
        fin_ref[rows, :] = normed
        fin_inv[rows, :] = inverse
        encoded[rows, :] = final.astype(LOW)
        return carry

    lax.fori_loop(0, count // size, dense, 0)


def dec_self_kernel(numbers, ins, outs, temps, total):
    halo, own, lens, table, w_in, gains, biases, w_out, w_query = [i.get() for i in ins]
    low_out, rows_out, lse_out, hid_out, normed_out, inv_out, query_out = outs
    (x,) = temps
    rows_in = rows_out.ref
    count = x.shape[0]
    start = numbers[0][0] * count
    len_row = lens[...].astype(F32)
    ends = pair_ends(len_row)
    input_rows([(halo, 0)], own, table, w_in, biases, x, low_out.ref, rows_in, start, count, ends, len_row)
    low_out.flush()
    rows_out.flush()
    width = 2 * BLOCK
    attend_local(
        rows_in, count // BLOCK, width, hid_out.ref, lse_out.ref,
        self_rule(ends, start, total, width, True),
    )
    size = min(256, count)
    hid, normed_ref, inv_ref, query_ref = [o.ref for o in (hid_out, normed_out, inv_out, query_out)]

    def dense(step, carry):
        rows = pl.ds(pl.multiple_of(step * size, size), size)
        z = x[rows, :] + dot_nn(hid[rows, :], w_out[...]) + biases[2:3, :]
        mid, normed, inverse = norm_forward(z, gains[0:1, :], biases[3:4, :])
        normed_ref[rows, :] = normed
        inv_ref[rows, :] = inverse
        query = dot_nn(mid.astype(LOW), w_query[...]) + biases[4:5, :]
        query_ref[rows, :] = query.astype(LOW)
        return carry

    lax.fori_loop(0, count // size, dense, 0)


def cross_span(src_lens, tgt_lens, first):
    def step(k, carry):
        begin, low, high = carry
        end = begin + tgt_lens[0, k]
        length = src_lens[0, k]
        low = low + jnp.where(end <= first, length, 0)
        high = high + jnp.where(begin <= first + (BLOCK - 1), length, 0)
        return (end, low, high)

    zero = jnp.int32(0)
    _, low, high = lax.fori_loop(0, src_lens.shape[1], step, (zero, zero, zero), unroll=True)
    low = (low // 16) * 16
    return (low, (high - low + (WINDOW - 1)) // WINDOW)


def cross_rule(src_ends_row, tgt_ends_col, first, begin, total):
    key_places = iota((WINDOW, 1), 0) + begin.astype(F32)
    query_places = iota((1, BLOCK), 1) + first.astype(F32)
    allowed = pair_col(src_ends_row, key_places, total) == pair_row(tgt_ends_col, query_places)
    return jnp.where(allowed, 0.0, MASKED)


def cross_forward(numbers, query, memory, others, src_vec, tgt_vec, biases, w, att_out, lse_out, keyval_out, memory_out, max_ref, sum_ref, acc_ref, total):
    idx, src_lens, tgt_lens = numbers
    count = query.shape[0]
    length = memory.shape[0]
    shards = others.shape[0] + 1
    start = idx[0] * count
    src_ends_row, _ = pair_ends(src_vec[...].astype(F32))
    _, tgt_ends_col = pair_ends(tgt_vec[...].astype(F32))
    size = min(256, length)
    for s in range(shards):
        base = lax.rem(idx[0] + s, shards) * length
        memory_out[pl.ds(pl.multiple_of(base, BLOCK), length), :] = memory[...] if s == 0 else others[s - 1]

    def project(step, carry):
        rows = pl.ds(pl.multiple_of(step * size, size), size)
        source = memory_out[rows, :]
        keyval_out[rows, :512] = dot_nn(source, w[:, :512]).astype(LOW)
        keyval_out[rows, 512:] = (dot_nn(source, w[:, 512:]) + biases[5:6, :]).astype(LOW)
        return carry

    lax.fori_loop(0, total // size, project, 0)
    keyval_out[total:, :] = jnp.zeros((WINDOW, 1024), LOW)

    def body(j, carry):
        at = pl.multiple_of(j * BLOCK, BLOCK)
        rows = pl.ds(at, BLOCK)
        first = start + at
        low, windows = cross_span(src_lens, tgt_lens, first)
        max_ref[...] = jnp.full(max_ref.shape, MASKED, F32)
        sum_ref[...] = jnp.zeros(sum_ref.shape, F32)
        acc_ref[...] = jnp.zeros(acc_ref.shape, F32)

        def window(n, carry):
            begin = pl.multiple_of(low + n * WINDOW, 16)
            keys = pl.ds(begin, WINDOW)
            bias = cross_rule(src_ends_row, tgt_ends_col, first, begin, total)
            for group in range(2):
                def part(ref, rows, offset):
                    return lambda lanes: ref[rows, offset + lanes.start : offset + lanes.stop]

                outs, maxima, sums = attend_block(
                    part(query, rows, 0), part(keyval_out, keys, 0), part(keyval_out, keys, 512), bias, group
                )
                for h in range(4):
                    head = group * 4 + h
                    old = max_ref[head : head + 1, :]
                    new = jnp.maximum(old, maxima[h])
                    before, now = jnp.exp(old - new), jnp.exp(maxima[h] - new)
                    max_ref[head : head + 1, :] = new
                    sum_ref[head : head + 1, :] = sum_ref[head : head + 1, :] * before + sums[h] * now
                    part_rows = slice(head * HEAD_DIM, (head + 1) * HEAD_DIM)
                    acc_ref[part_rows, :] = acc_ref[part_rows, :] * before + outs[h] * now
            return carry

        lax.fori_loop(0, windows, window, 0)
        for group in range(2):
            heads = range(group * 4, group * 4 + 4)
            mixed = jnp.concatenate(
                [
                    acc_ref[h * HEAD_DIM : (h + 1) * HEAD_DIM, :] * (1.0 / sum_ref[h : h + 1, :])
                    for h in heads
                ],
                axis=0,
            )
            att_out[rows, group * GROUP : (group + 1) * GROUP] = mixed.T
            lse_out[j, group : group + 1, :] = jnp.concatenate(
                [max_ref[h : h + 1, :] + jnp.log(sum_ref[h : h + 1, :]) for h in heads], axis=1
            )
        return carry

    lax.fori_loop(0, count // BLOCK, body, 0)


def feed_forward_grads(mid, up_low, ffn, active, hid, branch, sums, blocks):
    hidden = up_low.shape[1]
    devices, rows, _ = blocks.held.shape
    width = hidden // devices
    down = hidden + BLOCK

    def down_part(c, carry):
        cols = pl.ds(pl.multiple_of(c * 512, 512), 512)
        blocks.put_cols(dot_tn(ffn[...], active[:, cols]), sums[pl.ds(8 + c, 1), :], c * (512 // width), 0)
        return carry

    def up_part(c, carry):
        cols = pl.ds(pl.multiple_of(c * 512, 512), 512)
        blocks.put_rows(dot_tn(mid[...], up_low[:, cols]), down + c * 512)
        return carry

    lax.fori_loop(0, hidden // 512, down_part, 0)
    blocks.spread(0, down)
    lax.fori_loop(0, hidden // 512, up_part, 0)
    blocks.spread(down, hidden)
    blocks.put_rows(dot_tn(hid[...], branch[...]), down + hidden)
    blocks.spread(down + hidden, 512)


def cross_tail_kernel(numbers, ins, outs, temps, blocks, total):
    (query, memory, others, src_vec, tgt_vec, gains, biases, upbias, w_keyval, normed_in, cot, w_out, w_up, w_down) = [
        i.get() for i in ins
    ]
    att, lse_out, keyval_out, memory_out, decoded_out, att_grad_out, branch_out, sums_out = [o.ref for o in outs]
    hid_ref, branch_ref, mid_ref, up_ref, active_ref, ffn_ref, up_low_ref, *running = temps
    cross_forward(
        numbers, query, memory, others, src_vec, tgt_vec, biases, w_keyval, att, lse_out, keyval_out, memory_out,
        *running, total,
    )
    count = att.shape[0]
    hidden = w_up.shape[1]
    sums_out[...] = jnp.zeros(sums_out.shape, F32)
    size = min(256, count)

    def dense(step, carry):
        rows = pl.ds(pl.multiple_of(step * size, size), size)
        hid = att[rows, :].astype(LOW)
        hid_ref[rows, :] = hid
        first = normed_in[rows, :] * gains[0:1, :] + biases[3:4, :]
        z = first + dot_nn(hid, w_out[...]) + biases[6:7, :]
        mid, normed, inverse = norm_forward(z, gains[1:2, :], biases[7:8, :])
        low = mid.astype(LOW)
        mid_ref[rows, :] = low
        z = mid + biases[8:9, :]
        for c in range(0, hidden, 512):
            up = dot_nn(low, w_up[:, c : c + 512]) + upbias[:, c : c + 512]
            gate = sigmoid(up)
            active = up * gate
            up_ref[:, c : c + 512] = gate + active * (1.0 - gate)
            active = active.astype(LOW)
            active_ref[rows, c : c + 512] = active
            z = z + dot_nn(active, w_down[c : c + 512, :])
        final, normed_final, inverse_final = norm_forward(z, gains[2:3, :], biases[9:10, :])
        decoded_out[rows, :] = final.astype(LOW)
        grad = cot[rows, :].astype(F32)
        ffn = norm_backward(grad, normed_final, inverse_final, gains[2:3, :])
        ffn_low = ffn.astype(LOW)
        ffn_ref[rows, :] = ffn_low
        mid_grad = ffn
        for c in range(0, hidden, 512):
            up_grad = dot_nt(ffn_low, w_down[c : c + 512, :]) * up_ref[:, c : c + 512]
            sums_out[8 + c // 512 : 9 + c // 512, :] += col_sum(up_grad)
            up_low = up_grad.astype(LOW)
            up_low_ref[rows, c : c + 512] = up_low
            mid_grad = mid_grad + dot_nt(up_low, w_up[:, c : c + 512])
        branch = norm_backward(mid_grad, normed, inverse, gains[1:2, :])
        branch_low = branch.astype(LOW)
        branch_out[rows, :] = branch
        branch_ref[rows, :] = branch_low
        att_grad_out[rows, :] = dot_nt(branch_low, w_out[...]).astype(LOW)
        sums_out[0:1, :] += col_sum(mid_grad * normed)
        sums_out[1:2, :] += col_sum(grad * normed_final)
        sums_out[2:3, :] += col_sum(branch)
        sums_out[3:4, :] += col_sum(mid_grad)
        sums_out[4:5, :] += col_sum(ffn)
        sums_out[5:6, :] += col_sum(grad)
        return carry

    lax.fori_loop(0, count // size, dense, 0)
    for out in (outs[0], outs[3], outs[4], outs[6]):
        out.flush()
    feed_forward_grads(
        mid_ref, up_low_ref, ffn_ref, active_ref, hid_ref, branch_ref, sums_out, blocks
    )


def cross_back_kernel(numbers, ins, outs, temps, total):
    idx, src_lens, tgt_lens = numbers
    query, keyval, att, att_grad, lse, src_vec, tgt_vec = [i.get() for i in ins[:7]]
    mem_own_out, mem_out, query_out, keyval_low, sums_out = [o.ref for o in outs]
    (keyval_ref,) = temps
    count = query.shape[0]
    start = idx[0] * count
    src_ends_row, _ = pair_ends(src_vec[...].astype(F32))
    _, tgt_ends_col = pair_ends(tgt_vec[...].astype(F32))
    keyval_ref[...] = jnp.zeros(keyval_ref.shape, F32)
    query_out[...] = jnp.zeros(query_out.shape, F32)
    sums_out[...] = jnp.zeros(sums_out.shape, F32)
    select = jnp.where(
        lax.broadcasted_iota(jnp.int32, (HEADS, 512), 1) // HEAD_DIM
        == lax.broadcasted_iota(jnp.int32, (HEADS, 512), 0),
        1.0,
        0.0,
    )

    def body(j, carry):
        at = pl.multiple_of(j * BLOCK, BLOCK)
        rows = pl.ds(at, BLOCK)
        first = start + at
        low, windows = cross_span(src_lens, tgt_lens, first)
        weighed = att[rows, :] * att_grad[rows, :].astype(F32)
        deltas = lax.dot_general(
            select, weighed, (((1,), (1,)), ((), ())),
            precision=lax.Precision.HIGHEST, preferred_element_type=F32,
        )

        def window(n, carry):
            begin = pl.multiple_of(low + n * WINDOW, 16)
            keys = pl.ds(begin, WINDOW)
            bias = cross_rule(src_ends_row, tgt_ends_col, first, begin, total)
            for group in range(2):
                lo, hi = group * GROUP, (group + 1) * GROUP
                query_grad, key_grad, value_grad = attend_back_block(
                    query[rows, lo:hi],
                    att_grad[rows, lo:hi],
                    keyval[keys, lo:hi],
                    keyval[keys, 512 + lo : 512 + hi],
                    bias,
                    lse[j, group : group + 1, :],
                    [deltas[group * 4 + h : group * 4 + h + 1, :] for h in range(4)],
                )
                query_out[rows, lo:hi] += query_grad.T
                keyval_ref[keys, lo:hi] += key_grad
                keyval_ref[keys, 512 + lo : 512 + hi] += value_grad
            return carry

        lax.fori_loop(0, windows, window, 0)
        return carry

    lax.fori_loop(0, count // BLOCK, body, 0)
    size = min(256, total)
    shards = mem_out.shape[0] + 1
    length = total // shards

    def to_memory(step, carry):
        rows = pl.ds(pl.multiple_of(step * size, size), size)
        grads = keyval_ref[rows, :]
        sums_out[0:1, :] += col_sum(grads[:, 512:])
        keyval_low[rows, :] = grads.astype(LOW)
        return carry

    lax.fori_loop(0, total // size, to_memory, 0)
    w_keyval = ins[7].get()
    for s in reversed(range(shards)):
        base = pl.multiple_of(lax.rem(idx[0] + s, shards) * length, BLOCK)
        grads = dot_nt(keyval_low[pl.ds(base, length), :], w_keyval[...])
        if s == 0:
            mem_own_out[...] = grads
        else:
            mem_out[s - 1] = grads.astype(LOW)


def dec_self_back_kernel(numbers, ins, outs, temps, total):
    query_grads, keyval_low, memory, normed_in, inv_in, branch_in, hid_in, gains, biases, w_query, w_out = [
        i.get() for i in ins[:11]
    ]
    branch_out, sums_out = [o.ref for o in outs[:2]]
    branch_ref, query_low, mid_ref, att_grad_out = temps[:4]
    count = query_grads.shape[0]
    sums_out[...] = jnp.zeros(sums_out.shape, F32)
    size = min(256, count)

    def dense(step, carry):
        rows = pl.ds(pl.multiple_of(step * size, size), size)
        query_grad = query_grads[rows, :]
        low = query_grad.astype(LOW)
        query_low[rows, :] = low
        normed = normed_in[rows, :]
        mid_ref[rows, :] = (normed * gains[0:1, :] + biases[3:4, :]).astype(LOW)
        mid_grad = branch_in[rows, :] + dot_nt(low, w_query[...])
        branch = norm_backward(mid_grad, normed, inv_in[rows, :], gains[0:1, :])
        branch_low = branch.astype(LOW)
        branch_out[rows, :] = branch
        branch_ref[rows, :] = branch_low
        att_grad_out[rows, :] = dot_nt(branch_low, w_out[...]).astype(LOW)
        sums_out[0:1, :] += col_sum(mid_grad * normed)
        sums_out[1:2, :] += col_sum(branch)
        sums_out[2:3, :] += col_sum(mid_grad)
        sums_out[3:4, :] += col_sum(query_grad)
        return carry

    lax.fori_loop(0, count // size, dense, 0)
    outs[0].flush()
    held = outs[2].ref

    def keyval_part(c, carry):
        cols = pl.ds(pl.multiple_of(c * 512, 512), 512)
        put_rows(held, dot_tn(memory[...], keyval_low[:, cols]), c * 512)
        return carry

    lax.fori_loop(0, 2, keyval_part, 0)
    put_rows(held, dot_tn(mid_ref[...], query_low[...]), 1024)
    put_rows(held, dot_tn(hid_in[...], branch_ref[...]), 1536)
    outs[2].flush()
    self_back(numbers, Loaded(att_grad_out), *ins[11:], outs[3:], *temps[4:], total, True)


def enc_self_back_kernel(numbers, ins, outs, temps, total):
    self_back(numbers, *ins, outs, *temps, total, False)


def self_back(numbers, att_grad, lse, lens, rows_in, outs, query_ref, keyval_ref, total, causal):
    own_out, halos = outs[0].ref, [o.ref for o in outs[1:]]
    rows_in, att_grad, lse = rows_in.get(), att_grad.get(), lse.get()
    count = att_grad.shape[0]
    ends = pair_ends(lens.get()[...].astype(F32))
    width = (2 if causal else 3) * BLOCK
    attend_local_back(
        rows_in, att_grad, lse, count // BLOCK, width, query_ref, keyval_ref,
        self_rule(ends, numbers[0][0] * count, total, width, causal),
    )
    if causal:
        halos[0][...] = keyval_ref[:BLOCK, :].astype(LOW)
    elif len(halos) == 1:
        edge = pl.multiple_of((1 - numbers[0][0]) * (BLOCK + count), BLOCK)
        halos[0][...] = keyval_ref[pl.ds(edge, BLOCK), :].astype(LOW)
    else:
        halos[0][...] = keyval_ref[:BLOCK, :].astype(LOW)
        halos[1][...] = keyval_ref[BLOCK + count :, :].astype(LOW)
    for out in outs[1:]:
        out.flush()
    own_out[:, :512] = query_ref[...]
    own_out[:, 512:] = keyval_ref[BLOCK : BLOCK + count, :]


def input_grad(own, edges, low_in, branch, w, grad_out, sums_out, low_ref, put, count):
    sums_out[...] = jnp.zeros(sums_out.shape, F32)
    size = min(256, count)

    def dense(step, carry):
        rows = pl.ds(pl.multiple_of(step * size, size), size)
        grads = own[rows, :]
        sums_out[0:1, :] += col_sum(grads[:, :512])
        sums_out[1:2, :] += col_sum(grads[:, 1024:])
        low_ref[rows, :] = grads.astype(LOW)
        return carry

    lax.fori_loop(0, count // size, dense, 0)
    returned = jnp.zeros((count, 1024), F32) if len(edges) > 1 and count == BLOCK else None
    for at, halo in edges:
        edge = pl.ds(at, BLOCK)
        grads = halo[...].astype(F32)
        sums_out[1:2, :] += col_sum(grads[:, 512:])
        if returned is not None:
            returned = grads = returned + grads
        low_ref[edge, 512:] = (own[edge, 512:] + grads).astype(LOW)

    def weight_part(c, carry):
        cols = pl.ds(pl.multiple_of(c * 512, 512), 512)
        put(dot_tn(low_in[...], low_ref[:, cols]), c * 512)
        return carry

    lax.fori_loop(0, 3, weight_part, 0)

    def back():
        def dense_grad(step, carry):
            rows = pl.ds(pl.multiple_of(step * size, size), size)
            grad_out[rows, :] = (branch[rows, :] + dot_nt(low_ref[rows, :], w[...])).astype(grad_out.dtype)
            return carry

        lax.fori_loop(0, count // size, dense_grad, 0)

    return back


def dec_input_grad_kernel(numbers, ins, outs, temps, blocks):
    blocks.fill(ins[-1], 1536)
    halo, own, branch, low_in, w = [i.get() for i in ins[:-1]]
    grad_out, sums_out = [o.ref for o in outs]
    (low_ref,) = temps
    count = own.shape[0]
    back = input_grad(
        own, [(count - BLOCK, halo)], low_in, branch, w, grad_out, sums_out, low_ref, blocks.put_rows, count
    )
    blocks.filled()
    blocks.spread(0, blocks.held.shape[2])
    back()


def enc_input_grad_kernel(numbers, ins, outs, temps, blocks, halo_count):
    halos = [i.get() for i in ins[:halo_count]]
    own, branch, low_in, w, *sums = [i.get() for i in ins[halo_count:]]
    (grad_out,) = [o.ref for o in outs]
    low_ref, sums_ref, small_ref = temps
    count = own.shape[0]
    if halo_count == 1:
        edges = [(pl.multiple_of((1 - numbers[0][0]) * (count - BLOCK), BLOCK), halos[0])]
    else:
        edges = [(0, halos[0]), (count - BLOCK, halos[1])]
    back = input_grad(own, edges, low_in, branch, w, grad_out, sums_ref, low_ref, blocks.put_rows, count)
    small_ref[...] = jnp.zeros(small_ref.shape, F32)
    for n, part in enumerate((*sums, sums_ref)):
        small_ref[n * 8 : (n + 1) * 8, :] = part[:8, :]
    blocks.put_rows(small_ref[...].T, 1536)
    blocks.spread(0, 1536 + BLOCK)
    back()


def enc_tail_back_kernel(numbers, ins, outs, temps, blocks):
    (mem_own, mem_others, cot, fin_in, fin_inv, mid_in, mid_inv, hid_in, gains, biases, upbias, w_down, w_up,
     w_out) = [i.get() for i in ins]
    branch_out, att_grad_out, sums_out = [o.ref for o in outs]
    branch_ref, mid_ref, active_ref, ffn_ref, up_low_ref = temps
    count = cot.shape[0]
    hidden = w_up.shape[1]
    sums_out[...] = jnp.zeros(sums_out.shape, F32)
    size = min(256, count)

    def dense(step, carry):
        rows = pl.ds(pl.multiple_of(step * size, size), size)
        grad = cot[rows, :].astype(F32) + mem_own[rows, :]
        for s in range(mem_others.shape[0]):
            grad = grad + mem_others[s, rows, :].astype(F32)
        normed_final = fin_in[rows, :]
        ffn = norm_backward(grad, normed_final, fin_inv[rows, :], gains[1:2, :])
        ffn_low = ffn.astype(LOW)
        ffn_ref[rows, :] = ffn_low
        normed = mid_in[rows, :]
        low = (normed * gains[0:1, :] + biases[3:4, :]).astype(LOW)
        mid_ref[rows, :] = low
        mid_grad = ffn
        for c in range(0, hidden, 512):
            up = dot_nn(low, w_up[:, c : c + 512]) + upbias[:, c : c + 512]
            gate = sigmoid(up)
            active = up * gate
            active_ref[rows, c : c + 512] = active.astype(LOW)
            up_grad = dot_nt(ffn_low, w_down[c : c + 512, :]) * (gate + active * (1.0 - gate))
            sums_out[8 + c // 512 : 9 + c // 512, :] += col_sum(up_grad)
            up_low = up_grad.astype(LOW)
            up_low_ref[rows, c : c + 512] = up_low
            mid_grad = mid_grad + dot_nt(up_low, w_up[:, c : c + 512])
        branch = norm_backward(mid_grad, normed, mid_inv[rows, :], gains[0:1, :])
        branch_low = branch.astype(LOW)
        branch_out[rows, :] = branch
        branch_ref[rows, :] = branch_low
        att_grad_out[rows, :] = dot_nt(branch_low, w_out[...]).astype(LOW)
        sums_out[0:1, :] += col_sum(mid_grad * normed)
        sums_out[1:2, :] += col_sum(grad * normed_final)
        sums_out[2:3, :] += col_sum(branch)
        sums_out[3:4, :] += col_sum(mid_grad)
        sums_out[4:5, :] += col_sum(ffn)
        sums_out[5:6, :] += col_sum(grad)
        return carry

    lax.fori_loop(0, count // size, dense, 0)
    outs[0].flush()
    feed_forward_grads(
        mid_ref, up_low_ref, ffn_ref, active_ref, hid_in, branch_ref, sums_out, blocks
    )


def log2(number):
    bits = number.bit_length() - 1
    assert number == 1 << bits
    return bits


def swapped(value, axis, bit, devices):
    return lax.ppermute(value, axis, [(i, i ^ (1 << bit)) for i in range(devices)])


class Chain:
    def __init__(self, token):
        self.token = token

    def tie(self, *values):
        self.token, *values = lax.optimization_barrier((self.token, *values))
        return values[0] if len(values) == 1 else values


class Reduction:
    def __init__(self, chain, arrays, order, devices, seq_count):
        self.chain, self.order, self.devices, self.seq_count = (chain, order, devices, seq_count)
        self.keep, send = arrays
        self.size = self.keep.shape[0]
        self.received, self.low, self.others = [], None, []
        self.push(send)

    def push(self, send):
        bit = self.order[len(self.received)]
        if bit == OVER_SEQ:
            self.received.append(swapped(send, "seq", 0, self.seq_count))
        else:
            self.received.append(swapped(send, "dp", bit, self.devices))

    def part(self, first, last):
        total = self.keep[first:last].astype(F32)
        for piece in self.received:
            total = total + piece[first:last].astype(F32)
        return total

    def next(self):
        self.received[-1] = self.chain.tie(self.received[-1])
        if len(self.received) < len(self.order):
            half = self.size // 2
            self.push(self.chain.tie(self.part(half, self.size).astype(LOW)))
            self.size = half
            return
        self.low = self.chain.tie(self.part(0, 1)[0].astype(LOW))
        if log2(self.seq_count):
            self.others.append(swapped(self.low, "seq", 0, self.seq_count))

    def pair(self):
        while self.low is None:
            self.next()
        low, other = self.low, self.others[0]
        if OVER_SEQ not in self.order:
            for bit in range(1, log2(self.seq_count)):
                low = lax.optimization_barrier((low.astype(F32) + other.astype(F32)).astype(LOW))
                other = swapped(low, "seq", bit, self.seq_count)
        return (low, other)


def from_shards(own, count):
    return jnp.stack(
        [lax.ppermute(own, "seq", [((i + s) % count, i) for i in range(count)]) for s in range(1, count)]
    )


def feed_forward_unpack(numbers, ins, outs, temps):
    low, other = [i.get() for i in ins]
    up_out, matrix_out, down_out, bias_out = [o.ref for o in outs]
    (total,) = temps
    total[...] = low[...].astype(F32) + other[...].astype(F32)
    share = up_out.shape[0]
    width = down_out.shape[0]
    pieces = BLOCK // width
    groups = FEATURES // pieces // share
    tall = jnp.concatenate([total[:, g * BLOCK : (g + 1) * BLOCK] for g in range(groups)], axis=0).T
    for p in range(pieces):
        rows = FEATURES // pieces
        down_out[:, p * rows : (p + 1) * rows] = tall[p * width : (p + 1) * width, :]
    end = groups * BLOCK
    bias_out[...] = total[0:1, end : end + width]
    up_out[...] = total[:, HIDDEN + BLOCK : 2 * HIDDEN + BLOCK]
    matrix_out[...] = total[:, 2 * HIDDEN + BLOCK :]


def decoder_unpack(numbers, ins, outs, temps, halved):
    low, other = [i.get() for i in ins]
    (total,) = temps
    if halved:
        width = low.shape[1]
        seq = numbers[0][0]
        total[:, pl.ds(pl.multiple_of(seq * width, BLOCK), width)] = low[...].astype(F32)
        total[:, pl.ds(pl.multiple_of((1 - seq) * width, BLOCK), width)] = other[...].astype(F32)
    else:
        total[...] = low[...].astype(F32) + other[...].astype(F32)
    at = 0
    for out in outs:
        width = out.ref.shape[1]
        out.ref[...] = total[:, at : at + width]
        at += width


def encoder_unpack(numbers, ins, outs, temps, picks):
    low, other = [i.get() for i in ins]
    total = low[...].astype(F32) + other[...].astype(F32)
    outs[0].ref[...] = total[:, :1536]
    small = total[:, 1536:].T
    for out, rows in zip(outs[1:], picks):
        for n, row in enumerate(rows):
            out.ref[n : n + 1, :] = small[row : row + 1, :]


def last_unpack(numbers, ins, outs, temps, picks, halved):
    feed_forward_unpack(numbers, ins[:2], outs[:4], temps[:1])
    for out in outs[:4]:
        out.flush()
    encoder_unpack(numbers, ins[2:4], outs[4:9], (), picks)
    for out in outs[4:9]:
        out.flush()
    decoder_unpack(numbers, ins[4:], outs[9:], temps[1:], halved)


def rows_unpack(numbers, ins, outs, temps):
    shards = numbers[0]
    for n, out in enumerate(outs):
        own, others = ins[2 * n].get(), ins[2 * n + 1].get()
        count = own.shape[0]
        parts = others.shape[0] + 1
        for s in range(parts):
            at = pl.ds(pl.multiple_of(lax.rem(shards[0] + s, parts) * count, BLOCK), count)
            out.ref[at, :] = (own[...] if s == 0 else others[s - 1]).astype(out.ref.dtype)
        out.flush()


def local(
    src_embed, tgt_embed, src_lengths, tgt_lengths, enc_cotangent, dec_cotangent,
    enc_inproj, enc_outproj, enc_upproj, enc_downproj, enc_gains, enc_biases, enc_upbias,
    dec_inproj, dec_outproj, cross_query, cross_keyval, cross_outproj, dec_upproj, dec_downproj,
    dec_gains, dec_biases, dec_upbias,
):
    _, count, features = src_embed.shape
    total = tgt_embed.shape[1]
    hidden = enc_upproj.shape[1]
    devices = lax.axis_size("dp")
    seq_count = lax.axis_size("seq")
    pair = seq_count == 2
    blocks = count // BLOCK
    bits = log2(devices)
    x_first = tuple(range(bits))
    y_first = (0, OVER_SEQ, *range(1, bits)) if seq_count == 2 else x_first
    seq_index = lax.axis_index("seq")
    dp_index = lax.axis_index("dp")
    idx = jnp.where(jnp.arange(2) == 0, seq_index, dp_index).astype(jnp.int32)
    chain = Chain(idx)
    table = jnp.asarray(place_table(features))
    src_own, tgt_all = src_embed[0], tgt_embed[0]
    enc_ub, dec_ub = enc_upbias[None], dec_upbias[None]
    up = [(i, i + 1) for i in range(seq_count - 1)]
    down = [(i + 1, i) for i in range(seq_count - 1)]
    swap = [(0, 1), (1, 0)]
    wide = (count, features)
    near = lambda *arrays: [(a, NEAR) for a in arrays]
    far = lambda *arrays: [(a, FAR) for a in arrays]
    part = functools.partial
    lse = ((blocks, 2, 512), F32)
    inv = ((count, 1), F32)
    begin = lambda numbers: pl.multiple_of(numbers[0] * count, BLOCK)
    before = lambda numbers: pl.multiple_of(jnp.maximum(numbers[0] * count - BLOCK, 0), BLOCK)

    if pair:
        edge = lax.dynamic_slice_in_dim(src_own, (1 - seq_index) * (count - BLOCK), BLOCK, 0)
        left = right = lax.ppermute(chain.tie(edge), "seq", swap)
    else:
        left = lax.ppermute(src_own[count - BLOCK :], "seq", up)
        right = lax.ppermute(src_own[:BLOCK], "seq", down)
    (enc_rows, src_low, enc_lse, enc_hid, mid_normed, mid_inv, fin_normed, fin_inv, encoded), _, self_near = call(
        part(enc_kernel, total=total), "enc_forward", [chain.token],
        [*near(left), *far(src_own), *near(right), *far(src_lengths, table, enc_inproj, enc_gains, enc_biases, enc_ub),
         *far(enc_outproj, enc_upproj, enc_downproj)],
        [((count + 2 * BLOCK, 1536), LOW, FAR), (wide, LOW, FAR), (*lse, FAR),
         (wide, LOW, FAR), (wide, F32, FAR), (*inv, FAR),
         (wide, F32, FAR), (*inv, FAR), (wide, LOW, FAR)],
        [(wide, F32)],
        ahead=[(tgt_all, FAR, before, BLOCK), (tgt_all, FAR, begin, count),
               *far(tgt_lengths, table, dec_inproj, dec_gains, dec_biases, dec_outproj, cross_query)],
    )
    encoded = chain.tie(encoded)
    others = from_shards(encoded, seq_count)
    idx_self, _ = lax.optimization_barrier((chain.token, encoded))
    (tgt_low, dec_rows, dec_lse, dec_hid, self_normed, self_inv, cross_q), _, tail_near = call(
        part(dec_self_kernel, total=total), "dec_self", [idx_self], near(*self_near),
        [(wide, LOW, FAR), ((count + BLOCK, 1536), LOW, FAR), (*lse, FAR), (wide, LOW, FAR), (wide, F32, FAR), (*inv, FAR),
         (wide, LOW, FAR)],
        [(wide, F32)],
        ahead=[*far(encoded, src_lengths, tgt_lengths, dec_gains, dec_biases, dec_ub, cross_keyval),
               (dec_cotangent[0], FAR, begin, count), *far(cross_outproj, dec_upproj, dec_downproj)],
    )
    (cross_att, cross_lse, keyval, memory, decoded, cross_att_grad, cross_branch, tail_sums), tail, back_near = call(
        part(cross_tail_kernel, total=total), "cross_tail", [chain.token, src_lengths, tgt_lengths],
        [*far(cross_q), *near(tail_near[0]), *near(others), *near(*tail_near[1:7]), *far(self_normed), *near(*tail_near[7:])],
        [(wide, F32, FAR), (*lse, NEAR), ((total + WINDOW, 1024), LOW, NEAR), ((total, features), LOW, FAR),
         (wide, LOW, FAR), (wide, LOW, NEAR), (wide, F32, FAR), ((16, features), F32, FAR)],
        [(wide, LOW), (wide, LOW), (wide, LOW), ((min(256, count), hidden), F32), ((count, hidden), LOW),
         (wide, LOW), ((count, hidden), LOW),
         ((HEADS, BLOCK), F32), ((HEADS, BLOCK), F32), ((features, BLOCK), F32)],
        [2 * hidden + BLOCK + 512], x_first,
        ahead=far(src_lengths, tgt_lengths),
    )
    decoded = chain.tie(decoded)
    decoded_others = from_shards(decoded, seq_count)
    make = part(Reduction, devices=devices, seq_count=seq_count)
    tail = make(chain, tail, x_first)
    (mem_own, mem_send, query_grads, keyval_grads, mem_sums), _, dense_near = call(
        part(cross_back_kernel, total=total), "cross_back", [chain.token, src_lengths, tgt_lengths],
        [*far(cross_q), *near(keyval), *far(cross_att), *near(cross_att_grad, cross_lse, *back_near), *far(cross_keyval)],
        [(wide, F32, FAR), ((seq_count - 1, *wide), LOW, FAR), (wide, F32, NEAR),
         ((total, 1024), LOW, NEAR), ((8, features), F32, FAR)],
        [((total + WINDOW, 1024), F32)],
        ahead=[*far(memory, self_normed, self_inv, cross_branch),
               *far(dec_hid, dec_gains, dec_biases, cross_query, dec_outproj, dec_lse, tgt_lengths, dec_rows)],
    )
    mem_send = chain.tie(mem_send)
    mem_others = jnp.stack(
        [
            lax.ppermute(mem_send[s - 1], "seq", [(i, (i + s) % seq_count) for i in range(seq_count)])
            for s in range(1, seq_count)
        ]
    )
    decoded_others = chain.tie(decoded_others)
    tail.next()
    (self_branch, cross_sums, cross_held, self_own, self_halo), _, enc_near = call(
        part(dec_self_back_kernel, total=total), "dec_self_back", [chain.token],
        near(query_grads, keyval_grads, *dense_near),
        [(wide, F32, FAR), ((8, features), F32, FAR), ((devices, features // devices, 2048), LOW, FAR),
         ((count, 1536), F32, FAR), ((BLOCK, 1024), LOW, FAR)],
        [(wide, LOW), (wide, LOW), (wide, LOW), (wide, LOW), (wide, F32), ((count + BLOCK, 1024), F32)],
        ahead=far(enc_cotangent[0], fin_normed, fin_inv, mid_normed, mid_inv, enc_hid, enc_gains, enc_biases,
                  enc_ub, enc_downproj, enc_upproj, enc_outproj),
    )
    self_halo = chain.tie(self_halo)
    self_returned = lax.ppermute(self_halo, "seq", down)
    mem_others = chain.tie(mem_others)
    (enc_branch, enc_att_grad, enc_sums), enc, self_near = call(
        enc_tail_back_kernel, "enc_tail_back", [chain.token],
        [*far(mem_own), *near(mem_others), *near(*enc_near)],
        [(wide, F32, FAR), (wide, LOW, FAR), ((16, features), F32, FAR)],
        [(wide, LOW), (wide, LOW), ((count, hidden), LOW), (wide, LOW), ((count, hidden), LOW)],
        [2 * hidden + BLOCK + 512], x_first,
        ahead=far(self_own, self_branch, tgt_low, dec_inproj),
    )
    enc_sums = chain.tie(enc_sums)
    enc = make(chain, enc, x_first)
    self_returned = chain.tie(self_returned)
    (tgt_part, self_sums), cross, back_near = call(
        dec_input_grad_kernel, "dec_input_grad", [chain.token],
        [*near(self_returned), *near(*self_near), (cross_held, RAW)],
        [(wide, LOW, FAR), ((8, features), F32, FAR)],
        [((count, 1536), LOW)],
        [1536 + 2048], y_first,
        ahead=far(enc_att_grad, enc_lse, src_lengths, enc_rows),
    )
    tgt_part = chain.tie(tgt_part)
    cross = make(chain, cross, y_first)
    tgt_others = from_shards(tgt_part, seq_count)
    tail.next()
    enc.next()
    (enc_own, *halos), _, in_near = call(
        part(enc_self_back_kernel, total=total), "enc_self_back", [chain.token], near(*back_near),
        [((count, 1536), F32, NEAR)] + [((BLOCK, 1024), LOW, FAR)] * (1 if pair else 2),
        [(wide, F32), ((count + 2 * BLOCK, 1024), F32)],
        ahead=far(enc_branch, src_low, enc_inproj),
    )
    halos = [chain.tie(h) for h in halos]
    if pair:
        halos = [lax.ppermute(halos[0], "seq", swap)]
    else:
        halos = [lax.ppermute(halos[1], "seq", up), lax.ppermute(halos[0], "seq", down)]
    cross.next()
    tail.next()
    tgt_others = chain.tie(tgt_others)
    halos = [chain.tie(h) for h in halos]
    (src_grad,), ins, _ = call(
        part(enc_input_grad_kernel, halo_count=len(halos)), "enc_input_grad", [chain.token],
        [*near(*halos), *near(enc_own, *in_near), *far(tail_sums, mem_sums, cross_sums, self_sums, enc_sums)],
        [(wide, F32, FAR)],
        [((count, 1536), LOW), ((8, features), F32), ((BLOCK, features), F32)],
        [1536 + BLOCK], x_first,
    )
    src_grad = chain.tie(src_grad)
    ins = make(chain, ins, x_first)
    share = features // devices
    slim = lambda *widths: [((share, w), F32, FAR) for w in widths]
    matrices = [*slim(hidden, 512), ((hidden // devices, 512), F32, FAR), ((1, hidden // devices), F32, FAR)]
    all_rows = (total, features)
    packed = ((share, 2 * hidden + BLOCK + 512), F32)
    enc.next()
    ins.next()
    tail.next()
    cross.next()
    ins.next()
    enc.next()
    (decoded_all, tgt_all_grad), _, _ = call(
        rows_unpack, "rows_unpack", [chain.token], [*far(decoded), *near(decoded_others), *far(tgt_part), *near(tgt_others)],
        [(all_rows, LOW, FAR), (all_rows, F32, FAR)],
    )
    tgt_all_grad = chain.tie(tgt_all_grad)
    (dec_up, cross_out, dec_down, dec_ub_grad), _, _ = call(
        feed_forward_unpack, "tail_unpack", [chain.token], near(*tail.pair()), matrices, [packed]
    )
    dec_up = chain.tie(dec_up)
    cross.next()
    ins.next()
    enc.next()
    cross.next()
    ins.next()
    cross.next()
    t, m, c, d, e, i = range(0, 48, 8)
    picks = [
        (e, e + 1),
        (i, i + 1, e + 2, e + 3, e + 4, e + 5),
        (c, t, t + 1),
        (d, d + 1, c + 1, c + 2, c + 3, m, t + 2, t + 3, t + 4, t + 5),
    ]
    (enc_up, enc_out, enc_down, enc_ub_grad, enc_in, enc_gains_grad, enc_biases_grad, dec_gains_grad, dec_biases_grad,
     dec_in, keyval_grad, query_grad, dec_out), _, _ = call(
        part(last_unpack, picks=picks, halved=OVER_SEQ in y_first), "last_unpack", [chain.token],
        near(*enc.pair(), *ins.pair(), *cross.pair()),
        [*matrices, *slim(1536), *[((len(p), share), F32, FAR) for p in picks], *slim(1536, 1024, 512, 512)],
        [packed, ((share, 3584), F32)],
    )
    return (
        encoded[None],
        decoded_all[None],
        src_grad[None],
        tgt_all_grad[None],
        enc_in,
        enc_out,
        enc_up,
        enc_down,
        enc_gains_grad,
        enc_biases_grad,
        enc_ub_grad[0],
        dec_in,
        dec_out,
        query_grad,
        keyval_grad,
        cross_out,
        dec_up,
        dec_down,
        dec_gains_grad,
        dec_biases_grad,
        dec_ub_grad[0],
    )


def solution(mesh):
    rows, whole = P("dp", "seq", None), P("dp", None, None)
    return jax.shard_map(
        local,
        mesh=mesh,
        in_specs=(rows, whole, P("dp", None), P("dp", None), rows, whole, *([P()] * 17)),
        out_specs=(
            rows, whole, rows, whole,
            *([P("dp", None)] * 4), P(None, "dp"), P(None, "dp"), P("dp"),
            *([P("dp", None)] * 7), P(None, "dp"), P(None, "dp"), P("dp"),
        ),
        check_vma=False,
    )
```

```python
import functools
import math

import jax
import jax.numpy as jnp
import numpy as np
from jax import lax
from jax.experimental import pallas as pl
from jax.experimental.pallas import tpu as pltpu
from jax.sharding import PartitionSpec as P

HEADS = 8
HEAD_DIM = 64
MAXPAIR = 128
BLOCK = 128
GROUP = 256
WINDOW = 256
LOW = jnp.bfloat16
F32 = jnp.float32
MASKED = -1e30
FEATURES = 512
HIDDEN = 2048


def place_table(features):
    half = features // 2
    frequency = np.exp(-math.log(10000.0) * np.arange(half, dtype=np.float32) / np.float32(half)).astype(np.float32)
    angles = (np.arange(MAXPAIR, dtype=np.float32)[:, None] * frequency[None, :]).astype(np.float32)
    table = np.concatenate([np.sin(angles), np.cos(angles)], axis=-1).astype(np.float32)
    pieces, rest = [], table
    for _ in range(3):
        piece = rest.astype(jnp.bfloat16)
        pieces.append(piece)
        rest = rest - piece.astype(np.float32)
    return np.stack(pieces)


def dot_nn(left, right):
    return lax.dot_general(left, right, (((1,), (0,)), ((), ())), preferred_element_type=F32)


def dot_nt(left, right):
    return lax.dot_general(left, right, (((1,), (1,)), ((), ())), preferred_element_type=F32)


def dot_tn(left, right):
    return lax.dot_general(left, right, (((0,), (0,)), ((), ())), preferred_element_type=F32)


def iota(shape, dim):
    return lax.broadcasted_iota(jnp.int32, shape, dim).astype(F32)


def pair_ends(len_row):
    count = len_row.shape[1]
    lengths = jnp.broadcast_to(len_row, (count, count))
    down, across = iota((count, count), 0), iota((count, count), 1)
    ends_col = jnp.sum(jnp.where(across <= down, lengths, 0.0), axis=1, keepdims=True)
    len_col = jnp.sum(jnp.where(across == down, lengths, 0.0), axis=1, keepdims=True)
    ends_row = jnp.sum(jnp.where(down <= across, len_col, 0.0), axis=0, keepdims=True)
    return (ends_row, ends_col)


def pair_col(ends_row, places, total):
    number = jnp.sum(jnp.where(ends_row <= places, 1.0, 0.0), axis=1, keepdims=True)
    return jnp.where((places >= 0.0) & (places < total), number, -1.0)


def pair_row(ends_col, places):
    return jnp.sum(jnp.where(ends_col <= places, 1.0, 0.0), axis=0, keepdims=True)


def with_places(embed, places, ends_row, len_row, table_ref):
    started = jnp.sum(jnp.where(ends_row <= places, len_row, 0.0), axis=1, keepdims=True)
    inside = places - started
    hot = jnp.where(iota((embed.shape[0], MAXPAIR), 1) == inside, 1.0, 0.0).astype(LOW)
    sines = dot_nn(hot, table_ref[0]) + dot_nn(hot, table_ref[1]) + dot_nn(hot, table_ref[2])
    return embed.astype(F32) + sines


def norm_forward(values, gain_row, shift_row):
    centred = values - jnp.mean(values, axis=-1, keepdims=True)
    inverse = lax.rsqrt(jnp.mean(centred * centred, axis=-1, keepdims=True) + 1e-05)
    normed = centred * inverse
    return (normed * gain_row + shift_row, normed, inverse)


def norm_backward(grad_rows, normed, inverse, gain_row):
    scaled = grad_rows * gain_row
    return inverse * (
        scaled
        - jnp.mean(scaled, axis=-1, keepdims=True)
        - normed * jnp.mean(scaled * normed, axis=-1, keepdims=True)
    )


def sigmoid(values):
    return 0.5 * jnp.tanh(0.5 * values) + 0.5


def col_sum(values):
    return jnp.sum(values, axis=0, keepdims=True)


def head_masks(scale):
    lane = lax.broadcasted_iota(jnp.int32, (1, GROUP), 1) // HEAD_DIM
    return [jnp.where(lane == h, scale, 0.0).astype(LOW) for h in range(GROUP // HEAD_DIM)]


def spread(rows, masks):
    return jnp.concatenate([rows * mask for mask in masks], axis=0)


def diagonal(wide):
    count = GROUP // HEAD_DIM
    return [
        wide[h * HEAD_DIM : (h + 1) * HEAD_DIM, h * BLOCK : (h + 1) * BLOCK] for h in range(count)
    ]


def attend_block(query, keys, values, bias, group):
    lanes = slice(group * GROUP, (group + 1) * GROUP)
    stacked = spread(query(lanes), head_masks(HEAD_DIM**-0.5))
    scores = dot_nt(keys(lanes), stacked)
    probs, maxima, sums = [], [], []
    for h in range(GROUP // HEAD_DIM):
        score = scores[:, h * BLOCK : (h + 1) * BLOCK] + bias
        row_max = jnp.max(score, axis=0, keepdims=True)
        exp_score = jnp.exp(score - row_max)
        maxima.append(row_max)
        sums.append(col_sum(exp_score))
        probs.append(exp_score.astype(LOW))
    wide = dot_tn(values(lanes), jnp.concatenate(probs, axis=1))
    return (diagonal(wide), maxima, sums)


def attend_local(rows_ref, count, width, att_ref, lse_ref, rule):
    def body(j, carry):
        first = pl.multiple_of(j * BLOCK, BLOCK)
        queries = pl.ds(pl.multiple_of(first + BLOCK, BLOCK), BLOCK)
        keys = pl.ds(first, width)
        bias = rule(first)
        for group in range(2):
            def part(rows, offset):
                return lambda lanes: rows_ref[rows, offset + lanes.start : offset + lanes.stop]

            outs, maxima, sums = attend_block(
                part(queries, 0), part(keys, 512), part(keys, 1024), bias, group
            )
            mixed = jnp.concatenate([o * (1.0 / s) for o, s in zip(outs, sums)], axis=0)
            att_ref[pl.ds(first, BLOCK), group * GROUP : (group + 1) * GROUP] = mixed.T.astype(
                att_ref.dtype
            )
            lse_ref[j, group : group + 1, :] = jnp.concatenate(
                [m + jnp.log(s) for m, s in zip(maxima, sums)], axis=1
            )
        return carry

    lax.fori_loop(0, count, body, 0)


def attend_back_block(query, grad, keys, values, bias, lse, deltas):
    stacked = spread(query, head_masks(HEAD_DIM**-0.5))
    grads = spread(grad, head_masks(1.0))
    scores = dot_nt(keys, stacked)
    prob_grads = dot_nt(values, grads)
    probs, score_grads = [], []
    for h in range(GROUP // HEAD_DIM):
        cols = slice(h * BLOCK, (h + 1) * BLOCK)
        prob = jnp.exp(scores[:, cols] + bias - lse[:, cols])
        prob_grad = prob_grads[:, cols]
        delta = col_sum(prob * prob_grad) if deltas is None else deltas[h]
        score_grads.append((prob * (prob_grad - delta)).astype(LOW))
        probs.append(prob.astype(LOW))
    prob_wide = jnp.concatenate(probs, axis=1)
    grad_wide = jnp.concatenate(score_grads, axis=1)
    value_grad = dot_nn(prob_wide, grads)
    key_grad = dot_nn(grad_wide, stacked)
    query_grad = jnp.concatenate(diagonal(dot_tn(keys, grad_wide)), axis=0) * HEAD_DIM**-0.5
    return (query_grad, key_grad, value_grad)


def attend_local_back(rows_ref, grad_ref, lse_ref, count, width, query_ref, keyval_ref, rule):
    keyval_ref[...] = jnp.zeros(keyval_ref.shape, F32)

    def body(j, carry):
        first = pl.multiple_of(j * BLOCK, BLOCK)
        queries = pl.ds(pl.multiple_of(first + BLOCK, BLOCK), BLOCK)
        own = pl.ds(first, BLOCK)
        keys = pl.ds(first, width)
        bias = rule(first)
        for group in range(2):
            low, high = group * GROUP, (group + 1) * GROUP
            query_grad, key_grad, value_grad = attend_back_block(
                rows_ref[queries, low:high],
                grad_ref[own, low:high],
                rows_ref[keys, 512 + low : 512 + high],
                rows_ref[keys, 1024 + low : 1024 + high],
                bias,
                lse_ref[j, group : group + 1, :],
                None,
            )
            query_ref[own, low:high] = query_grad.T
            keyval_ref[keys, low:high] += key_grad
            keyval_ref[keys, 512 + low : 512 + high] += value_grad
        return carry

    lax.fori_loop(0, count, body, 0)


def self_rule(ends, start, total, width, causal):
    ends_row, ends_col = ends

    def rule(first):
        shift = (start + first).astype(F32)
        key_places = iota((width, 1), 0) + (shift - BLOCK)
        query_places = iota((1, BLOCK), 1) + shift
        allowed = pair_col(ends_row, key_places, total) == pair_row(ends_col, query_places)
        if causal:
            allowed = allowed & (key_places <= query_places)
        return jnp.where(allowed, 0.0, MASKED)

    return rule


class Loaded:
    def __init__(self, ref):
        self.ref = ref

    def get(self):
        return self.ref


class Coming:
    def __init__(self, far, near, sem):
        self.near = near
        self.copy = pltpu.make_async_copy(far, near, sem)
        self.copy.start()
        self.waiting = True

    def get(self):
        if self.waiting:
            self.copy.wait()
            self.waiting = False
        return self.near


class Leaving:
    def __init__(self, near, far, sem):
        self.ref = near
        self.copy = pltpu.make_async_copy(near, far, sem)
        self.started = False

    def flush(self):
        if not self.started:
            self.copy.start()
            self.started = True

    def finish(self):
        self.flush()
        self.copy.wait()


OVER_SEQ = "seq"


def put_rows(held, result, col):
    devices, rows, _ = held.shape
    cols = pl.ds(col if isinstance(col, int) else pl.multiple_of(col, BLOCK), result.shape[1])
    low = result.astype(LOW)
    for i in range(devices):
        held[i, :, cols] = low[i * rows : (i + 1) * rows, :]


class Blocks:
    def __init__(self, keep, send, held, sems, numbers, order):
        self.keep, self.send, self.held, self.sems = (keep, send, held, sems)
        self.numbers, self.order = (numbers, order)
        self.used = []

    def spread(self, col, width):
        half, bits = (self.keep.shape[0], len(self.order))
        chunk = len(self.used)
        seq, mine = self.numbers[0], self.numbers[1]
        for place in range(2 * half):
            flips = {bit: (place >> (bits - 1 - s)) & 1 for s, bit in enumerate(self.order)}
            source = target = pl.ds(col, width)
            if OVER_SEQ in flips:
                source = pl.ds(pl.multiple_of((seq ^ flips.pop(OVER_SEQ)) * (width // 2), BLOCK), width // 2)
                target = pl.ds(0, width // 2)
            flip = sum(value << bit for bit, value in flips.items())
            refs = self.keep if place < half else self.send
            pltpu.make_async_copy(
                self.held.at[mine ^ flip, :, source],
                refs.at[place % half, :, target],
                self.sems.at[chunk],
            ).start()
        self.used.append(pl.ds(col, width))

    def fill(self, source, col):
        width = source.ref.shape[2]
        self.filling = pltpu.make_async_copy(
            source.ref, self.held.at[:, :, pl.ds(col, width)], self.sems.at[15]
        )
        self.filling.start()

    def filled(self):
        self.filling.wait()

    def put_rows(self, result, col):
        put_rows(self.held, result, col)

    def put_cols(self, result, sums, first, col):
        devices, rows, _ = self.held.shape
        width = result.shape[1] // (result.shape[1] * devices // HIDDEN)
        pieces = BLOCK // width
        low = result.astype(LOW)
        tall = low.shape[0] // pieces
        top = iota((rows, width), 0) == 0.0
        for n in range(result.shape[1] // width):
            at = slice(n * width, (n + 1) * width)
            piece = [low[p * tall : (p + 1) * tall, at] for p in range(pieces)]
            piece = piece[0] if pieces == 1 else jnp.concatenate(piece, axis=1)
            for g in range(tall // rows):
                self.held[first + n, :, col + g * BLOCK : col + (g + 1) * BLOCK] = piece[
                    g * rows : (g + 1) * rows, :
                ]
            row = jnp.where(top, sums[:, at], 0.0).astype(LOW)
            row = row if pieces == 1 else jnp.concatenate([row] * pieces, axis=1)
            end = col + (tall // rows) * BLOCK
            self.held[first + n, :, end : end + BLOCK] = row

    def finish(self):
        for chunk, cols in enumerate(self.used):
            whole = self.held.at[:, :, cols]
            pltpu.make_async_copy(whole, whole, self.sems.at[chunk]).wait()


NEAR, FAR, RAW = "near", "far", "raw"
IN_HBM = pl.BlockSpec(memory_space=pltpu.HBM)
IN_VMEM = pl.BlockSpec(memory_space=pltpu.VMEM)
IN_SMEM = pl.BlockSpec(memory_space=pltpu.SMEM)


LIMITS = {'rows_unpack': 14, 'tail_unpack': 6, 'last_unpack': 8, 'cross_unpack': 4, 'dec_pre': 8, 'enc_pre': 8, 'enc_forward': 18, 'dec_self': 13, 'cross_tail': 27, 'cross_back': 13, 'dec_self_back': 18, 'enc_tail_back': 20, 'enc_self_back': 12, 'dec_input_grad': 10, 'enc_input_grad': 9}
MICROS = {'dec_pre': 30, 'enc_forward': 30, 'dec_self': 30, 'cross_tail': 30, 'cross_back': 30, 'dec_self_back': 30, 'enc_tail_back': 30, 'enc_self_back': 30, 'dec_input_grad': 30, 'enc_input_grad': 30}


def call(kernel, name, scalars, operands, outs, scratch=(), blocks=(), order=(), ahead=()):
    arrays, specs = [], []
    for array, mode, *_ in (*operands, *ahead):
        near = mode == NEAR
        arrays.append(pltpu.with_memory_space_constraint(array, pltpu.VMEM if near else pltpu.HBM))
        specs.append(IN_VMEM if near else IN_HBM)

    def taken(array, mode, start=None, size=None):
        return array.shape if size is None else (size, *array.shape[1:])

    shapes, out_specs = [], []
    for shape, dtype, mode in outs:
        shapes.append((pltpu.VMEM if mode == NEAR else pltpu.HBM)(shape, dtype))
        out_specs.append(IN_VMEM if mode == NEAR else IN_HBM)
    over_seq = OVER_SEQ in order
    devices = 1 << (len(order) - over_seq)
    share = FEATURES // devices
    for columns in blocks:
        shapes += [pltpu.HBM(((1 << len(order)) // 2, share, columns // (1 + over_seq)), LOW)] * 2
        out_specs += [IN_HBM] * 2
    for one in ahead:
        shapes.append(pltpu.VMEM(taken(*one), one[0].dtype))
        out_specs.append(IN_VMEM)
    far_in = [i for i, one in enumerate(operands) if one[1] == FAR]
    far_out = [i for i, one in enumerate(outs) if one[2] == FAR]
    extra = [pltpu.VMEM(*one) if isinstance(one, tuple) else one for one in scratch]
    extra += [pltpu.VMEM(taken(*operands[i]), operands[i][0].dtype) for i in far_in]
    extra += [pltpu.VMEM(outs[i][0], outs[i][1]) for i in far_out]
    extra += [pltpu.VMEM((devices, share, columns), LOW) for columns in blocks]
    extra += [pltpu.SemaphoreType.DMA((len(far_in) + len(far_out) + len(ahead) + 1,))]
    extra += [pltpu.SemaphoreType.DMA((16,)) for _ in blocks]

    def body(*refs):
        refs = list(refs)
        take = lambda n: [refs.pop(0) for _ in range(n)]
        numbers = take(len(scalars))
        ins = take(len(operands))
        sources = take(len(ahead))
        results = take(len(outs))
        sends = [take(2) for _ in blocks]
        copies = take(len(ahead))
        temps = take(len(scratch))
        near_in = take(len(far_in))
        near_out = take(len(far_out))
        helds = take(len(blocks))
        sems = take(1)[0]
        block_sems = take(len(blocks))
        used = iter(range(len(far_in) + len(far_out) + len(ahead)))

        def coming(ref, near, array, mode, start=None, size=None):
            source = ref if size is None else ref.at[pl.ds(start(numbers[0]), size)]
            return Coming(source, near, sems.at[next(used)])

        given = [Loaded(ref) for ref in ins]
        for n, i in enumerate(far_in):
            given[i] = coming(ins[i], near_in[n], *operands[i])
        later = [coming(ref, near, *one) for ref, near, one in zip(sources, copies, ahead)]
        leaving = {}
        for n, i in enumerate(far_out):
            leaving[i] = Leaving(near_out[n], results[i], sems.at[next(used)])
        made = [leaving.get(i, Loaded(results[i])) for i in range(len(outs))]
        moved = [
            Blocks(keep, send, held, sem, numbers[0], order)
            for (keep, send), held, sem in zip(sends, helds, block_sems)
        ]
        kernel(numbers, given, made, temps, *moved)
        for one in leaving.values():
            one.flush()
        for one in (*given, *later):
            one.get()
        for one in leaving.values():
            one.finish()
        for one in moved:
            one.finish()

    results = pl.pallas_call(
        body,
        name=name,
        out_shape=shapes,
        in_specs=[IN_SMEM] * len(scalars) + specs,
        out_specs=out_specs,
        scratch_shapes=extra,
        cost_estimate=pl.CostEstimate(flops=int(MICROS.get(name, 1.0) * 1.0 * 1.15e9), bytes_accessed=1, transcendentals=0),
        compiler_params=pltpu.CompilerParams(vmem_limit_bytes=LIMITS[name] * 1024 * 1024),
    )(*scalars, *arrays)
    made = len(outs) + 2 * len(blocks)
    return (results[: len(outs)], results[len(outs) : made], results[made:])


def input_rows(halos, own, table, w_in, biases, x_ref, low_ref, rows_ref, start, count, ends, len_row, shift=0):
    def chunk(embed, target, size):
        places = iota((size, 1), 0) + (start + target - BLOCK).astype(F32)
        x = with_places(embed, places, ends[0], len_row, table)
        low = x.astype(LOW)
        for c in range(3):
            part = dot_nn(low, w_in[:, c * 512 : (c + 1) * 512])
            if c != 1:
                part = part + biases[c // 2 : c // 2 + 1, :]
            rows_ref[pl.ds(target - shift, size), c * 512 : (c + 1) * 512] = part.astype(LOW)
        return (x, low)

    size = min(256, count)

    def body(step, carry):
        at = pl.multiple_of(step * size, size)
        rows = pl.ds(at, size)
        x_ref[rows, :], low_ref[rows, :] = chunk(own[rows, :], pl.multiple_of(at + BLOCK, BLOCK), size)
        return carry

    if own is not None:
        lax.fori_loop(0, count // size, body, 0)
    for embed, target in halos:
        chunk(embed[...], target, BLOCK)


def enc_pre_kernel(numbers, ins, outs, temps):
    own, lens, table, w_in, biases = [i.get() for i in ins]
    x_out, low_out, rows_out = [o.ref for o in outs]
    count = own.shape[0]
    len_row = lens[...].astype(F32)
    input_rows(
        [], own, table, w_in, biases, x_out, low_out, rows_out, numbers[0][0] * count, count, pair_ends(len_row), len_row,
        BLOCK,
    )


def enc_kernel(numbers, ins, outs, temps, total):
    left, right, x_ref, own_rows, lens, table, w_in, gains, biases, upbias, w_out, w_up, w_down = ins
    rows_out, lse_out, hid_out, mid_out, mid_inv_out, fin_out, fin_inv_out, encoded_out = outs
    x_ref = x_ref.get()
    count = x_ref.shape[0]
    start = numbers[0][0] * count
    len_row = lens.get()[...].astype(F32)
    ends = pair_ends(len_row)
    size = min(256, count)
    left, right, table, w_in, gains, biases, upbias = [
        i.get() for i in (left, right, table, w_in, gains, biases, upbias)
    ]
    rows_out.ref[BLOCK : BLOCK + count, :] = own_rows.get()[...]
    input_rows(
        [(left, 0), (right, BLOCK + count)], None, table, w_in, biases, None, None, rows_out.ref, start, count, ends,
        len_row,
    )
    rows_out.flush()
    width = 3 * BLOCK
    attend_local(
        rows_out.ref, count // BLOCK, width, hid_out.ref, lse_out.ref,
        self_rule(ends, start, total, width, False),
    )
    lse_out.flush()
    hid_out.flush()
    w_out, w_up, w_down = w_out.get(), w_up.get(), w_down.get()
    hid, mid_ref, mid_inv, fin_ref, fin_inv, encoded = [
        o.ref for o in (hid_out, mid_out, mid_inv_out, fin_out, fin_inv_out, encoded_out)
    ]

    def dense(step, carry):
        rows = pl.ds(pl.multiple_of(step * size, size), size)
        z = x_ref[rows, :] + dot_nn(hid[rows, :], w_out[...]) + biases[2:3, :]
        mid, normed, inverse = norm_forward(z, gains[0:1, :], biases[3:4, :])
        mid_ref[rows, :] = normed
        mid_inv[rows, :] = inverse
        low = mid.astype(LOW)
        z = mid + biases[4:5, :]
        for c in range(0, w_up.shape[1], 512):
            up = dot_nn(low, w_up[:, c : c + 512]) + upbias[:, c : c + 512]
            active = (up * sigmoid(up)).astype(LOW)
            z = z + dot_nn(active, w_down[c : c + 512, :])
        final, normed, inverse = norm_forward(z, gains[1:2, :], biases[5:6, :])
        fin_ref[rows, :] = normed
        fin_inv[rows, :] = inverse
        encoded[rows, :] = final.astype(LOW)
        return carry

    lax.fori_loop(0, count // size, dense, 0)


def dec_self_kernel(numbers, ins, outs, temps, total):
    halo, own, lens, table, w_in, gains, biases, w_out, w_query = [i.get() for i in ins[:9]]
    low_out, rows_out, lse_out, hid_out, normed_out, inv_out, query_out, keyval_out = outs
    (x,) = temps
    rows_in = rows_out.ref
    count = x.shape[0]
    start = numbers[0][0] * count
    len_row = lens[...].astype(F32)
    ends = pair_ends(len_row)
    input_rows([(halo, 0)], own, table, w_in, biases, x, low_out.ref, rows_in, start, count, ends, len_row)
    low_out.flush()
    rows_out.flush()
    width = 2 * BLOCK
    attend_local(
        rows_in, count // BLOCK, width, hid_out.ref, lse_out.ref,
        self_rule(ends, start, total, width, True),
    )
    size = min(256, count)
    hid, normed_ref, inv_ref, query_ref = [o.ref for o in (hid_out, normed_out, inv_out, query_out)]

    def dense(step, carry):
        rows = pl.ds(pl.multiple_of(step * size, size), size)
        z = x[rows, :] + dot_nn(hid[rows, :], w_out[...]) + biases[2:3, :]
        mid, normed, inverse = norm_forward(z, gains[0:1, :], biases[3:4, :])
        normed_ref[rows, :] = normed
        inv_ref[rows, :] = inverse
        query = dot_nn(mid.astype(LOW), w_query[...]) + biases[4:5, :]
        query_ref[rows, :] = query.astype(LOW)
        return carry

    lax.fori_loop(0, count // size, dense, 0)
    for out in (normed_out, inv_out, query_out):
        out.flush()
    project(ins[9].get(), ins[10].get(), biases, keyval_out.ref, 0, count)


def project(source, w, biases, keyval_out, base, length):
    size = min(256, length)

    def body(step, carry):
        at = pl.multiple_of(step * size, size)
        rows = pl.ds(pl.multiple_of(base + at, BLOCK), size)
        values = source[pl.ds(at, size), :]
        keyval_out[rows, :512] = dot_nn(values, w[:, :512]).astype(LOW)
        keyval_out[rows, 512:] = (dot_nn(values, w[:, 512:]) + biases[5:6, :]).astype(LOW)
        return carry

    lax.fori_loop(0, length // size, body, 0)


def cross_span(src_lens, tgt_lens, first):
    def step(k, carry):
        begin, low, high = carry
        end = begin + tgt_lens[0, k]
        length = src_lens[0, k]
        low = low + jnp.where(end <= first, length, 0)
        high = high + jnp.where(begin <= first + (BLOCK - 1), length, 0)
        return (end, low, high)

    zero = jnp.int32(0)
    _, low, high = lax.fori_loop(0, src_lens.shape[1], step, (zero, zero, zero), unroll=True)
    low = (low // 16) * 16
    return (low, (high - low + (WINDOW - 1)) // WINDOW)


def cross_rule(src_ends_row, tgt_ends_col, first, begin, total):
    key_places = iota((WINDOW, 1), 0) + begin.astype(F32)
    query_places = iota((1, BLOCK), 1) + first.astype(F32)
    allowed = pair_col(src_ends_row, key_places, total) == pair_row(tgt_ends_col, query_places)
    return jnp.where(allowed, 0.0, MASKED)


def cross_forward(
    numbers, query, memory, others, own_keyval, src_vec, tgt_vec, biases, w, att_out, lse_out, keyval_out, memory_out,
    max_ref, sum_ref, acc_ref, copy_sem, total,
):
    idx, src_lens, tgt_lens = numbers
    count = query.shape[0]
    length = memory.shape[0]
    shards = others.shape[0] + 1
    start = idx[0] * count
    src_ends_row, _ = pair_ends(src_vec[...].astype(F32))
    _, tgt_ends_col = pair_ends(tgt_vec[...].astype(F32))
    own_rows = pl.ds(pl.multiple_of(idx[0] * length, BLOCK), length)
    own_copy = pltpu.make_async_copy(own_keyval, keyval_out.at[own_rows], copy_sem.at[0])
    own_copy.start()
    for s in range(shards):
        base = lax.rem(idx[0] + s, shards) * length
        memory_out[pl.ds(pl.multiple_of(base, BLOCK), length), :] = memory[...] if s == 0 else others[s - 1]
        if s:
            project(others.at[s - 1], w, biases, keyval_out, base, length)
    own_copy.wait()
    keyval_out[total:, :] = jnp.zeros((WINDOW, 1024), LOW)

    def body(j, carry):
        at = pl.multiple_of(j * BLOCK, BLOCK)
        rows = pl.ds(at, BLOCK)
        first = start + at
        low, windows = cross_span(src_lens, tgt_lens, first)
        max_ref[...] = jnp.full(max_ref.shape, MASKED, F32)
        sum_ref[...] = jnp.zeros(sum_ref.shape, F32)
        acc_ref[...] = jnp.zeros(acc_ref.shape, F32)

        def window(n, carry):
            begin = pl.multiple_of(low + n * WINDOW, 16)
            keys = pl.ds(begin, WINDOW)
            bias = cross_rule(src_ends_row, tgt_ends_col, first, begin, total)
            for group in range(2):
                def part(ref, rows, offset):
                    return lambda lanes: ref[rows, offset + lanes.start : offset + lanes.stop]

                outs, maxima, sums = attend_block(
                    part(query, rows, 0), part(keyval_out, keys, 0), part(keyval_out, keys, 512), bias, group
                )
                for h in range(4):
                    head = group * 4 + h
                    old = max_ref[head : head + 1, :]
                    new = jnp.maximum(old, maxima[h])
                    before, now = jnp.exp(old - new), jnp.exp(maxima[h] - new)
                    max_ref[head : head + 1, :] = new
                    sum_ref[head : head + 1, :] = sum_ref[head : head + 1, :] * before + sums[h] * now
                    part_rows = slice(head * HEAD_DIM, (head + 1) * HEAD_DIM)
                    acc_ref[part_rows, :] = acc_ref[part_rows, :] * before + outs[h] * now
            return carry

        lax.fori_loop(0, windows, window, 0)
        for group in range(2):
            heads = range(group * 4, group * 4 + 4)
            mixed = jnp.concatenate(
                [
                    acc_ref[h * HEAD_DIM : (h + 1) * HEAD_DIM, :] * (1.0 / sum_ref[h : h + 1, :])
                    for h in heads
                ],
                axis=0,
            )
            att_out[rows, group * GROUP : (group + 1) * GROUP] = mixed.T
            lse_out[j, group : group + 1, :] = jnp.concatenate(
                [max_ref[h : h + 1, :] + jnp.log(sum_ref[h : h + 1, :]) for h in heads], axis=1
            )
        return carry

    lax.fori_loop(0, count // BLOCK, body, 0)


def feed_forward_grads(mid, up_low, ffn, active, hid, branch, sums, blocks):
    hidden = up_low.shape[1]
    devices, rows, _ = blocks.held.shape
    width = hidden // devices
    down = hidden + BLOCK

    def down_part(c, carry):
        cols = pl.ds(pl.multiple_of(c * 512, 512), 512)
        blocks.put_cols(dot_tn(ffn[...], active[:, cols]), sums[pl.ds(8 + c, 1), :], c * (512 // width), 0)
        return carry

    def up_part(c, carry):
        cols = pl.ds(pl.multiple_of(c * 512, 512), 512)
        blocks.put_rows(dot_tn(mid[...], up_low[:, cols]), down + c * 512)
        return carry

    lax.fori_loop(0, hidden // 512, down_part, 0)
    blocks.spread(0, down)
    lax.fori_loop(0, hidden // 512, up_part, 0)
    blocks.spread(down, hidden)
    blocks.put_rows(dot_tn(hid[...], branch[...]), down + hidden)
    blocks.spread(down + hidden, 512)


def cross_tail_kernel(numbers, ins, outs, temps, blocks, total):
    (query, memory, others, own_keyval, src_vec, tgt_vec, gains, biases, upbias, w_keyval, normed_in, cot, w_out, w_up,
     w_down) = [i.get() for i in ins]
    att, lse_out, keyval_out, memory_out, decoded_out, att_grad_out, branch_out, sums_out = [o.ref for o in outs]
    hid_ref, branch_ref, mid_ref, up_ref, active_ref, ffn_ref, up_low_ref, *running = temps
    cross_forward(
        numbers, query, memory, others, own_keyval, src_vec, tgt_vec, biases, w_keyval, att, lse_out, keyval_out,
        memory_out, *running, total,
    )
    count = att.shape[0]
    hidden = w_up.shape[1]
    sums_out[...] = jnp.zeros(sums_out.shape, F32)
    size = min(256, count)

    def dense(step, carry):
        rows = pl.ds(pl.multiple_of(step * size, size), size)
        hid = att[rows, :].astype(LOW)
        hid_ref[rows, :] = hid
        first = normed_in[rows, :] * gains[0:1, :] + biases[3:4, :]
        z = first + dot_nn(hid, w_out[...]) + biases[6:7, :]
        mid, normed, inverse = norm_forward(z, gains[1:2, :], biases[7:8, :])
        low = mid.astype(LOW)
        mid_ref[rows, :] = low
        z = mid + biases[8:9, :]
        for c in range(0, hidden, 512):
            up = dot_nn(low, w_up[:, c : c + 512]) + upbias[:, c : c + 512]
            gate = sigmoid(up)
            active = up * gate
            up_ref[:, c : c + 512] = gate + active * (1.0 - gate)
            active = active.astype(LOW)
            active_ref[rows, c : c + 512] = active
            z = z + dot_nn(active, w_down[c : c + 512, :])
        final, normed_final, inverse_final = norm_forward(z, gains[2:3, :], biases[9:10, :])
        decoded_out[rows, :] = final.astype(LOW)
        grad = cot[rows, :].astype(F32)
        ffn = norm_backward(grad, normed_final, inverse_final, gains[2:3, :])
        ffn_low = ffn.astype(LOW)
        ffn_ref[rows, :] = ffn_low
        mid_grad = ffn
        for c in range(0, hidden, 512):
            up_grad = dot_nt(ffn_low, w_down[c : c + 512, :]) * up_ref[:, c : c + 512]
            sums_out[8 + c // 512 : 9 + c // 512, :] += col_sum(up_grad)
            up_low = up_grad.astype(LOW)
            up_low_ref[rows, c : c + 512] = up_low
            mid_grad = mid_grad + dot_nt(up_low, w_up[:, c : c + 512])
        branch = norm_backward(mid_grad, normed, inverse, gains[1:2, :])
        branch_low = branch.astype(LOW)
        branch_out[rows, :] = branch
        branch_ref[rows, :] = branch_low
        att_grad_out[rows, :] = dot_nt(branch_low, w_out[...]).astype(LOW)
        sums_out[0:1, :] += col_sum(mid_grad * normed)
        sums_out[1:2, :] += col_sum(grad * normed_final)
        sums_out[2:3, :] += col_sum(branch)
        sums_out[3:4, :] += col_sum(mid_grad)
        sums_out[4:5, :] += col_sum(ffn)
        sums_out[5:6, :] += col_sum(grad)
        return carry

    lax.fori_loop(0, count // size, dense, 0)
    for out in (outs[0], outs[3], outs[4], outs[6]):
        out.flush()
    feed_forward_grads(
        mid_ref, up_low_ref, ffn_ref, active_ref, hid_ref, branch_ref, sums_out, blocks
    )


def cross_back_kernel(numbers, ins, outs, temps, total):
    idx, src_lens, tgt_lens = numbers
    query, keyval, att, att_grad, lse, src_vec, tgt_vec = [i.get() for i in ins[:7]]
    mem_own_out, mem_out, query_out, keyval_low, sums_out = [o.ref for o in outs]
    (keyval_ref,) = temps
    count = query.shape[0]
    start = idx[0] * count
    src_ends_row, _ = pair_ends(src_vec[...].astype(F32))
    _, tgt_ends_col = pair_ends(tgt_vec[...].astype(F32))
    keyval_ref[...] = jnp.zeros(keyval_ref.shape, F32)
    query_out[...] = jnp.zeros(query_out.shape, F32)
    sums_out[...] = jnp.zeros(sums_out.shape, F32)
    select = jnp.where(
        lax.broadcasted_iota(jnp.int32, (HEADS, 512), 1) // HEAD_DIM
        == lax.broadcasted_iota(jnp.int32, (HEADS, 512), 0),
        1.0,
        0.0,
    )

    def body(j, carry):
        at = pl.multiple_of(j * BLOCK, BLOCK)
        rows = pl.ds(at, BLOCK)
        first = start + at
        low, windows = cross_span(src_lens, tgt_lens, first)
        weighed = att[rows, :] * att_grad[rows, :].astype(F32)
        deltas = lax.dot_general(
            select, weighed, (((1,), (1,)), ((), ())),
            precision=lax.Precision.HIGHEST, preferred_element_type=F32,
        )

        def window(n, carry):
            begin = pl.multiple_of(low + n * WINDOW, 16)
            keys = pl.ds(begin, WINDOW)
            bias = cross_rule(src_ends_row, tgt_ends_col, first, begin, total)
            for group in range(2):
                lo, hi = group * GROUP, (group + 1) * GROUP
                query_grad, key_grad, value_grad = attend_back_block(
                    query[rows, lo:hi],
                    att_grad[rows, lo:hi],
                    keyval[keys, lo:hi],
                    keyval[keys, 512 + lo : 512 + hi],
                    bias,
                    lse[j, group : group + 1, :],
                    [deltas[group * 4 + h : group * 4 + h + 1, :] for h in range(4)],
                )
                query_out[rows, lo:hi] += query_grad.T
                keyval_ref[keys, lo:hi] += key_grad
                keyval_ref[keys, 512 + lo : 512 + hi] += value_grad
            return carry

        lax.fori_loop(0, windows, window, 0)
        return carry

    lax.fori_loop(0, count // BLOCK, body, 0)
    size = min(256, total)
    shards = mem_out.shape[0] + 1
    length = total // shards

    def to_memory(step, carry):
        rows = pl.ds(pl.multiple_of(step * size, size), size)
        grads = keyval_ref[rows, :]
        sums_out[0:1, :] += col_sum(grads[:, 512:])
        keyval_low[rows, :] = grads.astype(LOW)
        return carry

    lax.fori_loop(0, total // size, to_memory, 0)
    w_keyval = ins[7].get()
    for s in reversed(range(shards)):
        base = pl.multiple_of(lax.rem(idx[0] + s, shards) * length, BLOCK)
        grads = dot_nt(keyval_low[pl.ds(base, length), :], w_keyval[...])
        if s == 0:
            mem_own_out[...] = grads
        else:
            mem_out[s - 1] = grads.astype(LOW)


def dec_self_back_kernel(numbers, ins, outs, temps, total):
    query_grads, keyval_low, memory, normed_in, inv_in, branch_in, hid_in, gains, biases, w_query, w_out = [
        i.get() for i in ins[:11]
    ]
    branch_out, sums_out = [o.ref for o in outs[:2]]
    branch_ref, query_low, mid_ref, att_grad_out = temps[:4]
    count = query_grads.shape[0]
    sums_out[...] = jnp.zeros(sums_out.shape, F32)
    size = min(256, count)

    def dense(step, carry):
        rows = pl.ds(pl.multiple_of(step * size, size), size)
        query_grad = query_grads[rows, :]
        low = query_grad.astype(LOW)
        query_low[rows, :] = low
        normed = normed_in[rows, :]
        mid_ref[rows, :] = (normed * gains[0:1, :] + biases[3:4, :]).astype(LOW)
        mid_grad = branch_in[rows, :] + dot_nt(low, w_query[...])
        branch = norm_backward(mid_grad, normed, inv_in[rows, :], gains[0:1, :])
        branch_low = branch.astype(LOW)
        branch_out[rows, :] = branch
        branch_ref[rows, :] = branch_low
        att_grad_out[rows, :] = dot_nt(branch_low, w_out[...]).astype(LOW)
        sums_out[0:1, :] += col_sum(mid_grad * normed)
        sums_out[1:2, :] += col_sum(branch)
        sums_out[2:3, :] += col_sum(mid_grad)
        sums_out[3:4, :] += col_sum(query_grad)
        return carry

    lax.fori_loop(0, count // size, dense, 0)
    outs[0].flush()
    held = outs[2].ref

    def keyval_part(c, carry):
        cols = pl.ds(pl.multiple_of(c * 512, 512), 512)
        put_rows(held, dot_tn(memory[...], keyval_low[:, cols]), c * 512)
        return carry

    lax.fori_loop(0, 2, keyval_part, 0)
    put_rows(held, dot_tn(mid_ref[...], query_low[...]), 1024)
    put_rows(held, dot_tn(hid_in[...], branch_ref[...]), 1536)
    outs[2].flush()
    self_back(numbers, Loaded(att_grad_out), *ins[11:], outs[3:], *temps[4:], total, True)


def enc_self_back_kernel(numbers, ins, outs, temps, total):
    self_back(numbers, *ins, outs, *temps, total, False)


def self_back(numbers, att_grad, lse, lens, rows_in, outs, query_ref, keyval_ref, total, causal):
    own_out, halos = outs[0].ref, [o.ref for o in outs[1:]]
    rows_in, att_grad, lse = rows_in.get(), att_grad.get(), lse.get()
    count = att_grad.shape[0]
    ends = pair_ends(lens.get()[...].astype(F32))
    width = (2 if causal else 3) * BLOCK
    attend_local_back(
        rows_in, att_grad, lse, count // BLOCK, width, query_ref, keyval_ref,
        self_rule(ends, numbers[0][0] * count, total, width, causal),
    )
    if causal:
        halos[0][...] = keyval_ref[:BLOCK, :].astype(LOW)
    elif len(halos) == 1:
        edge = pl.multiple_of((1 - numbers[0][0]) * (BLOCK + count), BLOCK)
        halos[0][...] = keyval_ref[pl.ds(edge, BLOCK), :].astype(LOW)
    else:
        halos[0][...] = keyval_ref[:BLOCK, :].astype(LOW)
        halos[1][...] = keyval_ref[BLOCK + count :, :].astype(LOW)
    for out in outs[1:]:
        out.flush()
    own_out[:, :512] = query_ref[...]
    own_out[:, 512:] = keyval_ref[BLOCK : BLOCK + count, :]


def input_grad(own, edges, low_in, branch, w, grad_out, sums_out, low_ref, put, count):
    sums_out[...] = jnp.zeros(sums_out.shape, F32)
    size = min(256, count)

    def dense(step, carry):
        rows = pl.ds(pl.multiple_of(step * size, size), size)
        grads = own[rows, :]
        sums_out[0:1, :] += col_sum(grads[:, :512])
        sums_out[1:2, :] += col_sum(grads[:, 1024:])
        low_ref[rows, :] = grads.astype(LOW)
        return carry

    lax.fori_loop(0, count // size, dense, 0)
    returned = jnp.zeros((count, 1024), F32) if len(edges) > 1 and count == BLOCK else None
    for at, halo in edges:
        edge = pl.ds(at, BLOCK)
        grads = halo[...].astype(F32)
        sums_out[1:2, :] += col_sum(grads[:, 512:])
        if returned is not None:
            returned = grads = returned + grads
        low_ref[edge, 512:] = (own[edge, 512:] + grads).astype(LOW)

    def weight_part(c, carry):
        cols = pl.ds(pl.multiple_of(c * 512, 512), 512)
        put(dot_tn(low_in[...], low_ref[:, cols]), c * 512)
        return carry

    lax.fori_loop(0, 3, weight_part, 0)

    def back():
        def dense_grad(step, carry):
            rows = pl.ds(pl.multiple_of(step * size, size), size)
            grad_out[rows, :] = (branch[rows, :] + dot_nt(low_ref[rows, :], w[...])).astype(grad_out.dtype)
            return carry

        lax.fori_loop(0, count // size, dense_grad, 0)

    return back


def dec_input_grad_kernel(numbers, ins, outs, temps, blocks):
    blocks.fill(ins[-1], 1536)
    halo, own, branch, low_in, w = [i.get() for i in ins[:-1]]
    grad_out, sums_out = [o.ref for o in outs]
    (low_ref,) = temps
    count = own.shape[0]
    back = input_grad(
        own, [(count - BLOCK, halo)], low_in, branch, w, grad_out, sums_out, low_ref, blocks.put_rows, count
    )
    blocks.filled()
    blocks.spread(0, blocks.held.shape[2])
    back()


def enc_input_grad_kernel(numbers, ins, outs, temps, blocks, halo_count):
    halos = [i.get() for i in ins[:halo_count]]
    own, branch, low_in, w, *sums = [i.get() for i in ins[halo_count:]]
    (grad_out,) = [o.ref for o in outs]
    low_ref, sums_ref, small_ref = temps
    count = own.shape[0]
    if halo_count == 1:
        edges = [(pl.multiple_of((1 - numbers[0][0]) * (count - BLOCK), BLOCK), halos[0])]
    else:
        edges = [(0, halos[0]), (count - BLOCK, halos[1])]
    back = input_grad(own, edges, low_in, branch, w, grad_out, sums_ref, low_ref, blocks.put_rows, count)
    small_ref[...] = jnp.zeros(small_ref.shape, F32)
    for n, part in enumerate((*sums, sums_ref)):
        small_ref[n * 8 : (n + 1) * 8, :] = part[:8, :]
    blocks.put_rows(small_ref[...].T, 1536)
    blocks.spread(0, 1536 + BLOCK)
    back()


def enc_tail_back_kernel(numbers, ins, outs, temps, blocks):
    (mem_own, mem_others, cot, fin_in, fin_inv, mid_in, mid_inv, hid_in, gains, biases, upbias, w_down, w_up,
     w_out) = [i.get() for i in ins]
    branch_out, att_grad_out, sums_out = [o.ref for o in outs]
    branch_ref, mid_ref, active_ref, ffn_ref, up_low_ref = temps
    count = cot.shape[0]
    hidden = w_up.shape[1]
    sums_out[...] = jnp.zeros(sums_out.shape, F32)
    size = min(256, count)

    def dense(step, carry):
        rows = pl.ds(pl.multiple_of(step * size, size), size)
        grad = cot[rows, :].astype(F32) + mem_own[rows, :]
        for s in range(mem_others.shape[0]):
            grad = grad + mem_others[s, rows, :].astype(F32)
        normed_final = fin_in[rows, :]
        ffn = norm_backward(grad, normed_final, fin_inv[rows, :], gains[1:2, :])
        ffn_low = ffn.astype(LOW)
        ffn_ref[rows, :] = ffn_low
        normed = mid_in[rows, :]
        low = (normed * gains[0:1, :] + biases[3:4, :]).astype(LOW)
        mid_ref[rows, :] = low
        mid_grad = ffn
        for c in range(0, hidden, 512):
            up = dot_nn(low, w_up[:, c : c + 512]) + upbias[:, c : c + 512]
            gate = sigmoid(up)
            active = up * gate
            active_ref[rows, c : c + 512] = active.astype(LOW)
            up_grad = dot_nt(ffn_low, w_down[c : c + 512, :]) * (gate + active * (1.0 - gate))
            sums_out[8 + c // 512 : 9 + c // 512, :] += col_sum(up_grad)
            up_low = up_grad.astype(LOW)
            up_low_ref[rows, c : c + 512] = up_low
            mid_grad = mid_grad + dot_nt(up_low, w_up[:, c : c + 512])
        branch = norm_backward(mid_grad, normed, mid_inv[rows, :], gains[0:1, :])
        branch_low = branch.astype(LOW)
        branch_out[rows, :] = branch
        branch_ref[rows, :] = branch_low
        att_grad_out[rows, :] = dot_nt(branch_low, w_out[...]).astype(LOW)
        sums_out[0:1, :] += col_sum(mid_grad * normed)
        sums_out[1:2, :] += col_sum(grad * normed_final)
        sums_out[2:3, :] += col_sum(branch)
        sums_out[3:4, :] += col_sum(mid_grad)
        sums_out[4:5, :] += col_sum(ffn)
        sums_out[5:6, :] += col_sum(grad)
        return carry

    lax.fori_loop(0, count // size, dense, 0)
    outs[0].flush()
    feed_forward_grads(
        mid_ref, up_low_ref, ffn_ref, active_ref, hid_in, branch_ref, sums_out, blocks
    )


def log2(number):
    bits = number.bit_length() - 1
    assert number == 1 << bits
    return bits


def swapped(value, axis, bit, devices):
    return lax.ppermute(value, axis, [(i, i ^ (1 << bit)) for i in range(devices)])


class Chain:
    def __init__(self, token):
        self.token = token

    def tie(self, *values):
        self.token, *values = lax.optimization_barrier((self.token, *values))
        return values[0] if len(values) == 1 else values


class Reduction:
    def __init__(self, chain, arrays, order, devices, seq_count):
        self.chain, self.order, self.devices, self.seq_count = (chain, order, devices, seq_count)
        self.keep, send = arrays
        self.size = self.keep.shape[0]
        self.received, self.low, self.others = [], None, []
        self.push(send)

    def push(self, send):
        bit = self.order[len(self.received)]
        if bit == OVER_SEQ:
            self.received.append(swapped(send, "seq", 0, self.seq_count))
        else:
            self.received.append(swapped(send, "dp", bit, self.devices))

    def part(self, first, last):
        total = self.keep[first:last].astype(F32)
        for piece in self.received:
            total = total + piece[first:last].astype(F32)
        return total

    def next(self):
        self.received[-1] = self.chain.tie(self.received[-1])
        if len(self.received) < len(self.order):
            half = self.size // 2
            self.push(self.chain.tie(self.part(half, self.size).astype(LOW)))
            self.size = half
            return
        self.low = self.chain.tie(self.part(0, 1)[0].astype(LOW))
        if log2(self.seq_count):
            self.others.append(swapped(self.low, "seq", 0, self.seq_count))

    def pair(self):
        while self.low is None:
            self.next()
        low, other = self.low, self.others[0]
        if OVER_SEQ not in self.order:
            for bit in range(1, log2(self.seq_count)):
                low = lax.optimization_barrier((low.astype(F32) + other.astype(F32)).astype(LOW))
                other = swapped(low, "seq", bit, self.seq_count)
        return (low, other)


def from_shards(own, count):
    return jnp.stack(
        [lax.ppermute(own, "seq", [((i + s) % count, i) for i in range(count)]) for s in range(1, count)]
    )


def feed_forward_unpack(numbers, ins, outs, temps):
    low, other = [i.get() for i in ins]
    up_out, matrix_out, down_out, bias_out = [o.ref for o in outs]
    (total,) = temps
    total[...] = low[...].astype(F32) + other[...].astype(F32)
    share = up_out.shape[0]
    width = down_out.shape[0]
    pieces = BLOCK // width
    groups = FEATURES // pieces // share
    tall = jnp.concatenate([total[:, g * BLOCK : (g + 1) * BLOCK] for g in range(groups)], axis=0).T
    for p in range(pieces):
        rows = FEATURES // pieces
        down_out[:, p * rows : (p + 1) * rows] = tall[p * width : (p + 1) * width, :]
    end = groups * BLOCK
    bias_out[...] = total[0:1, end : end + width]
    up_out[...] = total[:, HIDDEN + BLOCK : 2 * HIDDEN + BLOCK]
    matrix_out[...] = total[:, 2 * HIDDEN + BLOCK :]


def decoder_unpack(numbers, ins, outs, temps, halved):
    low, other = [i.get() for i in ins]
    (total,) = temps
    if halved:
        width = low.shape[1]
        seq = numbers[0][0]
        total[:, pl.ds(pl.multiple_of(seq * width, BLOCK), width)] = low[...].astype(F32)
        total[:, pl.ds(pl.multiple_of((1 - seq) * width, BLOCK), width)] = other[...].astype(F32)
    else:
        total[...] = low[...].astype(F32) + other[...].astype(F32)
    at = 0
    for out in outs:
        width = out.ref.shape[1]
        out.ref[...] = total[:, at : at + width]
        at += width


def encoder_unpack(numbers, ins, outs, temps, picks):
    low, other = [i.get() for i in ins]
    total = low[...].astype(F32) + other[...].astype(F32)
    outs[0].ref[...] = total[:, :1536]
    small = total[:, 1536:].T
    for out, rows in zip(outs[1:], picks):
        for n, row in enumerate(rows):
            out.ref[n : n + 1, :] = small[row : row + 1, :]


def encoders_unpack(numbers, ins, outs, temps, picks):
    feed_forward_unpack(numbers, ins[:2], outs[:4], temps[:1])
    for out in outs[:4]:
        out.flush()
    encoder_unpack(numbers, ins[2:4], outs[4:9], (), picks)


def rows_unpack(numbers, ins, outs, temps):
    shards = numbers[0]
    for n, out in enumerate(outs):
        own, others = ins[2 * n].get(), ins[2 * n + 1].get()
        count = own.shape[0]
        parts = others.shape[0] + 1
        for s in range(parts):
            at = pl.ds(pl.multiple_of(lax.rem(shards[0] + s, parts) * count, BLOCK), count)
            out.ref[at, :] = (own[...] if s == 0 else others[s - 1]).astype(out.ref.dtype)
        out.flush()


def local(
    src_embed, tgt_embed, src_lengths, tgt_lengths, enc_cotangent, dec_cotangent,
    enc_inproj, enc_outproj, enc_upproj, enc_downproj, enc_gains, enc_biases, enc_upbias,
    dec_inproj, dec_outproj, cross_query, cross_keyval, cross_outproj, dec_upproj, dec_downproj,
    dec_gains, dec_biases, dec_upbias,
):
    _, count, features = src_embed.shape
    total = tgt_embed.shape[1]
    hidden = enc_upproj.shape[1]
    devices = lax.axis_size("dp")
    seq_count = lax.axis_size("seq")
    pair = seq_count == 2
    blocks = count // BLOCK
    bits = log2(devices)
    x_first = tuple(range(bits))
    y_first = (0, OVER_SEQ, *range(1, bits)) if seq_count == 2 else x_first
    seq_index = lax.axis_index("seq")
    dp_index = lax.axis_index("dp")
    idx = jnp.where(jnp.arange(2) == 0, seq_index, dp_index).astype(jnp.int32)
    chain = Chain(idx)
    table = jnp.asarray(place_table(features))
    src_own, tgt_all = src_embed[0], tgt_embed[0]
    enc_ub, dec_ub = enc_upbias[None], dec_upbias[None]
    up = [(i, i + 1) for i in range(seq_count - 1)]
    down = [(i + 1, i) for i in range(seq_count - 1)]
    swap = [(0, 1), (1, 0)]
    wide = (count, features)
    near = lambda *arrays: [(a, NEAR) for a in arrays]
    far = lambda *arrays: [(a, FAR) for a in arrays]
    part = functools.partial
    lse = ((blocks, 2, 512), F32)
    inv = ((count, 1), F32)
    begin = lambda numbers: pl.multiple_of(numbers[0] * count, BLOCK)
    before = lambda numbers: pl.multiple_of(jnp.maximum(numbers[0] * count - BLOCK, 0), BLOCK)

    if pair:
        edge = lax.dynamic_slice_in_dim(src_own, (1 - seq_index) * (count - BLOCK), BLOCK, 0)
        left = right = lax.ppermute(chain.tie(edge), "seq", swap)
    else:
        left = lax.ppermute(src_own[count - BLOCK :], "seq", up)
        right = lax.ppermute(src_own[:BLOCK], "seq", down)
    (src_in, src_low, own_rows), _, enc_near = call(
        enc_pre_kernel, "enc_pre", [chain.token], far(src_own, src_lengths, table, enc_inproj, enc_biases),
        [(wide, F32, NEAR), (wide, LOW, FAR), ((count, 1536), LOW, NEAR)],
        ahead=far(src_lengths, table, enc_inproj, enc_gains, enc_biases, enc_ub, enc_outproj),
    )
    src_low = chain.tie(src_low)
    (enc_rows, enc_lse, enc_hid, mid_normed, mid_inv, fin_normed, fin_inv, encoded), _, self_near = call(
        part(enc_kernel, total=total), "enc_forward", [chain.token], [*near(left, right, src_in, own_rows, *enc_near), *far(enc_upproj, enc_downproj)],
        [((count + 2 * BLOCK, 1536), LOW, FAR), (*lse, FAR),
         (wide, LOW, FAR), (wide, F32, FAR), (*inv, FAR),
         (wide, F32, FAR), (*inv, FAR), (wide, LOW, FAR)],
        ahead=[(tgt_all, FAR, before, BLOCK), (tgt_all, FAR, begin, count),
               *far(tgt_lengths, table, dec_inproj, dec_gains, dec_biases, dec_outproj, cross_query)],
    )
    encoded = chain.tie(encoded)
    others = from_shards(encoded, seq_count)
    idx_self, _ = lax.optimization_barrier((chain.token, encoded))
    (tgt_low, dec_rows, dec_lse, dec_hid, self_normed, self_inv, cross_q, own_keyval), _, tail_near = call(
        part(dec_self_kernel, total=total), "dec_self", [idx_self], [*near(*self_near), *far(encoded, cross_keyval)],
        [(wide, LOW, FAR), ((count + BLOCK, 1536), LOW, FAR), (*lse, FAR), (wide, LOW, FAR), (wide, F32, FAR), (*inv, FAR),
         (wide, LOW, FAR), ((count, 1024), LOW, NEAR)],
        [(wide, F32)],
        ahead=[*far(encoded, src_lengths, tgt_lengths, dec_gains, dec_biases, dec_ub, cross_keyval),
               (dec_cotangent[0], FAR, begin, count), *far(cross_outproj, dec_upproj, dec_downproj)],
    )
    (cross_att, cross_lse, keyval, memory, decoded, cross_att_grad, cross_branch, tail_sums), tail, back_near = call(
        part(cross_tail_kernel, total=total), "cross_tail", [chain.token, src_lengths, tgt_lengths],
        [*far(cross_q), *near(tail_near[0]), *near(others, own_keyval), *near(*tail_near[1:7]), *far(self_normed), *near(*tail_near[7:])],
        [(wide, F32, FAR), (*lse, NEAR), ((total + WINDOW, 1024), LOW, NEAR), ((total, features), LOW, FAR),
         (wide, LOW, FAR), (wide, LOW, NEAR), (wide, F32, FAR), ((16, features), F32, FAR)],
        [(wide, LOW), (wide, LOW), (wide, LOW), ((min(256, count), hidden), F32), ((count, hidden), LOW),
         (wide, LOW), ((count, hidden), LOW),
         ((HEADS, BLOCK), F32), ((HEADS, BLOCK), F32), ((features, BLOCK), F32), pltpu.SemaphoreType.DMA((1,))],
        [2 * hidden + BLOCK + 512], x_first,
        ahead=far(src_lengths, tgt_lengths),
    )
    decoded = chain.tie(decoded)
    decoded_others = from_shards(decoded, seq_count)
    make = part(Reduction, devices=devices, seq_count=seq_count)
    tail = make(chain, tail, x_first)
    (mem_own, mem_send, query_grads, keyval_grads, mem_sums), _, dense_near = call(
        part(cross_back_kernel, total=total), "cross_back", [chain.token, src_lengths, tgt_lengths],
        [*far(cross_q), *near(keyval), *far(cross_att), *near(cross_att_grad, cross_lse, *back_near), *far(cross_keyval)],
        [(wide, F32, FAR), ((seq_count - 1, *wide), LOW, FAR), (wide, F32, NEAR),
         ((total, 1024), LOW, NEAR), ((8, features), F32, FAR)],
        [((total + WINDOW, 1024), F32)],
        ahead=[*far(memory, self_normed, self_inv, cross_branch),
               *far(dec_hid, dec_gains, dec_biases, cross_query, dec_outproj, dec_lse, tgt_lengths, dec_rows)],
    )
    mem_send = chain.tie(mem_send)
    mem_others = jnp.stack(
        [
            lax.ppermute(mem_send[s - 1], "seq", [(i, (i + s) % seq_count) for i in range(seq_count)])
            for s in range(1, seq_count)
        ]
    )
    decoded_others = chain.tie(decoded_others)
    tail.next()
    (self_branch, cross_sums, cross_held, self_own, self_halo), _, enc_near = call(
        part(dec_self_back_kernel, total=total), "dec_self_back", [chain.token],
        near(query_grads, keyval_grads, *dense_near),
        [(wide, F32, FAR), ((8, features), F32, FAR), ((devices, features // devices, 2048), LOW, FAR),
         ((count, 1536), F32, FAR), ((BLOCK, 1024), LOW, FAR)],
        [(wide, LOW), (wide, LOW), (wide, LOW), (wide, LOW), (wide, F32), ((count + BLOCK, 1024), F32)],
        ahead=far(enc_cotangent[0], fin_normed, fin_inv, mid_normed, mid_inv, enc_hid, enc_gains, enc_biases,
                  enc_ub, enc_downproj, enc_upproj, enc_outproj),
    )
    self_halo = chain.tie(self_halo)
    self_returned = lax.ppermute(self_halo, "seq", down)
    mem_others = chain.tie(mem_others)
    (enc_branch, enc_att_grad, enc_sums), enc, self_near = call(
        enc_tail_back_kernel, "enc_tail_back", [chain.token],
        [*far(mem_own), *near(mem_others), *near(*enc_near)],
        [(wide, F32, FAR), (wide, LOW, FAR), ((16, features), F32, FAR)],
        [(wide, LOW), (wide, LOW), ((count, hidden), LOW), (wide, LOW), ((count, hidden), LOW)],
        [2 * hidden + BLOCK + 512], x_first,
        ahead=far(self_own, self_branch, tgt_low, dec_inproj),
    )
    enc_sums = chain.tie(enc_sums)
    enc = make(chain, enc, x_first)
    self_returned = chain.tie(self_returned)
    (tgt_part, self_sums), cross, back_near = call(
        dec_input_grad_kernel, "dec_input_grad", [chain.token],
        [*near(self_returned), *near(*self_near), (cross_held, RAW)],
        [(wide, LOW, FAR), ((8, features), F32, FAR)],
        [((count, 1536), LOW)],
        [1536 + 2048], y_first,
        ahead=far(enc_att_grad, enc_lse, src_lengths, enc_rows),
    )
    tgt_part = chain.tie(tgt_part)
    cross = make(chain, cross, y_first)
    tgt_others = from_shards(tgt_part, seq_count)
    tail.next()
    enc.next()
    (enc_own, *halos), _, in_near = call(
        part(enc_self_back_kernel, total=total), "enc_self_back", [chain.token], near(*back_near),
        [((count, 1536), F32, NEAR)] + [((BLOCK, 1024), LOW, FAR)] * (1 if pair else 2),
        [(wide, F32), ((count + 2 * BLOCK, 1024), F32)],
        ahead=far(enc_branch, src_low, enc_inproj),
    )
    halos = [chain.tie(h) for h in halos]
    if pair:
        halos = [lax.ppermute(halos[0], "seq", swap)]
    else:
        halos = [lax.ppermute(halos[1], "seq", up), lax.ppermute(halos[0], "seq", down)]
    cross.next()
    tail.next()
    tgt_others = chain.tie(tgt_others)
    halos = [chain.tie(h) for h in halos]
    (src_grad,), ins, _ = call(
        part(enc_input_grad_kernel, halo_count=len(halos)), "enc_input_grad", [chain.token],
        [*near(*halos), *near(enc_own, *in_near), *far(tail_sums, mem_sums, cross_sums, self_sums, enc_sums)],
        [(wide, F32, FAR)],
        [((count, 1536), LOW), ((8, features), F32), ((BLOCK, features), F32)],
        [1536 + BLOCK], x_first,
    )
    src_grad = chain.tie(src_grad)
    ins = make(chain, ins, x_first)
    share = features // devices
    slim = lambda *widths: [((share, w), F32, FAR) for w in widths]
    matrices = [*slim(hidden, 512), ((hidden // devices, 512), F32, FAR), ((1, hidden // devices), F32, FAR)]
    all_rows = (total, features)
    packed = ((share, 2 * hidden + BLOCK + 512), F32)
    enc.next()
    ins.next()
    tail.next()
    cross.next()
    ins.next()
    enc.next()
    (decoded_all, tgt_all_grad), _, _ = call(
        rows_unpack, "rows_unpack", [chain.token], [*far(decoded), *near(decoded_others), *far(tgt_part), *near(tgt_others)],
        [(all_rows, LOW, FAR), (all_rows, F32, FAR)],
    )
    tgt_all_grad = chain.tie(tgt_all_grad)
    (dec_up, cross_out, dec_down, dec_ub_grad), _, _ = call(
        feed_forward_unpack, "tail_unpack", [chain.token], near(*tail.pair()), matrices, [packed]
    )
    dec_up = chain.tie(dec_up)
    cross.next()
    ins.next()
    enc.next()
    cross.next()
    ins.next()
    cross.next()
    t, m, c, d, e, i = range(0, 48, 8)
    picks = [
        (e, e + 1),
        (i, i + 1, e + 2, e + 3, e + 4, e + 5),
        (c, t, t + 1),
        (d, d + 1, c + 1, c + 2, c + 3, m, t + 2, t + 3, t + 4, t + 5),
    ]
    (enc_up, enc_out, enc_down, enc_ub_grad, enc_in, enc_gains_grad, enc_biases_grad, dec_gains_grad,
     dec_biases_grad), _, _ = call(
        part(encoders_unpack, picks=picks), "last_unpack", [chain.token], near(*enc.pair(), *ins.pair()),
        [*matrices, *slim(1536), *[((len(p), share), F32, FAR) for p in picks]], [packed],
    )
    enc_up = chain.tie(enc_up)
    (dec_in, keyval_grad, query_grad, dec_out), _, _ = call(
        part(decoder_unpack, halved=OVER_SEQ in y_first), "cross_unpack", [chain.token], near(*cross.pair()),
        slim(1536, 1024, 512, 512), [((share, 3584), F32)],
    )
    return (
        encoded[None],
        decoded_all[None],
        src_grad[None],
        tgt_all_grad[None],
        enc_in,
        enc_out,
        enc_up,
        enc_down,
        enc_gains_grad,
        enc_biases_grad,
        enc_ub_grad[0],
        dec_in,
        dec_out,
        query_grad,
        keyval_grad,
        cross_out,
        dec_up,
        dec_down,
        dec_gains_grad,
        dec_biases_grad,
        dec_ub_grad[0],
    )


def solution(mesh):
    rows, whole = P("dp", "seq", None), P("dp", None, None)
    return jax.shard_map(
        local,
        mesh=mesh,
        in_specs=(rows, whole, P("dp", None), P("dp", None), rows, whole, *([P()] * 17)),
        out_specs=(
            rows, whole, rows, whole,
            *([P("dp", None)] * 4), P(None, "dp"), P(None, "dp"), P("dp"),
            *([P("dp", None)] * 7), P(None, "dp"), P(None, "dp"), P("dp"),
        ),
        check_vma=False,
    )
```

```python
import functools
import math

import jax
import jax.numpy as jnp
import numpy as np
from jax import lax
from jax.experimental import pallas as pl
from jax.experimental.pallas import tpu as pltpu
from jax.sharding import PartitionSpec as P

HEADS = 8
HEAD_DIM = 64
MAXPAIR = 128
BLOCK = 128
GROUP = 256
WINDOW = 256
LOW = jnp.bfloat16
F32 = jnp.float32
MASKED = -1e30
FEATURES = 512
HIDDEN = 2048


def place_table(features):
    half = features // 2
    frequency = np.exp(-math.log(10000.0) * np.arange(half, dtype=np.float32) / np.float32(half)).astype(np.float32)
    angles = (np.arange(MAXPAIR, dtype=np.float32)[:, None] * frequency[None, :]).astype(np.float32)
    table = np.concatenate([np.sin(angles), np.cos(angles)], axis=-1).astype(np.float32)
    pieces, rest = [], table
    for _ in range(3):
        piece = rest.astype(jnp.bfloat16)
        pieces.append(piece)
        rest = rest - piece.astype(np.float32)
    return np.stack(pieces)


def dot_nn(left, right):
    return lax.dot_general(left, right, (((1,), (0,)), ((), ())), preferred_element_type=F32)


def dot_nt(left, right):
    return lax.dot_general(left, right, (((1,), (1,)), ((), ())), preferred_element_type=F32)


def dot_tn(left, right):
    return lax.dot_general(left, right, (((0,), (0,)), ((), ())), preferred_element_type=F32)


def iota(shape, dim):
    return lax.broadcasted_iota(jnp.int32, shape, dim).astype(F32)


def pair_ends(len_row):
    count = len_row.shape[1]
    lengths = jnp.broadcast_to(len_row, (count, count))
    down, across = iota((count, count), 0), iota((count, count), 1)
    ends_col = jnp.sum(jnp.where(across <= down, lengths, 0.0), axis=1, keepdims=True)
    len_col = jnp.sum(jnp.where(across == down, lengths, 0.0), axis=1, keepdims=True)
    ends_row = jnp.sum(jnp.where(down <= across, len_col, 0.0), axis=0, keepdims=True)
    return (ends_row, ends_col)


def pair_col(ends_row, places, total):
    number = jnp.sum(jnp.where(ends_row <= places, 1.0, 0.0), axis=1, keepdims=True)
    return jnp.where((places >= 0.0) & (places < total), number, -1.0)


def pair_row(ends_col, places):
    return jnp.sum(jnp.where(ends_col <= places, 1.0, 0.0), axis=0, keepdims=True)


def with_places(embed, places, ends_row, len_row, table_ref):
    started = jnp.sum(jnp.where(ends_row <= places, len_row, 0.0), axis=1, keepdims=True)
    inside = places - started
    hot = jnp.where(iota((embed.shape[0], MAXPAIR), 1) == inside, 1.0, 0.0).astype(LOW)
    sines = dot_nn(hot, table_ref[0]) + dot_nn(hot, table_ref[1]) + dot_nn(hot, table_ref[2])
    return embed.astype(F32) + sines


def norm_forward(values, gain_row, shift_row):
    centred = values - jnp.mean(values, axis=-1, keepdims=True)
    inverse = lax.rsqrt(jnp.mean(centred * centred, axis=-1, keepdims=True) + 1e-05)
    normed = centred * inverse
    return (normed * gain_row + shift_row, normed, inverse)


def norm_backward(grad_rows, normed, inverse, gain_row):
    scaled = grad_rows * gain_row
    return inverse * (
        scaled
        - jnp.mean(scaled, axis=-1, keepdims=True)
        - normed * jnp.mean(scaled * normed, axis=-1, keepdims=True)
    )


def sigmoid(values):
    return 0.5 * jnp.tanh(0.5 * values) + 0.5


def col_sum(values):
    return jnp.sum(values, axis=0, keepdims=True)


def head_masks(scale):
    lane = lax.broadcasted_iota(jnp.int32, (1, GROUP), 1) // HEAD_DIM
    return [jnp.where(lane == h, scale, 0.0).astype(LOW) for h in range(GROUP // HEAD_DIM)]


def spread(rows, masks):
    return jnp.concatenate([rows * mask for mask in masks], axis=0)


def diagonal(wide):
    count = GROUP // HEAD_DIM
    return [
        wide[h * HEAD_DIM : (h + 1) * HEAD_DIM, h * BLOCK : (h + 1) * BLOCK] for h in range(count)
    ]


def attend_block(query, keys, values, bias, group):
    lanes = slice(group * GROUP, (group + 1) * GROUP)
    stacked = spread(query(lanes), head_masks(HEAD_DIM**-0.5))
    scores = dot_nt(keys(lanes), stacked)
    probs, maxima, sums = [], [], []
    for h in range(GROUP // HEAD_DIM):
        score = scores[:, h * BLOCK : (h + 1) * BLOCK] + bias
        row_max = jnp.max(score, axis=0, keepdims=True)
        exp_score = jnp.exp(score - row_max)
        maxima.append(row_max)
        sums.append(col_sum(exp_score))
        probs.append(exp_score.astype(LOW))
    wide = dot_tn(values(lanes), jnp.concatenate(probs, axis=1))
    return (diagonal(wide), maxima, sums)


def attend_local(rows_ref, count, width, att_ref, lse_ref, rule):
    def body(j, carry):
        first = pl.multiple_of(j * BLOCK, BLOCK)
        queries = pl.ds(pl.multiple_of(first + BLOCK, BLOCK), BLOCK)
        keys = pl.ds(first, width)
        bias = rule(first)
        for group in range(2):
            def part(rows, offset):
                return lambda lanes: rows_ref[rows, offset + lanes.start : offset + lanes.stop]

            outs, maxima, sums = attend_block(
                part(queries, 0), part(keys, 512), part(keys, 1024), bias, group
            )
            mixed = jnp.concatenate([o * (1.0 / s) for o, s in zip(outs, sums)], axis=0)
            att_ref[pl.ds(first, BLOCK), group * GROUP : (group + 1) * GROUP] = mixed.T.astype(
                att_ref.dtype
            )
            lse_ref[j, group : group + 1, :] = jnp.concatenate(
                [m + jnp.log(s) for m, s in zip(maxima, sums)], axis=1
            )
        return carry

    lax.fori_loop(0, count, body, 0)


def attend_back_block(query, grad, keys, values, bias, lse, deltas):
    stacked = spread(query, head_masks(HEAD_DIM**-0.5))
    grads = spread(grad, head_masks(1.0))
    scores = dot_nt(keys, stacked)
    prob_grads = dot_nt(values, grads)
    probs, score_grads = [], []
    for h in range(GROUP // HEAD_DIM):
        cols = slice(h * BLOCK, (h + 1) * BLOCK)
        prob = jnp.exp(scores[:, cols] + bias - lse[:, cols])
        prob_grad = prob_grads[:, cols]
        delta = col_sum(prob * prob_grad) if deltas is None else deltas[h]
        score_grads.append((prob * (prob_grad - delta)).astype(LOW))
        probs.append(prob.astype(LOW))
    prob_wide = jnp.concatenate(probs, axis=1)
    grad_wide = jnp.concatenate(score_grads, axis=1)
    value_grad = dot_nn(prob_wide, grads)
    key_grad = dot_nn(grad_wide, stacked)
    query_grad = jnp.concatenate(diagonal(dot_tn(keys, grad_wide)), axis=0) * HEAD_DIM**-0.5
    return (query_grad, key_grad, value_grad)


def attend_local_back(rows_ref, grad_ref, lse_ref, count, width, query_ref, keyval_ref, rule):
    keyval_ref[...] = jnp.zeros(keyval_ref.shape, F32)

    def body(j, carry):
        first = pl.multiple_of(j * BLOCK, BLOCK)
        queries = pl.ds(pl.multiple_of(first + BLOCK, BLOCK), BLOCK)
        own = pl.ds(first, BLOCK)
        keys = pl.ds(first, width)
        bias = rule(first)
        for group in range(2):
            low, high = group * GROUP, (group + 1) * GROUP
            query_grad, key_grad, value_grad = attend_back_block(
                rows_ref[queries, low:high],
                grad_ref[own, low:high],
                rows_ref[keys, 512 + low : 512 + high],
                rows_ref[keys, 1024 + low : 1024 + high],
                bias,
                lse_ref[j, group : group + 1, :],
                None,
            )
            query_ref[own, low:high] = query_grad.T
            keyval_ref[keys, low:high] += key_grad
            keyval_ref[keys, 512 + low : 512 + high] += value_grad
        return carry

    lax.fori_loop(0, count, body, 0)


def self_rule(ends, start, total, width, causal):
    ends_row, ends_col = ends

    def rule(first):
        shift = (start + first).astype(F32)
        key_places = iota((width, 1), 0) + (shift - BLOCK)
        query_places = iota((1, BLOCK), 1) + shift
        allowed = pair_col(ends_row, key_places, total) == pair_row(ends_col, query_places)
        if causal:
            allowed = allowed & (key_places <= query_places)
        return jnp.where(allowed, 0.0, MASKED)

    return rule


class Loaded:
    def __init__(self, ref):
        self.ref = ref

    def get(self):
        return self.ref


class Coming:
    def __init__(self, far, near, sem):
        self.near = near
        self.copy = pltpu.make_async_copy(far, near, sem)
        self.copy.start()
        self.waiting = True

    def get(self):
        if self.waiting:
            self.copy.wait()
            self.waiting = False
        return self.near


class Leaving:
    def __init__(self, near, far, sem):
        self.ref = near
        self.copy = pltpu.make_async_copy(near, far, sem)
        self.started = False

    def flush(self):
        if not self.started:
            self.copy.start()
            self.started = True

    def finish(self):
        self.flush()
        self.copy.wait()


OVER_SEQ = "seq"


def put_rows(held, result, col):
    devices, rows, _ = held.shape
    cols = pl.ds(col if isinstance(col, int) else pl.multiple_of(col, BLOCK), result.shape[1])
    low = result.astype(LOW)
    for i in range(devices):
        held[i, :, cols] = low[i * rows : (i + 1) * rows, :]


class Blocks:
    def __init__(self, keep, send, held, sems, numbers, order):
        self.keep, self.send, self.held, self.sems = (keep, send, held, sems)
        self.numbers, self.order = (numbers, order)
        self.used = []

    def spread(self, col, width):
        half, bits = (self.keep.shape[0], len(self.order))
        chunk = len(self.used)
        seq, mine = self.numbers[0], self.numbers[1]
        for place in range(2 * half):
            flips = {bit: (place >> (bits - 1 - s)) & 1 for s, bit in enumerate(self.order)}
            source = target = pl.ds(col, width)
            if OVER_SEQ in flips:
                source = pl.ds(pl.multiple_of((seq ^ flips.pop(OVER_SEQ)) * (width // 2), BLOCK), width // 2)
                target = pl.ds(0, width // 2)
            flip = sum(value << bit for bit, value in flips.items())
            refs = self.keep if place < half else self.send
            pltpu.make_async_copy(
                self.held.at[mine ^ flip, :, source],
                refs.at[place % half, :, target],
                self.sems.at[chunk],
            ).start()
        self.used.append(pl.ds(col, width))

    def fill(self, source, col):
        width = source.ref.shape[2]
        self.filling = pltpu.make_async_copy(
            source.ref, self.held.at[:, :, pl.ds(col, width)], self.sems.at[15]
        )
        self.filling.start()

    def filled(self):
        self.filling.wait()

    def put_rows(self, result, col):
        put_rows(self.held, result, col)

    def put_cols(self, result, sums, first, col):
        devices, rows, _ = self.held.shape
        width = result.shape[1] // (result.shape[1] * devices // HIDDEN)
        pieces = BLOCK // width
        low = result.astype(LOW)
        tall = low.shape[0] // pieces
        top = iota((rows, width), 0) == 0.0
        for n in range(result.shape[1] // width):
            at = slice(n * width, (n + 1) * width)
            piece = [low[p * tall : (p + 1) * tall, at] for p in range(pieces)]
            piece = piece[0] if pieces == 1 else jnp.concatenate(piece, axis=1)
            for g in range(tall // rows):
                self.held[first + n, :, col + g * BLOCK : col + (g + 1) * BLOCK] = piece[
                    g * rows : (g + 1) * rows, :
                ]
            row = jnp.where(top, sums[:, at], 0.0).astype(LOW)
            row = row if pieces == 1 else jnp.concatenate([row] * pieces, axis=1)
            end = col + (tall // rows) * BLOCK
            self.held[first + n, :, end : end + BLOCK] = row

    def finish(self):
        for chunk, cols in enumerate(self.used):
            whole = self.held.at[:, :, cols]
            pltpu.make_async_copy(whole, whole, self.sems.at[chunk]).wait()


NEAR, FAR, RAW = "near", "far", "raw"
IN_HBM = pl.BlockSpec(memory_space=pltpu.HBM)
IN_VMEM = pl.BlockSpec(memory_space=pltpu.VMEM)
IN_SMEM = pl.BlockSpec(memory_space=pltpu.SMEM)


LIMITS = {'rows_unpack': 14, 'tail_unpack': 6, 'last_unpack': 8, 'cross_unpack': 4, 'dec_pre': 8, 'enc_pre': 8, 'enc_forward': 18, 'dec_self': 13, 'cross_tail': 27, 'cross_back': 13, 'dec_self_back': 18, 'enc_tail_back': 20, 'enc_self_back': 12, 'dec_input_grad': 10, 'enc_input_grad': 9}
MICROS = {'dec_pre': 42, 'enc_forward': 42, 'dec_self': 42, 'cross_tail': 42, 'cross_back': 42, 'dec_self_back': 42, 'enc_tail_back': 42, 'enc_self_back': 42, 'dec_input_grad': 42, 'enc_input_grad': 42}


def call(kernel, name, scalars, operands, outs, scratch=(), blocks=(), order=(), ahead=()):
    arrays, specs = [], []
    for array, mode, *_ in (*operands, *ahead):
        near = mode == NEAR
        arrays.append(pltpu.with_memory_space_constraint(array, pltpu.VMEM if near else pltpu.HBM))
        specs.append(IN_VMEM if near else IN_HBM)

    def taken(array, mode, start=None, size=None):
        return array.shape if size is None else (size, *array.shape[1:])

    shapes, out_specs = [], []
    for shape, dtype, mode in outs:
        shapes.append((pltpu.VMEM if mode == NEAR else pltpu.HBM)(shape, dtype))
        out_specs.append(IN_VMEM if mode == NEAR else IN_HBM)
    over_seq = OVER_SEQ in order
    devices = 1 << (len(order) - over_seq)
    share = FEATURES // devices
    for columns in blocks:
        shapes += [pltpu.HBM(((1 << len(order)) // 2, share, columns // (1 + over_seq)), LOW)] * 2
        out_specs += [IN_HBM] * 2
    for one in ahead:
        shapes.append(pltpu.VMEM(taken(*one), one[0].dtype))
        out_specs.append(IN_VMEM)
    far_in = [i for i, one in enumerate(operands) if one[1] == FAR]
    far_out = [i for i, one in enumerate(outs) if one[2] == FAR]
    extra = [pltpu.VMEM(*one) if isinstance(one, tuple) else one for one in scratch]
    extra += [pltpu.VMEM(taken(*operands[i]), operands[i][0].dtype) for i in far_in]
    extra += [pltpu.VMEM(outs[i][0], outs[i][1]) for i in far_out]
    extra += [pltpu.VMEM((devices, share, columns), LOW) for columns in blocks]
    extra += [pltpu.SemaphoreType.DMA((len(far_in) + len(far_out) + len(ahead) + 1,))]
    extra += [pltpu.SemaphoreType.DMA((16,)) for _ in blocks]

    def body(*refs):
        refs = list(refs)
        take = lambda n: [refs.pop(0) for _ in range(n)]
        numbers = take(len(scalars))
        ins = take(len(operands))
        sources = take(len(ahead))
        results = take(len(outs))
        sends = [take(2) for _ in blocks]
        copies = take(len(ahead))
        temps = take(len(scratch))
        near_in = take(len(far_in))
        near_out = take(len(far_out))
        helds = take(len(blocks))
        sems = take(1)[0]
        block_sems = take(len(blocks))
        used = iter(range(len(far_in) + len(far_out) + len(ahead)))

        def coming(ref, near, array, mode, start=None, size=None):
            source = ref if size is None else ref.at[pl.ds(start(numbers[0]), size)]
            return Coming(source, near, sems.at[next(used)])

        given = [Loaded(ref) for ref in ins]
        for n, i in enumerate(far_in):
            given[i] = coming(ins[i], near_in[n], *operands[i])
        later = [coming(ref, near, *one) for ref, near, one in zip(sources, copies, ahead)]
        leaving = {}
        for n, i in enumerate(far_out):
            leaving[i] = Leaving(near_out[n], results[i], sems.at[next(used)])
        made = [leaving.get(i, Loaded(results[i])) for i in range(len(outs))]
        moved = [
            Blocks(keep, send, held, sem, numbers[0], order)
            for (keep, send), held, sem in zip(sends, helds, block_sems)
        ]
        kernel(numbers, given, made, temps, *moved)
        for one in leaving.values():
            one.flush()
        for one in (*given, *later):
            one.get()
        for one in leaving.values():
            one.finish()
        for one in moved:
            one.finish()

    results = pl.pallas_call(
        body,
        name=name,
        out_shape=shapes,
        in_specs=[IN_SMEM] * len(scalars) + specs,
        out_specs=out_specs,
        scratch_shapes=extra,
        cost_estimate=pl.CostEstimate(flops=int(MICROS.get(name, 1.0) * 1.0 * 1.15e9), bytes_accessed=1, transcendentals=0),
        compiler_params=pltpu.CompilerParams(vmem_limit_bytes=LIMITS[name] * 1024 * 1024),
    )(*scalars, *arrays)
    made = len(outs) + 2 * len(blocks)
    return (results[: len(outs)], results[len(outs) : made], results[made:])


def input_rows(halos, own, table, w_in, biases, x_ref, low_ref, rows_ref, start, count, ends, len_row, shift=0):
    def chunk(embed, target, size):
        places = iota((size, 1), 0) + (start + target - BLOCK).astype(F32)
        x = with_places(embed, places, ends[0], len_row, table)
        low = x.astype(LOW)
        for c in range(3):
            part = dot_nn(low, w_in[:, c * 512 : (c + 1) * 512])
            if c != 1:
                part = part + biases[c // 2 : c // 2 + 1, :]
            rows_ref[pl.ds(target - shift, size), c * 512 : (c + 1) * 512] = part.astype(LOW)
        return (x, low)

    size = min(256, count)

    def body(step, carry):
        at = pl.multiple_of(step * size, size)
        rows = pl.ds(at, size)
        x_ref[rows, :], low_ref[rows, :] = chunk(own[rows, :], pl.multiple_of(at + BLOCK, BLOCK), size)
        return carry

    if own is not None:
        lax.fori_loop(0, count // size, body, 0)
    for embed, target in halos:
        chunk(embed[...], target, BLOCK)


def enc_pre_kernel(numbers, ins, outs, temps):
    own, lens, table, w_in, biases = [i.get() for i in ins]
    x_out, low_out, rows_out = [o.ref for o in outs]
    count = own.shape[0]
    len_row = lens[...].astype(F32)
    input_rows(
        [], own, table, w_in, biases, x_out, low_out, rows_out, numbers[0][0] * count, count, pair_ends(len_row), len_row,
        BLOCK,
    )


def enc_kernel(numbers, ins, outs, temps, total):
    left, right, x_ref, own_rows, lens, table, w_in, gains, biases, upbias, w_out, w_up, w_down = ins
    rows_out, lse_out, hid_out, mid_out, mid_inv_out, fin_out, fin_inv_out, encoded_out = outs
    x_ref = x_ref.get()
    count = x_ref.shape[0]
    start = numbers[0][0] * count
    len_row = lens.get()[...].astype(F32)
    ends = pair_ends(len_row)
    size = min(256, count)
    left, right, table, w_in, gains, biases, upbias = [
        i.get() for i in (left, right, table, w_in, gains, biases, upbias)
    ]
    rows_out.ref[BLOCK : BLOCK + count, :] = own_rows.get()[...]
    input_rows(
        [(left, 0), (right, BLOCK + count)], None, table, w_in, biases, None, None, rows_out.ref, start, count, ends,
        len_row,
    )
    rows_out.flush()
    width = 3 * BLOCK
    attend_local(
        rows_out.ref, count // BLOCK, width, hid_out.ref, lse_out.ref,
        self_rule(ends, start, total, width, False),
    )
    lse_out.flush()
    hid_out.flush()
    w_out, w_up, w_down = w_out.get(), w_up.get(), w_down.get()
    hid, mid_ref, mid_inv, fin_ref, fin_inv, encoded = [
        o.ref for o in (hid_out, mid_out, mid_inv_out, fin_out, fin_inv_out, encoded_out)
    ]

    def dense(step, carry):
        rows = pl.ds(pl.multiple_of(step * size, size), size)
        z = x_ref[rows, :] + dot_nn(hid[rows, :], w_out[...]) + biases[2:3, :]
        mid, normed, inverse = norm_forward(z, gains[0:1, :], biases[3:4, :])
        mid_ref[rows, :] = normed
        mid_inv[rows, :] = inverse
        low = mid.astype(LOW)
        z = mid + biases[4:5, :]
        for c in range(0, w_up.shape[1], 512):
            up = dot_nn(low, w_up[:, c : c + 512]) + upbias[:, c : c + 512]
            active = (up * sigmoid(up)).astype(LOW)
            z = z + dot_nn(active, w_down[c : c + 512, :])
        final, normed, inverse = norm_forward(z, gains[1:2, :], biases[5:6, :])
        fin_ref[rows, :] = normed
        fin_inv[rows, :] = inverse
        encoded[rows, :] = final.astype(LOW)
        return carry

    lax.fori_loop(0, count // size, dense, 0)


def dec_self_kernel(numbers, ins, outs, temps, total):
    halo, own, lens, table, w_in, gains, biases, w_out, w_query = [i.get() for i in ins[:9]]
    low_out, rows_out, lse_out, hid_out, normed_out, inv_out, query_out, keyval_out = outs
    (x,) = temps
    rows_in = rows_out.ref
    count = x.shape[0]
    start = numbers[0][0] * count
    len_row = lens[...].astype(F32)
    ends = pair_ends(len_row)
    input_rows([(halo, 0)], own, table, w_in, biases, x, low_out.ref, rows_in, start, count, ends, len_row)
    low_out.flush()
    rows_out.flush()
    width = 2 * BLOCK
    attend_local(
        rows_in, count // BLOCK, width, hid_out.ref, lse_out.ref,
        self_rule(ends, start, total, width, True),
    )
    size = min(256, count)
    hid, normed_ref, inv_ref, query_ref = [o.ref for o in (hid_out, normed_out, inv_out, query_out)]

    def dense(step, carry):
        rows = pl.ds(pl.multiple_of(step * size, size), size)
        z = x[rows, :] + dot_nn(hid[rows, :], w_out[...]) + biases[2:3, :]
        mid, normed, inverse = norm_forward(z, gains[0:1, :], biases[3:4, :])
        normed_ref[rows, :] = normed
        inv_ref[rows, :] = inverse
        query = dot_nn(mid.astype(LOW), w_query[...]) + biases[4:5, :]
        query_ref[rows, :] = query.astype(LOW)
        return carry

    lax.fori_loop(0, count // size, dense, 0)
    for out in (normed_out, inv_out, query_out):
        out.flush()
    project(ins[9].get(), ins[10].get(), biases, keyval_out.ref, 0, count)


def project(source, w, biases, keyval_out, base, length):
    size = min(256, length)

    def body(step, carry):
        at = pl.multiple_of(step * size, size)
        rows = pl.ds(pl.multiple_of(base + at, BLOCK), size)
        values = source[pl.ds(at, size), :]
        keyval_out[rows, :512] = dot_nn(values, w[:, :512]).astype(LOW)
        keyval_out[rows, 512:] = (dot_nn(values, w[:, 512:]) + biases[5:6, :]).astype(LOW)
        return carry

    lax.fori_loop(0, length // size, body, 0)


def cross_span(src_lens, tgt_lens, first):
    def step(k, carry):
        begin, low, high = carry
        end = begin + tgt_lens[0, k]
        length = src_lens[0, k]
        low = low + jnp.where(end <= first, length, 0)
        high = high + jnp.where(begin <= first + (BLOCK - 1), length, 0)
        return (end, low, high)

    zero = jnp.int32(0)
    _, low, high = lax.fori_loop(0, src_lens.shape[1], step, (zero, zero, zero), unroll=True)
    low = (low // 16) * 16
    return (low, (high - low + (WINDOW - 1)) // WINDOW)


def cross_rule(src_ends_row, tgt_ends_col, first, begin, total):
    key_places = iota((WINDOW, 1), 0) + begin.astype(F32)
    query_places = iota((1, BLOCK), 1) + first.astype(F32)
    allowed = pair_col(src_ends_row, key_places, total) == pair_row(tgt_ends_col, query_places)
    return jnp.where(allowed, 0.0, MASKED)


def cross_forward(
    numbers, query, memory, others, own_keyval, src_vec, tgt_vec, biases, w, att_out, lse_out, keyval_out, memory_out,
    max_ref, sum_ref, acc_ref, copy_sem, total,
):
    idx, src_lens, tgt_lens = numbers
    count = query.shape[0]
    length = memory.shape[0]
    shards = others.shape[0] + 1
    start = idx[0] * count
    src_ends_row, _ = pair_ends(src_vec[...].astype(F32))
    _, tgt_ends_col = pair_ends(tgt_vec[...].astype(F32))
    own_rows = pl.ds(pl.multiple_of(idx[0] * length, BLOCK), length)
    own_copy = pltpu.make_async_copy(own_keyval, keyval_out.at[own_rows], copy_sem.at[0])
    own_copy.start()
    for s in range(shards):
        base = lax.rem(idx[0] + s, shards) * length
        memory_out[pl.ds(pl.multiple_of(base, BLOCK), length), :] = memory[...] if s == 0 else others[s - 1]
        if s:
            project(others.at[s - 1], w, biases, keyval_out, base, length)
    own_copy.wait()
    keyval_out[total:, :] = jnp.zeros((WINDOW, 1024), LOW)

    def body(j, carry):
        at = pl.multiple_of(j * BLOCK, BLOCK)
        rows = pl.ds(at, BLOCK)
        first = start + at
        low, windows = cross_span(src_lens, tgt_lens, first)
        max_ref[...] = jnp.full(max_ref.shape, MASKED, F32)
        sum_ref[...] = jnp.zeros(sum_ref.shape, F32)
        acc_ref[...] = jnp.zeros(acc_ref.shape, F32)

        def window(n, carry):
            begin = pl.multiple_of(low + n * WINDOW, 16)
            keys = pl.ds(begin, WINDOW)
            bias = cross_rule(src_ends_row, tgt_ends_col, first, begin, total)
            for group in range(2):
                def part(ref, rows, offset):
                    return lambda lanes: ref[rows, offset + lanes.start : offset + lanes.stop]

                outs, maxima, sums = attend_block(
                    part(query, rows, 0), part(keyval_out, keys, 0), part(keyval_out, keys, 512), bias, group
                )
                for h in range(4):
                    head = group * 4 + h
                    old = max_ref[head : head + 1, :]
                    new = jnp.maximum(old, maxima[h])
                    before, now = jnp.exp(old - new), jnp.exp(maxima[h] - new)
                    max_ref[head : head + 1, :] = new
                    sum_ref[head : head + 1, :] = sum_ref[head : head + 1, :] * before + sums[h] * now
                    part_rows = slice(head * HEAD_DIM, (head + 1) * HEAD_DIM)
                    acc_ref[part_rows, :] = acc_ref[part_rows, :] * before + outs[h] * now
            return carry

        lax.fori_loop(0, windows, window, 0)
        for group in range(2):
            heads = range(group * 4, group * 4 + 4)
            mixed = jnp.concatenate(
                [
                    acc_ref[h * HEAD_DIM : (h + 1) * HEAD_DIM, :] * (1.0 / sum_ref[h : h + 1, :])
                    for h in heads
                ],
                axis=0,
            )
            att_out[rows, group * GROUP : (group + 1) * GROUP] = mixed.T
            lse_out[j, group : group + 1, :] = jnp.concatenate(
                [max_ref[h : h + 1, :] + jnp.log(sum_ref[h : h + 1, :]) for h in heads], axis=1
            )
        return carry

    lax.fori_loop(0, count // BLOCK, body, 0)


def feed_forward_grads(mid, up_low, ffn, active, hid, branch, sums, blocks):
    hidden = up_low.shape[1]
    devices, rows, _ = blocks.held.shape
    width = hidden // devices
    down = hidden + BLOCK

    def down_part(c, carry):
        cols = pl.ds(pl.multiple_of(c * 512, 512), 512)
        blocks.put_cols(dot_tn(ffn[...], active[:, cols]), sums[pl.ds(8 + c, 1), :], c * (512 // width), 0)
        return carry

    def up_part(c, carry):
        cols = pl.ds(pl.multiple_of(c * 512, 512), 512)
        blocks.put_rows(dot_tn(mid[...], up_low[:, cols]), down + c * 512)
        return carry

    lax.fori_loop(0, hidden // 512, down_part, 0)
    blocks.spread(0, down)
    lax.fori_loop(0, hidden // 512, up_part, 0)
    blocks.spread(down, hidden)
    blocks.put_rows(dot_tn(hid[...], branch[...]), down + hidden)
    blocks.spread(down + hidden, 512)


def cross_tail_kernel(numbers, ins, outs, temps, blocks, total):
    (query, memory, others, own_keyval, src_vec, tgt_vec, gains, biases, upbias, w_keyval, normed_in, cot, w_out, w_up,
     w_down) = [i.get() for i in ins]
    att, lse_out, keyval_out, memory_out, decoded_out, att_grad_out, branch_out, sums_out = [o.ref for o in outs]
    hid_ref, branch_ref, mid_ref, up_ref, active_ref, ffn_ref, up_low_ref, *running = temps
    cross_forward(
        numbers, query, memory, others, own_keyval, src_vec, tgt_vec, biases, w_keyval, att, lse_out, keyval_out,
        memory_out, *running, total,
    )
    count = att.shape[0]
    hidden = w_up.shape[1]
    sums_out[...] = jnp.zeros(sums_out.shape, F32)
    size = min(256, count)

    def dense(step, carry):
        rows = pl.ds(pl.multiple_of(step * size, size), size)
        hid = att[rows, :].astype(LOW)
        hid_ref[rows, :] = hid
        first = normed_in[rows, :] * gains[0:1, :] + biases[3:4, :]
        z = first + dot_nn(hid, w_out[...]) + biases[6:7, :]
        mid, normed, inverse = norm_forward(z, gains[1:2, :], biases[7:8, :])
        low = mid.astype(LOW)
        mid_ref[rows, :] = low
        z = mid + biases[8:9, :]
        for c in range(0, hidden, 512):
            up = dot_nn(low, w_up[:, c : c + 512]) + upbias[:, c : c + 512]
            gate = sigmoid(up)
            active = up * gate
            up_ref[:, c : c + 512] = gate + active * (1.0 - gate)
            active = active.astype(LOW)
            active_ref[rows, c : c + 512] = active
            z = z + dot_nn(active, w_down[c : c + 512, :])
        final, normed_final, inverse_final = norm_forward(z, gains[2:3, :], biases[9:10, :])
        decoded_out[rows, :] = final.astype(LOW)
        grad = cot[rows, :].astype(F32)
        ffn = norm_backward(grad, normed_final, inverse_final, gains[2:3, :])
        ffn_low = ffn.astype(LOW)
        ffn_ref[rows, :] = ffn_low
        mid_grad = ffn
        for c in range(0, hidden, 512):
            up_grad = dot_nt(ffn_low, w_down[c : c + 512, :]) * up_ref[:, c : c + 512]
            sums_out[8 + c // 512 : 9 + c // 512, :] += col_sum(up_grad)
            up_low = up_grad.astype(LOW)
            up_low_ref[rows, c : c + 512] = up_low
            mid_grad = mid_grad + dot_nt(up_low, w_up[:, c : c + 512])
        branch = norm_backward(mid_grad, normed, inverse, gains[1:2, :])
        branch_low = branch.astype(LOW)
        branch_out[rows, :] = branch
        branch_ref[rows, :] = branch_low
        att_grad_out[rows, :] = dot_nt(branch_low, w_out[...]).astype(LOW)
        sums_out[0:1, :] += col_sum(mid_grad * normed)
        sums_out[1:2, :] += col_sum(grad * normed_final)
        sums_out[2:3, :] += col_sum(branch)
        sums_out[3:4, :] += col_sum(mid_grad)
        sums_out[4:5, :] += col_sum(ffn)
        sums_out[5:6, :] += col_sum(grad)
        return carry

    lax.fori_loop(0, count // size, dense, 0)
    for out in (outs[0], outs[3], outs[4], outs[6]):
        out.flush()
    feed_forward_grads(
        mid_ref, up_low_ref, ffn_ref, active_ref, hid_ref, branch_ref, sums_out, blocks
    )


def cross_back_kernel(numbers, ins, outs, temps, total):
    idx, src_lens, tgt_lens = numbers
    query, keyval, att, att_grad, lse, src_vec, tgt_vec = [i.get() for i in ins[:7]]
    mem_own_out, mem_out, query_out, keyval_low, sums_out = [o.ref for o in outs]
    (keyval_ref,) = temps
    count = query.shape[0]
    start = idx[0] * count
    src_ends_row, _ = pair_ends(src_vec[...].astype(F32))
    _, tgt_ends_col = pair_ends(tgt_vec[...].astype(F32))
    keyval_ref[...] = jnp.zeros(keyval_ref.shape, F32)
    query_out[...] = jnp.zeros(query_out.shape, F32)
    sums_out[...] = jnp.zeros(sums_out.shape, F32)
    select = jnp.where(
        lax.broadcasted_iota(jnp.int32, (HEADS, 512), 1) // HEAD_DIM
        == lax.broadcasted_iota(jnp.int32, (HEADS, 512), 0),
        1.0,
        0.0,
    )

    def body(j, carry):
        at = pl.multiple_of(j * BLOCK, BLOCK)
        rows = pl.ds(at, BLOCK)
        first = start + at
        low, windows = cross_span(src_lens, tgt_lens, first)
        weighed = att[rows, :] * att_grad[rows, :].astype(F32)
        deltas = lax.dot_general(
            select, weighed, (((1,), (1,)), ((), ())),
            precision=lax.Precision.HIGHEST, preferred_element_type=F32,
        )

        def window(n, carry):
            begin = pl.multiple_of(low + n * WINDOW, 16)
            keys = pl.ds(begin, WINDOW)
            bias = cross_rule(src_ends_row, tgt_ends_col, first, begin, total)
            for group in range(2):
                lo, hi = group * GROUP, (group + 1) * GROUP
                query_grad, key_grad, value_grad = attend_back_block(
                    query[rows, lo:hi],
                    att_grad[rows, lo:hi],
                    keyval[keys, lo:hi],
                    keyval[keys, 512 + lo : 512 + hi],
                    bias,
                    lse[j, group : group + 1, :],
                    [deltas[group * 4 + h : group * 4 + h + 1, :] for h in range(4)],
                )
                query_out[rows, lo:hi] += query_grad.T
                keyval_ref[keys, lo:hi] += key_grad
                keyval_ref[keys, 512 + lo : 512 + hi] += value_grad
            return carry

        lax.fori_loop(0, windows, window, 0)
        return carry

    lax.fori_loop(0, count // BLOCK, body, 0)
    size = min(256, total)
    shards = mem_out.shape[0] + 1
    length = total // shards

    def to_memory(step, carry):
        rows = pl.ds(pl.multiple_of(step * size, size), size)
        grads = keyval_ref[rows, :]
        sums_out[0:1, :] += col_sum(grads[:, 512:])
        keyval_low[rows, :] = grads.astype(LOW)
        return carry

    lax.fori_loop(0, total // size, to_memory, 0)
    w_keyval = ins[7].get()
    for s in reversed(range(shards)):
        base = pl.multiple_of(lax.rem(idx[0] + s, shards) * length, BLOCK)
        grads = dot_nt(keyval_low[pl.ds(base, length), :], w_keyval[...])
        if s == 0:
            mem_own_out[...] = grads
        else:
            mem_out[s - 1] = grads.astype(LOW)


def dec_self_back_kernel(numbers, ins, outs, temps, total):
    query_grads, keyval_low, memory, normed_in, inv_in, branch_in, hid_in, gains, biases, w_query, w_out = [
        i.get() for i in ins[:11]
    ]
    branch_out, sums_out = [o.ref for o in outs[:2]]
    branch_ref, query_low, mid_ref, att_grad_out = temps[:4]
    count = query_grads.shape[0]
    sums_out[...] = jnp.zeros(sums_out.shape, F32)
    size = min(256, count)

    def dense(step, carry):
        rows = pl.ds(pl.multiple_of(step * size, size), size)
        query_grad = query_grads[rows, :]
        low = query_grad.astype(LOW)
        query_low[rows, :] = low
        normed = normed_in[rows, :]
        mid_ref[rows, :] = (normed * gains[0:1, :] + biases[3:4, :]).astype(LOW)
        mid_grad = branch_in[rows, :] + dot_nt(low, w_query[...])
        branch = norm_backward(mid_grad, normed, inv_in[rows, :], gains[0:1, :])
        branch_low = branch.astype(LOW)
        branch_out[rows, :] = branch
        branch_ref[rows, :] = branch_low
        att_grad_out[rows, :] = dot_nt(branch_low, w_out[...]).astype(LOW)
        sums_out[0:1, :] += col_sum(mid_grad * normed)
        sums_out[1:2, :] += col_sum(branch)
        sums_out[2:3, :] += col_sum(mid_grad)
        sums_out[3:4, :] += col_sum(query_grad)
        return carry

    lax.fori_loop(0, count // size, dense, 0)
    outs[0].flush()
    held = outs[2].ref

    def keyval_part(c, carry):
        cols = pl.ds(pl.multiple_of(c * 512, 512), 512)
        put_rows(held, dot_tn(memory[...], keyval_low[:, cols]), c * 512)
        return carry

    lax.fori_loop(0, 2, keyval_part, 0)
    put_rows(held, dot_tn(mid_ref[...], query_low[...]), 1024)
    put_rows(held, dot_tn(hid_in[...], branch_ref[...]), 1536)
    outs[2].flush()
    self_back(numbers, Loaded(att_grad_out), *ins[11:], outs[3:], *temps[4:], total, True)


def enc_self_back_kernel(numbers, ins, outs, temps, total):
    self_back(numbers, *ins, outs, *temps, total, False)


def self_back(numbers, att_grad, lse, lens, rows_in, outs, query_ref, keyval_ref, total, causal):
    own_out, halos = outs[0].ref, [o.ref for o in outs[1:]]
    rows_in, att_grad, lse = rows_in.get(), att_grad.get(), lse.get()
    count = att_grad.shape[0]
    ends = pair_ends(lens.get()[...].astype(F32))
    width = (2 if causal else 3) * BLOCK
    attend_local_back(
        rows_in, att_grad, lse, count // BLOCK, width, query_ref, keyval_ref,
        self_rule(ends, numbers[0][0] * count, total, width, causal),
    )
    if causal:
        halos[0][...] = keyval_ref[:BLOCK, :].astype(LOW)
    elif len(halos) == 1:
        edge = pl.multiple_of((1 - numbers[0][0]) * (BLOCK + count), BLOCK)
        halos[0][...] = keyval_ref[pl.ds(edge, BLOCK), :].astype(LOW)
    else:
        halos[0][...] = keyval_ref[:BLOCK, :].astype(LOW)
        halos[1][...] = keyval_ref[BLOCK + count :, :].astype(LOW)
    for out in outs[1:]:
        out.flush()
    own_out[:, :512] = query_ref[...]
    own_out[:, 512:] = keyval_ref[BLOCK : BLOCK + count, :]


def input_grad(own, edges, low_in, branch, w, grad_out, sums_out, low_ref, put, count):
    sums_out[...] = jnp.zeros(sums_out.shape, F32)
    size = min(256, count)

    def dense(step, carry):
        rows = pl.ds(pl.multiple_of(step * size, size), size)
        grads = own[rows, :]
        sums_out[0:1, :] += col_sum(grads[:, :512])
        sums_out[1:2, :] += col_sum(grads[:, 1024:])
        low_ref[rows, :] = grads.astype(LOW)
        return carry

    lax.fori_loop(0, count // size, dense, 0)
    returned = jnp.zeros((count, 1024), F32) if len(edges) > 1 and count == BLOCK else None
    for at, halo in edges:
        edge = pl.ds(at, BLOCK)
        grads = halo[...].astype(F32)
        sums_out[1:2, :] += col_sum(grads[:, 512:])
        if returned is not None:
            returned = grads = returned + grads
        low_ref[edge, 512:] = (own[edge, 512:] + grads).astype(LOW)

    def weight_part(c, carry):
        cols = pl.ds(pl.multiple_of(c * 512, 512), 512)
        put(dot_tn(low_in[...], low_ref[:, cols]), c * 512)
        return carry

    lax.fori_loop(0, 3, weight_part, 0)

    def back():
        def dense_grad(step, carry):
            rows = pl.ds(pl.multiple_of(step * size, size), size)
            grad_out[rows, :] = (branch[rows, :] + dot_nt(low_ref[rows, :], w[...])).astype(grad_out.dtype)
            return carry

        lax.fori_loop(0, count // size, dense_grad, 0)

    return back


def dec_input_grad_kernel(numbers, ins, outs, temps, blocks):
    blocks.fill(ins[-1], 1536)
    halo, own, branch, low_in, w = [i.get() for i in ins[:-1]]
    grad_out, sums_out = [o.ref for o in outs]
    (low_ref,) = temps
    count = own.shape[0]
    back = input_grad(
        own, [(count - BLOCK, halo)], low_in, branch, w, grad_out, sums_out, low_ref, blocks.put_rows, count
    )
    blocks.filled()
    blocks.spread(0, blocks.held.shape[2])
    back()


def enc_input_grad_kernel(numbers, ins, outs, temps, blocks, halo_count):
    halos = [i.get() for i in ins[:halo_count]]
    own, branch, low_in, w, *sums = [i.get() for i in ins[halo_count:]]
    (grad_out,) = [o.ref for o in outs]
    low_ref, sums_ref, small_ref = temps
    count = own.shape[0]
    if halo_count == 1:
        edges = [(pl.multiple_of((1 - numbers[0][0]) * (count - BLOCK), BLOCK), halos[0])]
    else:
        edges = [(0, halos[0]), (count - BLOCK, halos[1])]
    back = input_grad(own, edges, low_in, branch, w, grad_out, sums_ref, low_ref, blocks.put_rows, count)
    small_ref[...] = jnp.zeros(small_ref.shape, F32)
    for n, part in enumerate((*sums, sums_ref)):
        small_ref[n * 8 : (n + 1) * 8, :] = part[:8, :]
    blocks.put_rows(small_ref[...].T, 1536)
    blocks.spread(0, 1536 + BLOCK)
    back()


def enc_tail_back_kernel(numbers, ins, outs, temps, blocks):
    (mem_own, mem_others, cot, fin_in, fin_inv, mid_in, mid_inv, hid_in, gains, biases, upbias, w_down, w_up,
     w_out) = [i.get() for i in ins]
    branch_out, att_grad_out, sums_out = [o.ref for o in outs]
    branch_ref, mid_ref, active_ref, ffn_ref, up_low_ref = temps
    count = cot.shape[0]
    hidden = w_up.shape[1]
    sums_out[...] = jnp.zeros(sums_out.shape, F32)
    size = min(256, count)

    def dense(step, carry):
        rows = pl.ds(pl.multiple_of(step * size, size), size)
        grad = cot[rows, :].astype(F32) + mem_own[rows, :]
        for s in range(mem_others.shape[0]):
            grad = grad + mem_others[s, rows, :].astype(F32)
        normed_final = fin_in[rows, :]
        ffn = norm_backward(grad, normed_final, fin_inv[rows, :], gains[1:2, :])
        ffn_low = ffn.astype(LOW)
        ffn_ref[rows, :] = ffn_low
        normed = mid_in[rows, :]
        low = (normed * gains[0:1, :] + biases[3:4, :]).astype(LOW)
        mid_ref[rows, :] = low
        mid_grad = ffn
        for c in range(0, hidden, 512):
            up = dot_nn(low, w_up[:, c : c + 512]) + upbias[:, c : c + 512]
            gate = sigmoid(up)
            active = up * gate
            active_ref[rows, c : c + 512] = active.astype(LOW)
            up_grad = dot_nt(ffn_low, w_down[c : c + 512, :]) * (gate + active * (1.0 - gate))
            sums_out[8 + c // 512 : 9 + c // 512, :] += col_sum(up_grad)
            up_low = up_grad.astype(LOW)
            up_low_ref[rows, c : c + 512] = up_low
            mid_grad = mid_grad + dot_nt(up_low, w_up[:, c : c + 512])
        branch = norm_backward(mid_grad, normed, mid_inv[rows, :], gains[0:1, :])
        branch_low = branch.astype(LOW)
        branch_out[rows, :] = branch
        branch_ref[rows, :] = branch_low
        att_grad_out[rows, :] = dot_nt(branch_low, w_out[...]).astype(LOW)
        sums_out[0:1, :] += col_sum(mid_grad * normed)
        sums_out[1:2, :] += col_sum(grad * normed_final)
        sums_out[2:3, :] += col_sum(branch)
        sums_out[3:4, :] += col_sum(mid_grad)
        sums_out[4:5, :] += col_sum(ffn)
        sums_out[5:6, :] += col_sum(grad)
        return carry

    lax.fori_loop(0, count // size, dense, 0)
    outs[0].flush()
    feed_forward_grads(
        mid_ref, up_low_ref, ffn_ref, active_ref, hid_in, branch_ref, sums_out, blocks
    )


def log2(number):
    bits = number.bit_length() - 1
    assert number == 1 << bits
    return bits


def swapped(value, axis, bit, devices):
    return lax.ppermute(value, axis, [(i, i ^ (1 << bit)) for i in range(devices)])


class Chain:
    def __init__(self, token):
        self.token = token

    def tie(self, *values):
        self.token, *values = lax.optimization_barrier((self.token, *values))
        return values[0] if len(values) == 1 else values


class Reduction:
    def __init__(self, chain, arrays, order, devices, seq_count):
        self.chain, self.order, self.devices, self.seq_count = (chain, order, devices, seq_count)
        self.keep, send = arrays
        self.size = self.keep.shape[0]
        self.received, self.low, self.others = [], None, []
        self.push(send)

    def push(self, send):
        bit = self.order[len(self.received)]
        if bit == OVER_SEQ:
            self.received.append(swapped(send, "seq", 0, self.seq_count))
        else:
            self.received.append(swapped(send, "dp", bit, self.devices))

    def part(self, first, last):
        total = self.keep[first:last].astype(F32)
        for piece in self.received:
            total = total + piece[first:last].astype(F32)
        return total

    def next(self):
        self.received[-1] = self.chain.tie(self.received[-1])
        if len(self.received) < len(self.order):
            half = self.size // 2
            self.push(self.chain.tie(self.part(half, self.size).astype(LOW)))
            self.size = half
            return
        self.low = self.chain.tie(self.part(0, 1)[0].astype(LOW))
        if log2(self.seq_count):
            self.others.append(swapped(self.low, "seq", 0, self.seq_count))

    def pair(self):
        while self.low is None:
            self.next()
        low, other = self.low, self.others[0]
        if OVER_SEQ not in self.order:
            for bit in range(1, log2(self.seq_count)):
                low = lax.optimization_barrier((low.astype(F32) + other.astype(F32)).astype(LOW))
                other = swapped(low, "seq", bit, self.seq_count)
        return (low, other)


def from_shards(own, count):
    return jnp.stack(
        [lax.ppermute(own, "seq", [((i + s) % count, i) for i in range(count)]) for s in range(1, count)]
    )


def feed_forward_unpack(numbers, ins, outs, temps):
    low, other = [i.get() for i in ins]
    up_out, matrix_out, down_out, bias_out = [o.ref for o in outs]
    (total,) = temps
    total[...] = low[...].astype(F32) + other[...].astype(F32)
    share = up_out.shape[0]
    width = down_out.shape[0]
    pieces = BLOCK // width
    groups = FEATURES // pieces // share
    tall = jnp.concatenate([total[:, g * BLOCK : (g + 1) * BLOCK] for g in range(groups)], axis=0).T
    for p in range(pieces):
        rows = FEATURES // pieces
        down_out[:, p * rows : (p + 1) * rows] = tall[p * width : (p + 1) * width, :]
    end = groups * BLOCK
    bias_out[...] = total[0:1, end : end + width]
    up_out[...] = total[:, HIDDEN + BLOCK : 2 * HIDDEN + BLOCK]
    matrix_out[...] = total[:, 2 * HIDDEN + BLOCK :]


def decoder_unpack(numbers, ins, outs, temps, halved):
    low, other = [i.get() for i in ins]
    (total,) = temps
    if halved:
        width = low.shape[1]
        seq = numbers[0][0]
        total[:, pl.ds(pl.multiple_of(seq * width, BLOCK), width)] = low[...].astype(F32)
        total[:, pl.ds(pl.multiple_of((1 - seq) * width, BLOCK), width)] = other[...].astype(F32)
    else:
        total[...] = low[...].astype(F32) + other[...].astype(F32)
    at = 0
    for out in outs:
        width = out.ref.shape[1]
        out.ref[...] = total[:, at : at + width]
        at += width


def encoder_unpack(numbers, ins, outs, temps, picks):
    low, other = [i.get() for i in ins]
    total = low[...].astype(F32) + other[...].astype(F32)
    outs[0].ref[...] = total[:, :1536]
    small = total[:, 1536:].T
    for out, rows in zip(outs[1:], picks):
        for n, row in enumerate(rows):
            out.ref[n : n + 1, :] = small[row : row + 1, :]


def encoders_unpack(numbers, ins, outs, temps, picks):
    feed_forward_unpack(numbers, ins[:2], outs[:4], temps[:1])
    for out in outs[:4]:
        out.flush()
    encoder_unpack(numbers, ins[2:4], outs[4:9], (), picks)


def rows_unpack(numbers, ins, outs, temps):
    shards = numbers[0]
    for n, out in enumerate(outs):
        own, others = ins[2 * n].get(), ins[2 * n + 1].get()
        count = own.shape[0]
        parts = others.shape[0] + 1
        for s in range(parts):
            at = pl.ds(pl.multiple_of(lax.rem(shards[0] + s, parts) * count, BLOCK), count)
            out.ref[at, :] = (own[...] if s == 0 else others[s - 1]).astype(out.ref.dtype)
        out.flush()


def local(
    src_embed, tgt_embed, src_lengths, tgt_lengths, enc_cotangent, dec_cotangent,
    enc_inproj, enc_outproj, enc_upproj, enc_downproj, enc_gains, enc_biases, enc_upbias,
    dec_inproj, dec_outproj, cross_query, cross_keyval, cross_outproj, dec_upproj, dec_downproj,
    dec_gains, dec_biases, dec_upbias,
):
    _, count, features = src_embed.shape
    total = tgt_embed.shape[1]
    hidden = enc_upproj.shape[1]
    devices = lax.axis_size("dp")
    seq_count = lax.axis_size("seq")
    pair = seq_count == 2
    blocks = count // BLOCK
    bits = log2(devices)
    x_first = tuple(range(bits))
    y_first = (0, OVER_SEQ, *range(1, bits)) if seq_count == 2 else x_first
    seq_index = lax.axis_index("seq")
    dp_index = lax.axis_index("dp")
    idx = jnp.where(jnp.arange(2) == 0, seq_index, dp_index).astype(jnp.int32)
    chain = Chain(idx)
    table = jnp.asarray(place_table(features))
    src_own, tgt_all = src_embed[0], tgt_embed[0]
    enc_ub, dec_ub = enc_upbias[None], dec_upbias[None]
    up = [(i, i + 1) for i in range(seq_count - 1)]
    down = [(i + 1, i) for i in range(seq_count - 1)]
    swap = [(0, 1), (1, 0)]
    wide = (count, features)
    near = lambda *arrays: [(a, NEAR) for a in arrays]
    far = lambda *arrays: [(a, FAR) for a in arrays]
    part = functools.partial
    lse = ((blocks, 2, 512), F32)
    inv = ((count, 1), F32)
    begin = lambda numbers: pl.multiple_of(numbers[0] * count, BLOCK)
    before = lambda numbers: pl.multiple_of(jnp.maximum(numbers[0] * count - BLOCK, 0), BLOCK)

    if pair:
        edge = lax.dynamic_slice_in_dim(src_own, (1 - seq_index) * (count - BLOCK), BLOCK, 0)
        left = right = lax.ppermute(chain.tie(edge), "seq", swap)
    else:
        left = lax.ppermute(src_own[count - BLOCK :], "seq", up)
        right = lax.ppermute(src_own[:BLOCK], "seq", down)
    (src_in, src_low, own_rows), _, enc_near = call(
        enc_pre_kernel, "enc_pre", [chain.token], far(src_own, src_lengths, table, enc_inproj, enc_biases),
        [(wide, F32, NEAR), (wide, LOW, FAR), ((count, 1536), LOW, NEAR)],
        ahead=far(src_lengths, table, enc_inproj, enc_gains, enc_biases, enc_ub, enc_outproj),
    )
    src_low = chain.tie(src_low)
    (enc_rows, enc_lse, enc_hid, mid_normed, mid_inv, fin_normed, fin_inv, encoded), _, self_near = call(
        part(enc_kernel, total=total), "enc_forward", [chain.token], [*near(left, right, src_in, own_rows, *enc_near), *far(enc_upproj, enc_downproj)],
        [((count + 2 * BLOCK, 1536), LOW, FAR), (*lse, FAR),
         (wide, LOW, FAR), (wide, F32, FAR), (*inv, FAR),
         (wide, F32, FAR), (*inv, FAR), (wide, LOW, FAR)],
        ahead=[(tgt_all, FAR, before, BLOCK), (tgt_all, FAR, begin, count),
               *far(tgt_lengths, table, dec_inproj, dec_gains, dec_biases, dec_outproj, cross_query)],
    )
    encoded = chain.tie(encoded)
    others = from_shards(encoded, seq_count)
    idx_self, _ = lax.optimization_barrier((chain.token, encoded))
    (tgt_low, dec_rows, dec_lse, dec_hid, self_normed, self_inv, cross_q, own_keyval), _, tail_near = call(
        part(dec_self_kernel, total=total), "dec_self", [idx_self], [*near(*self_near), *far(encoded, cross_keyval)],
        [(wide, LOW, FAR), ((count + BLOCK, 1536), LOW, FAR), (*lse, FAR), (wide, LOW, FAR), (wide, F32, FAR), (*inv, FAR),
         (wide, LOW, FAR), ((count, 1024), LOW, NEAR)],
        [(wide, F32)],
        ahead=[*far(encoded, src_lengths, tgt_lengths, dec_gains, dec_biases, dec_ub, cross_keyval),
               (dec_cotangent[0], FAR, begin, count), *far(cross_outproj, dec_upproj, dec_downproj)],
    )
    (cross_att, cross_lse, keyval, memory, decoded, cross_att_grad, cross_branch, tail_sums), tail, back_near = call(
        part(cross_tail_kernel, total=total), "cross_tail", [chain.token, src_lengths, tgt_lengths],
        [*far(cross_q), *near(tail_near[0]), *near(others, own_keyval), *near(*tail_near[1:7]), *far(self_normed), *near(*tail_near[7:])],
        [(wide, F32, FAR), (*lse, NEAR), ((total + WINDOW, 1024), LOW, NEAR), ((total, features), LOW, FAR),
         (wide, LOW, FAR), (wide, LOW, NEAR), (wide, F32, FAR), ((16, features), F32, FAR)],
        [(wide, LOW), (wide, LOW), (wide, LOW), ((min(256, count), hidden), F32), ((count, hidden), LOW),
         (wide, LOW), ((count, hidden), LOW),
         ((HEADS, BLOCK), F32), ((HEADS, BLOCK), F32), ((features, BLOCK), F32), pltpu.SemaphoreType.DMA((1,))],
        [2 * hidden + BLOCK + 512], x_first,
        ahead=far(src_lengths, tgt_lengths),
    )
    decoded = chain.tie(decoded)
    decoded_others = from_shards(decoded, seq_count)
    make = part(Reduction, devices=devices, seq_count=seq_count)
    tail = make(chain, tail, x_first)
    (mem_own, mem_send, query_grads, keyval_grads, mem_sums), _, dense_near = call(
        part(cross_back_kernel, total=total), "cross_back", [chain.token, src_lengths, tgt_lengths],
        [*far(cross_q), *near(keyval), *far(cross_att), *near(cross_att_grad, cross_lse, *back_near), *far(cross_keyval)],
        [(wide, F32, FAR), ((seq_count - 1, *wide), LOW, FAR), (wide, F32, NEAR),
         ((total, 1024), LOW, NEAR), ((8, features), F32, FAR)],
        [((total + WINDOW, 1024), F32)],
        ahead=[*far(memory, self_normed, self_inv, cross_branch),
               *far(dec_hid, dec_gains, dec_biases, cross_query, dec_outproj, dec_lse, tgt_lengths, dec_rows)],
    )
    mem_send = chain.tie(mem_send)
    mem_others = jnp.stack(
        [
            lax.ppermute(mem_send[s - 1], "seq", [(i, (i + s) % seq_count) for i in range(seq_count)])
            for s in range(1, seq_count)
        ]
    )
    decoded_others = chain.tie(decoded_others)
    tail.next()
    (self_branch, cross_sums, cross_held, self_own, self_halo), _, enc_near = call(
        part(dec_self_back_kernel, total=total), "dec_self_back", [chain.token],
        near(query_grads, keyval_grads, *dense_near),
        [(wide, F32, FAR), ((8, features), F32, FAR), ((devices, features // devices, 2048), LOW, FAR),
         ((count, 1536), F32, FAR), ((BLOCK, 1024), LOW, FAR)],
        [(wide, LOW), (wide, LOW), (wide, LOW), (wide, LOW), (wide, F32), ((count + BLOCK, 1024), F32)],
        ahead=far(enc_cotangent[0], fin_normed, fin_inv, mid_normed, mid_inv, enc_hid, enc_gains, enc_biases,
                  enc_ub, enc_downproj, enc_upproj, enc_outproj),
    )
    self_halo = chain.tie(self_halo)
    self_returned = lax.ppermute(self_halo, "seq", down)
    mem_others = chain.tie(mem_others)
    (enc_branch, enc_att_grad, enc_sums), enc, self_near = call(
        enc_tail_back_kernel, "enc_tail_back", [chain.token],
        [*far(mem_own), *near(mem_others), *near(*enc_near)],
        [(wide, F32, FAR), (wide, LOW, FAR), ((16, features), F32, FAR)],
        [(wide, LOW), (wide, LOW), ((count, hidden), LOW), (wide, LOW), ((count, hidden), LOW)],
        [2 * hidden + BLOCK + 512], x_first,
        ahead=far(self_own, self_branch, tgt_low, dec_inproj),
    )
    enc_sums = chain.tie(enc_sums)
    enc = make(chain, enc, x_first)
    self_returned = chain.tie(self_returned)
    (tgt_part, self_sums), cross, back_near = call(
        dec_input_grad_kernel, "dec_input_grad", [chain.token],
        [*near(self_returned), *near(*self_near), (cross_held, RAW)],
        [(wide, LOW, FAR), ((8, features), F32, FAR)],
        [((count, 1536), LOW)],
        [1536 + 2048], y_first,
        ahead=far(enc_att_grad, enc_lse, src_lengths, enc_rows),
    )
    tgt_part = chain.tie(tgt_part)
    cross = make(chain, cross, y_first)
    tgt_others = from_shards(tgt_part, seq_count)
    tail.next()
    enc.next()
    (enc_own, *halos), _, in_near = call(
        part(enc_self_back_kernel, total=total), "enc_self_back", [chain.token], near(*back_near),
        [((count, 1536), F32, NEAR)] + [((BLOCK, 1024), LOW, FAR)] * (1 if pair else 2),
        [(wide, F32), ((count + 2 * BLOCK, 1024), F32)],
        ahead=far(enc_branch, src_low, enc_inproj),
    )
    halos = [chain.tie(h) for h in halos]
    if pair:
        halos = [lax.ppermute(halos[0], "seq", swap)]
    else:
        halos = [lax.ppermute(halos[1], "seq", up), lax.ppermute(halos[0], "seq", down)]
    cross.next()
    tail.next()
    tgt_others = chain.tie(tgt_others)
    halos = [chain.tie(h) for h in halos]
    (src_grad,), ins, _ = call(
        part(enc_input_grad_kernel, halo_count=len(halos)), "enc_input_grad", [chain.token],
        [*near(*halos), *near(enc_own, *in_near), *far(tail_sums, mem_sums, cross_sums, self_sums, enc_sums)],
        [(wide, F32, FAR)],
        [((count, 1536), LOW), ((8, features), F32), ((BLOCK, features), F32)],
        [1536 + BLOCK], x_first,
    )
    src_grad = chain.tie(src_grad)
    ins = make(chain, ins, x_first)
    share = features // devices
    slim = lambda *widths: [((share, w), F32, FAR) for w in widths]
    matrices = [*slim(hidden, 512), ((hidden // devices, 512), F32, FAR), ((1, hidden // devices), F32, FAR)]
    all_rows = (total, features)
    packed = ((share, 2 * hidden + BLOCK + 512), F32)
    enc.next()
    ins.next()
    tail.next()
    cross.next()
    ins.next()
    enc.next()
    (decoded_all, tgt_all_grad), _, _ = call(
        rows_unpack, "rows_unpack", [chain.token], [*far(decoded), *near(decoded_others), *far(tgt_part), *near(tgt_others)],
        [(all_rows, LOW, FAR), (all_rows, F32, FAR)],
    )
    tgt_all_grad = chain.tie(tgt_all_grad)
    (dec_up, cross_out, dec_down, dec_ub_grad), _, _ = call(
        feed_forward_unpack, "tail_unpack", [chain.token], near(*tail.pair()), matrices, [packed]
    )
    dec_up = chain.tie(dec_up)
    cross.next()
    ins.next()
    enc.next()
    cross.next()
    ins.next()
    cross.next()
    t, m, c, d, e, i = range(0, 48, 8)
    picks = [
        (e, e + 1),
        (i, i + 1, e + 2, e + 3, e + 4, e + 5),
        (c, t, t + 1),
        (d, d + 1, c + 1, c + 2, c + 3, m, t + 2, t + 3, t + 4, t + 5),
    ]
    (enc_up, enc_out, enc_down, enc_ub_grad, enc_in, enc_gains_grad, enc_biases_grad, dec_gains_grad,
     dec_biases_grad), _, _ = call(
        part(encoders_unpack, picks=picks), "last_unpack", [chain.token], near(*enc.pair(), *ins.pair()),
        [*matrices, *slim(1536), *[((len(p), share), F32, FAR) for p in picks]], [packed],
    )
    enc_up = chain.tie(enc_up)
    (dec_in, keyval_grad, query_grad, dec_out), _, _ = call(
        part(decoder_unpack, halved=OVER_SEQ in y_first), "cross_unpack", [chain.token], near(*cross.pair()),
        slim(1536, 1024, 512, 512), [((share, 3584), F32)],
    )
    return (
        encoded[None],
        decoded_all[None],
        src_grad[None],
        tgt_all_grad[None],
        enc_in,
        enc_out,
        enc_up,
        enc_down,
        enc_gains_grad,
        enc_biases_grad,
        enc_ub_grad[0],
        dec_in,
        dec_out,
        query_grad,
        keyval_grad,
        cross_out,
        dec_up,
        dec_down,
        dec_gains_grad,
        dec_biases_grad,
        dec_ub_grad[0],
    )


def solution(mesh):
    rows, whole = P("dp", "seq", None), P("dp", None, None)
    return jax.shard_map(
        local,
        mesh=mesh,
        in_specs=(rows, whole, P("dp", None), P("dp", None), rows, whole, *([P()] * 17)),
        out_specs=(
            rows, whole, rows, whole,
            *([P("dp", None)] * 4), P(None, "dp"), P(None, "dp"), P("dp"),
            *([P("dp", None)] * 7), P(None, "dp"), P(None, "dp"), P("dp"),
        ),
        check_vma=False,
    )
```
